32 devices in a mesh: span: 8 (over y, x, core), head: 4 (over z).
Axes of the slice: x: 2, y: 2, z: 4, core: 2. Of those that a mesh axis runs over, the one named last changes fastest.
Arguments:
- neighbour_query: bfloat16 [8192, 4096], P('span', 'head'), may hold values from -12 to 12
- neighbour_key: bfloat16 [8192, 4096], P('span', 'head'), may hold values from -6 to 6
- neighbour_value: bfloat16 [8192, 4096], P('span', 'head'), may hold values from -12.2 to 12.2
- segment_key: bfloat16 [2048, 4096], P('span', 'head'), may hold values from -30 to 30
- segment_value: bfloat16 [2048, 4096], P('span', 'head'), may hold values from -6 to 6
- decoder_query: bfloat16 [2048, 4096], P('span', 'head'), may hold values from -24 to 24
- sources: int32 [32, 2], P('span'), may hold values from 0 to 31, as said below
Outputs:
- blended: bfloat16 [2048, 4096], P('span', 'head')
The draws below stay inside these ranges and needn't reach their ends.
Inputs may be any that keep to these rules, and one draw needn't show every extreme that they name: `sources`: the segments of index o of span are o * 4 to (o + 1) * 4 - 1. Among the 8 entries of the segments of one index of span, at most 2 name segments of one index of span, and in every such block some index is named exactly 2 times.
All inputs are finite; a program needn't handle non-finite values.
Results may differ from the reference program's by a relative error of at most 0.035.
Values may be sent and summed in bfloat16 or wider, within the bound.
A program may use at most 192 MiB of HBM per device.

```python
import math
import jax
import jax.numpy as jnp
from jax import lax

HEAD_DIM = 128
SEG_LEN = 64
NBR_LEN = 128
NEIGHBOURS = 2
SEG_DEV = 4
HIDDEN_COLS = 4096
SEGMENTS = 32
CAPACITY = 2
N_SPAN = 8


def rising_scales():
    return 0.3 * jnp.exp(math.log(10.0) * jnp.arange(HIDDEN_COLS, dtype=jnp.float32) / HIDDEN_COLS)


def draw_sources(key, part):
    keys = jax.random.split(jax.random.fold_in(key, 26), 5)
    per_block = SEG_DEV * NEIGHBOURS
    slot_count_total = N_SPAN * CAPACITY
    favoured_rows = jax.random.randint(keys[0], (N_SPAN,), 0, 4)
    slot_holder_index = jnp.arange(slot_count_total) // CAPACITY
    random_jitter = jax.random.randint(keys[1], (N_SPAN, slot_count_total), 0, 1024)
    hotspot_row = jax.random.randint(keys[2], (N_SPAN,), 0, N_SPAN)
    extra_score = jnp.where(slot_holder_index[None, :] == hotspot_row[:, None], 8, 0)
    logit_scores = ((favoured_rows[slot_holder_index][None, :] + extra_score) * 1024 + random_jitter) * slot_count_total + jnp.arange(slot_count_total)[None, :]
    top_values, top_index = lax.top_k(logit_scores, per_block)
    owners = slot_holder_index[top_index]
    mixing = jax.random.randint(keys[3], (N_SPAN, per_block), 0, 1 << 20) * per_block + jnp.arange(per_block)[None, :]
    shuffle = jnp.argsort(mixing, axis=1)
    owners = jnp.take_along_axis(owners, shuffle, axis=1)
    within = jax.random.randint(keys[4], (N_SPAN, per_block), 0, SEG_DEV)
    return (owners * SEG_DEV + within).reshape(SEGMENTS, NEIGHBOURS).astype(jnp.int32)


def draw_neighbour_query(key, part):
    row_total = SEGMENTS * NEIGHBOURS * NBR_LEN
    sample_key = jax.random.fold_in(key, 21)
    return jnp.clip(2.0 * jax.random.normal(sample_key, (row_total, HIDDEN_COLS), jnp.float32), -12.0, 12.0).astype(jnp.bfloat16)


def draw_neighbour_key(key, part):
    row_total = SEGMENTS * NEIGHBOURS * NBR_LEN
    sample_key = jax.random.fold_in(key, 22)
    return jnp.clip(jax.random.normal(sample_key, (row_total, HIDDEN_COLS), jnp.float32), -6.0, 6.0).astype(jnp.bfloat16)


def draw_neighbour_value(key, part):
    row_total = SEGMENTS * NEIGHBOURS * NBR_LEN
    sample_key = jax.random.fold_in(key, 23)
    filler = jnp.clip(jax.random.normal(sample_key, (row_total, HIDDEN_COLS), jnp.float32), -4.0, 4.0)
    return (filler * rising_scales()[None, :]).astype(jnp.bfloat16)


def draw_segment_key(key, part):
    row_total = SEGMENTS * SEG_LEN
    sample_key = jax.random.fold_in(key, 24)
    return jnp.clip(2.0 * jax.random.normal(sample_key, (row_total, HIDDEN_COLS), jnp.float32), -12.0, 12.0).astype(jnp.bfloat16)


def draw_decoder_query(key, part):
    row_total = SEGMENTS * SEG_LEN
    sample_key = jax.random.fold_in(key, 25)
    return jnp.clip(3.0 * jax.random.normal(sample_key, (row_total, HIDDEN_COLS), jnp.float32), -18.0, 18.0).astype(jnp.bfloat16)


def block_levels(rng, extent, pieces, low, high):
    loudness = 1.0
    for dim, shards_of in pieces:
        draws = jax.random.uniform(jax.random.fold_in(jax.random.fold_in(rng, 6), dim), (shards_of,), jnp.float32, low / len(pieces), high / len(pieces))
        loudness = loudness * jnp.repeat(jnp.exp(draws), extent[dim] // shards_of).reshape((-1,) + (1,) * (len(extent) - 1 - dim))
    return loudness


def normal_values(key, extent, spread, most, cuts=(), held_as=jnp.bfloat16):
    values = jax.random.normal(key, extent, jnp.float32) * spread
    if len(cuts) > 0:
        values = block_levels(key, extent, cuts, -0.22, 0.18) * values
    return jnp.clip(values, min=-most, max=most).astype(held_as)


def setup_inputs(seed: int = 0) -> dict:
    seeds = jax.random.split(jax.random.key(seed), 8)
    neighbour_query = draw_neighbour_query(jax.random.fold_in(seeds[7], 71), 0)
    neighbour_key = draw_neighbour_key(jax.random.fold_in(seeds[7], 71), 0)
    neighbour_value = draw_neighbour_value(jax.random.fold_in(seeds[7], 71), 0)
    segment_key = draw_segment_key(jax.random.fold_in(seeds[7], 71), 0)
    segment_value = normal_values(seeds[4], (SEGMENTS * SEG_LEN, HIDDEN_COLS), 1.0, 6.0, ((0, 8), (1, 4)))
    decoder_query = draw_decoder_query(jax.random.fold_in(seeds[7], 71), 0)
    sources = draw_sources(jax.random.fold_in(seeds[7], 71), 0)
    return {"neighbour_query": neighbour_query, "neighbour_key": neighbour_key, "neighbour_value": neighbour_value, "segment_key": segment_key, "segment_value": segment_value, "decoder_query": decoder_query, "sources": sources}


epsilon = 1e-06

def attend(query_rows, key_rows, value_rows):
    groups, length, columns = query_rows.shape
    head_count = columns // HEAD_DIM
    query_heads = query_rows.astype(jnp.float32).reshape(groups, length, head_count, HEAD_DIM)
    key_heads = key_rows.astype(jnp.float32).reshape(groups, key_rows.shape[1], head_count, HEAD_DIM)
    value_heads = value_rows.astype(jnp.float32).reshape(groups, value_rows.shape[1], head_count, HEAD_DIM)
    logit_scores = jnp.einsum('bqhd,bkhd->bhqk', query_heads, key_heads) * HEAD_DIM ** (-0.5)
    logit_scores = logit_scores - lax.optimization_barrier(jnp.max(logit_scores, axis=-1, keepdims=True))
    weights = jnp.exp(logit_scores)
    weights = (weights / lax.optimization_barrier(jnp.sum(weights, axis=-1, keepdims=True))).astype(jnp.bfloat16)
    output = jnp.einsum('bhqk,bkhd->bqhd', weights.astype(jnp.float32), value_heads)
    return output.reshape(groups, length, columns)

def normalize(rows):
    wide = rows.astype(jnp.float32)
    meansq = lax.optimization_barrier(jnp.mean(wide * wide, axis=-1, keepdims=True))
    return (wide * lax.rsqrt(meansq + epsilon)).astype(jnp.bfloat16)

def reference(neighbour_query, neighbour_key, neighbour_value, segment_key, segment_value, decoder_query, sources):
    columns = neighbour_query.shape[1]
    per_device = SEG_DEV * NEIGHBOURS
    all_keys = segment_key.reshape(SEGMENTS, SEG_LEN, columns)
    all_values = segment_value.reshape(SEGMENTS, SEG_LEN, columns)

    def encode(group):
        query_rows, key_rows, value_rows, listed = group
        self_out = attend(query_rows, key_rows, value_rows).astype(jnp.bfloat16)
        cross_query = normalize(self_out)
        crossed = attend(cross_query, all_keys[listed], all_values[listed]).astype(jnp.bfloat16)
        return (self_out.astype(jnp.float32) + crossed.astype(jnp.float32)).astype(jnp.bfloat16)

    def shaped(array):
        return array.reshape(N_SPAN, per_device, NBR_LEN, columns)
    listed_all = sources.reshape(N_SPAN, per_device).astype(jnp.int32)
    encoded = lax.map(encode, (shaped(neighbour_query), shaped(neighbour_key), shaped(neighbour_value), listed_all))
    encoded = encoded.reshape(SEGMENTS, NEIGHBOURS * NBR_LEN, columns)
    prior = jnp.concatenate([jnp.zeros((1, NEIGHBOURS * NBR_LEN, columns), jnp.bfloat16), encoded[:-1]], axis=0)

    def decode(group):
        query_rows, value_rows = group
        return attend(query_rows, normalize(value_rows), value_rows).astype(jnp.bfloat16)
    blended = lax.map(decode, (decoder_query.reshape(N_SPAN, SEG_DEV, SEG_LEN, columns), prior.reshape(N_SPAN, SEG_DEV, NEIGHBOURS * NBR_LEN, columns)))
    return blended.reshape(SEGMENTS * SEG_LEN, columns)
```

```python
import functools
import math

import jax
import jax.numpy as jnp
from jax import lax
from jax.experimental import pallas as pl
from jax.experimental.pallas import tpu as pltpu
from jax.sharding import PartitionSpec as P

HEAD_DIM = 128
SEG_LEN = 64
NBR_LEN = 128
NEIGHBOURS = 2
SEG_DEV = 4


epsilon = 1e-06


def from_behind(x, axis, by):
    count = lax.axis_size(axis)
    pairs = [(i, i + by) for i in range(count) if 0 <= i + by < count]
    return lax.ppermute(x, axis, pairs)


def attend(query_rows, key_rows, value_rows):
    groups, length, columns = query_rows.shape
    head_count = columns // HEAD_DIM
    query_heads = query_rows.reshape(groups, length, head_count, HEAD_DIM)
    key_heads = key_rows.reshape(groups, key_rows.shape[1], head_count, HEAD_DIM)
    value_heads = value_rows.reshape(groups, value_rows.shape[1], head_count, HEAD_DIM)
    logit_scores = jnp.einsum(
        "bqhd,bkhd->bhqk", query_heads, key_heads, preferred_element_type=jnp.float32
    ) * HEAD_DIM ** (-0.5)
    logit_scores = logit_scores - jnp.max(logit_scores, axis=-1, keepdims=True)
    weights = jnp.exp(logit_scores)
    weights = (weights / jnp.sum(weights, axis=-1, keepdims=True)).astype(jnp.bfloat16)
    output = jnp.einsum("bhqk,bkhd->bqhd", weights, value_heads, preferred_element_type=jnp.float32)
    return output.reshape(groups, length, columns)


def squares(rows):
    wide = rows.astype(jnp.float32)
    return jnp.sum(wide * wide, axis=-1)


def normalize(rows, totals, full_width):
    scale = lax.rsqrt(totals / full_width + epsilon)
    return (rows.astype(jnp.float32) * scale[:, None]).astype(jnp.bfloat16)


def pick(blocks, index):
    chosen = (index[:, None] == jnp.arange(blocks.shape[0])[None, :]).astype(blocks.dtype)
    return jnp.einsum("ws,slc->wlc", chosen, blocks, preferred_element_type=jnp.float32).astype(blocks.dtype)


def body(
    neighbour_query,
    neighbour_key,
    neighbour_value,
    segment_key,
    segment_value,
    decoder_query,
    sources,
):
    columns = neighbour_query.shape[1]
    full_width = columns * lax.axis_size("head")
    devices = lax.axis_size("span")
    per_device = SEG_DEV * NEIGHBOURS
    capacity = max(2, 2 * per_device // devices)
    panel_rows = NEIGHBOURS * NBR_LEN
    self_out = attend(
        neighbour_query.reshape(per_device, NBR_LEN, columns),
        neighbour_key.reshape(per_device, NBR_LEN, columns),
        neighbour_value.reshape(per_device, NBR_LEN, columns),
    ).astype(jnp.bfloat16)
    flat_self = self_out.reshape(per_device * NBR_LEN, columns)
    totals = lax.psum(squares(flat_self), "head")
    cross_query = normalize(flat_self, totals, full_width).reshape(per_device, NBR_LEN, columns)
    listed = sources.reshape(per_device)
    owners = listed // SEG_DEV
    within = listed % SEG_DEV
    position = jnp.arange(per_device)
    earlier = (owners[:, None] == owners[None, :]) & (position[:, None] > position[None, :])
    ranked = jnp.sum(earlier.astype(jnp.int32), axis=1)
    slots = owners * capacity + ranked
    picked = (slots[:, None] == jnp.arange(devices * capacity)[None, :]).astype(jnp.int32)
    request = jnp.sum(picked * (within + 1)[:, None], axis=0).reshape(devices, capacity)
    asked = lax.all_to_all(request, "span", split_axis=0, concat_axis=0, tiled=True)
    wanted = jnp.maximum(asked - 1, 0).reshape(devices * capacity)
    own_keys = pick(segment_key.reshape(SEG_DEV, SEG_LEN, columns), wanted)
    own_values = pick(segment_value.reshape(SEG_DEV, SEG_LEN, columns), wanted)
    got_keys, got_values = (
        lax.all_to_all(
            own_keys.reshape(devices, capacity, SEG_LEN, columns),
            "span",
            split_axis=0,
            concat_axis=0,
            tiled=True,
        ),
        lax.all_to_all(
            own_values.reshape(devices, capacity, SEG_LEN, columns),
            "span",
            split_axis=0,
            concat_axis=0,
            tiled=True,
        ),
    )
    source_keys = pick(got_keys.reshape(devices * capacity, SEG_LEN, columns), slots)
    source_values = pick(got_values.reshape(devices * capacity, SEG_LEN, columns), slots)
    crossed = attend(cross_query, source_keys, source_values).astype(jnp.bfloat16)
    encoded = (self_out.astype(jnp.float32) + crossed.astype(jnp.float32)).astype(jnp.bfloat16)
    encoded = encoded.reshape(per_device * NBR_LEN, columns)
    key_totals = lax.psum(squares(encoded), "head")
    keys_all = normalize(encoded, key_totals, full_width)
    before_keys, before_values = from_behind(
        (keys_all[-panel_rows:], encoded[-panel_rows:]), "span", 1
    )
    used_keys = jnp.concatenate([before_keys, keys_all[:-panel_rows]], axis=0)
    used_values = jnp.concatenate([before_values, encoded[:-panel_rows]], axis=0)
    blended = attend(
        decoder_query.reshape(SEG_DEV, SEG_LEN, columns),
        used_keys.reshape(SEG_DEV, panel_rows, columns),
        used_values.reshape(SEG_DEV, panel_rows, columns),
    ).astype(jnp.bfloat16)
    return blended.reshape(SEG_DEV * SEG_LEN, columns)


MESH = pl.DeviceIdType.MESH
GROUPS = 4


def dot_t(a, b):
    return lax.dot_general(a, b, (((1,), (1,)), ((), ())), preferred_element_type=jnp.float32)


def dot_first(a, b):
    return lax.dot_general(a, b, (((0,), (0,)), ((), ())), preferred_element_type=jnp.float32)


def apart(rows):
    count = rows.shape[1] // HEAD_DIM
    zero = jnp.zeros((rows.shape[0], HEAD_DIM), rows.dtype)
    lines = []
    for h in range(count):
        own = rows[:, h * HEAD_DIM:(h + 1) * HEAD_DIM]
        lines.append(jnp.concatenate([own if k == h else zero for k in range(count)], axis=1))
    return jnp.concatenate(lines, axis=0)


def softmax(scores, axis):
    weights = jnp.exp2(scores - jnp.max(scores, axis=axis, keepdims=True))
    inverse = 1.0 / jnp.sum(weights, axis=axis, keepdims=True)
    return (weights * inverse).astype(jnp.bfloat16)


def gather_kernel(
    heads_axis, full_width,
    src_ref, nq_hbm, nk_hbm, nv_hbm, sk_hbm, sv_hbm, dq_hbm, out_ref,
    nq, nk, nv, dq, *rest,
):
    kbufs, vbufs = rest[:GROUPS], rest[GROUPS:2 * GROUPS]
    (own_out, mixing, asked, enc, squares_acc, row_scale, key_scale,
     stat1, stat2, peer1, peer2, behind2,
     in_sem, dq_sem, local_sem, send_sem, recv_sem,
     stat_send, stat_recv, prior_send, prior_recv) = rest[2 * GROUPS:]
    per_device = nq.shape[0]
    seg_dev = dq.shape[0]
    columns = nq.shape[2]
    width = columns // GROUPS
    group_heads = width // HEAD_DIM
    span = lax.axis_size("span")
    me = lax.axis_index("span")
    lane = lax.axis_index("head")
    core, across, along = me ^ 1, me ^ 2, me ^ 4
    after = lax.rem(me + 1, span)
    before = lax.rem(me + span - 1, span)
    softmax_scale = HEAD_DIM ** (-0.5) / math.log(2.0)

    barrier = pltpu.get_barrier_semaphore()
    greeted = 0
    for target in (core, across, along):
        pl.semaphore_signal(barrier, inc=1, device_id={"span": target, "head": lane}, device_id_type=MESH)
        greeted += 1
    for k in range(1, heads_axis):
        other = lax.rem(lane + k, heads_axis)
        pl.semaphore_signal(barrier, inc=1, device_id={"span": me, "head": other}, device_id_type=MESH)
        greeted += 1
    for k in range(heads_axis):
        other = lax.rem(lane + k, heads_axis)
        for target in (after, before):
            pl.semaphore_signal(barrier, inc=1, device_id={"span": target, "head": other}, device_id_type=MESH)
            greeted += 1
    pl.semaphore_wait(barrier, greeted)

    chunks = 2 * GROUPS

    def buffer(j):
        return (kbufs + vbufs)[j]

    def source(j):
        hbm = (sk_hbm, sv_hbm)[j // GROUPS]
        return hbm.at[:, :, pl.ds((j % GROUPS) * width, width)]

    def block(j, owner):
        return buffer(j).at[pl.ds(owner * seg_dev, seg_dev)]

    def half(j, owner, part):
        rows = seg_dev // 2
        return buffer(j).at[pl.ds(owner * seg_dev + part * rows, rows)]

    sent = {}

    def push(kind, j, src, dst, target):
        copy = pltpu.make_async_remote_copy(
            src_ref=src, dst_ref=dst, send_sem=send_sem.at[kind, j], recv_sem=recv_sem.at[kind, j],
            device_id={"span": target, "head": lane}, device_id_type=MESH)
        copy.start()
        sent[kind, j] = copy

    def direct(j):
        push(0, j, source(j), block(j, me), across)
        push(1, j, source(j), block(j, me), along)

    local = []
    for j in range(chunks):
        direct(j)

    for i in range(per_device):
        for a, (hbm, vm) in enumerate(((nq_hbm, nq), (nk_hbm, nk), (nv_hbm, nv))):
            pltpu.make_async_copy(hbm.at[i], vm.at[i], in_sem.at[a, i]).start()
    dq_copy = pltpu.make_async_copy(dq_hbm, dq, dq_sem)
    dq_copy.start()

    for j in range(chunks):
        push(4, j, source(j), block(j, me), core)
        copy = pltpu.make_async_copy(source(j), block(j, me), local_sem.at[j])
        copy.start()
        local.append(copy)

    def forward(j):
        for part in range(2):
            sent[2 + part, j].wait_recv()
            push(7 + part, j, half(j, me ^ 6, part), half(j, me ^ 6, part), core)

    def step(j):
        sent[1, j].wait_recv()
        push(2, j, half(j, along, 0), half(j, along, 0), across)
        sent[0, j].wait_recv()
        push(3, j, half(j, across, 1), half(j, across, 1), along)
        push(5, j, block(j, across), block(j, across), core)
        push(6, j, block(j, along), block(j, along), core)

    def arrived(j):
        local[j].wait()
        for kind in (4, 5, 6, 7, 8):
            sent[kind, j].wait_recv()

    def self_step(i, carry):
        for a, (hbm, vm) in enumerate(((nq_hbm, nq), (nk_hbm, nk), (nv_hbm, nv))):
            pltpu.make_async_copy(hbm.at[i], vm.at[i], in_sem.at[a, i]).wait()
        total = jnp.zeros((NBR_LEN, HEAD_DIM), jnp.float32)
        for base in range(0, columns // HEAD_DIM, 8):
            together = range(base, base + 8)
            cols = [pl.ds(h * HEAD_DIM, HEAD_DIM) for h in together]
            scores = [dot_t(nk[i, :, c], nq[i, :, c]) * softmax_scale for c in cols]
            weights = [softmax(x, 0) for x in scores]
            outs = [dot_first(w, nv[i, :, c]).astype(jnp.bfloat16) for w, c in zip(weights, cols)]
            for h, o in zip(together, outs):
                own_out[h // group_heads, i, :, pl.ds((h % group_heads) * HEAD_DIM, HEAD_DIM)] = o
                wide = o.astype(jnp.float32)
                total = total + wide * wide
        stat1[pl.ds(i, 1), :] = jnp.sum(total.T, axis=0, keepdims=True)
        return carry

    def exchange(kind, stat, peer):
        out = []
        for k in range(1, heads_axis):
            other = lax.rem(lane + k, heads_axis)
            copy = pltpu.make_async_remote_copy(
                src_ref=stat, dst_ref=peer.at[k - 1],
                send_sem=stat_send.at[kind, k - 1], recv_sem=stat_recv.at[kind, k - 1],
                device_id={"span": me, "head": other}, device_id_type=MESH)
            copy.start()
            out.append(copy)
        return out

    def weigh(g):
        arrived(g)

        def some(t, carry):
            rows = [4 * t + b for b in range(4)]
            keys = [apart(kbufs[g][src_ref[i % NEIGHBOURS, i // NEIGHBOURS]]) for i in rows]
            scores = [dot_t(k, own_out[g, i]) * row_scale[pl.ds(i, 1), :] for k, i in zip(keys, rows)]
            weights = [softmax(x.reshape(group_heads, SEG_LEN, NBR_LEN), 1) for x in scores]
            for i, w in zip(rows, weights):
                mixing[g, i] = w.reshape(group_heads * SEG_LEN, NBR_LEN)
            return carry

        lax.fori_loop(0, per_device // 4, some, 0)

    def cross_rows(g, rows):
        values = [apart(vbufs[g][src_ref[i % NEIGHBOURS, i // NEIGHBOURS]]) for i in rows]
        crossed = [dot_first(mixing[g, i], v).astype(jnp.bfloat16) for i, v in zip(rows, values)]
        for i, x in zip(rows, crossed):
            both = (own_out[g, i].astype(jnp.float32) + x.astype(jnp.float32)).astype(jnp.bfloat16)
            enc[g, NEIGHBOURS + i] = both
            wide = both.astype(jnp.float32)
            wide = wide * wide
            total = wide[:, :HEAD_DIM]
            for h in range(1, group_heads):
                total = total + wide[:, h * HEAD_DIM:(h + 1) * HEAD_DIM]
            if g > 0:
                total = total + squares_acc[i]
            if g < GROUPS - 1:
                squares_acc[i] = total
            else:
                stat2[pl.ds(i, 1), :] = jnp.sum(total.T, axis=0, keepdims=True)

    prior = []

    def panel(g, u):
        return enc[g, pl.ds(NEIGHBOURS * u, NEIGHBOURS)].reshape(NEIGHBOURS * NBR_LEN, width)

    def ask(g, u):
        asked[u, g] = dot_t(panel(g, u), apart(dq[u, :, pl.ds(g * width, width)]))

    def cross(g):
        arrived(GROUPS + g)
        cross_rows(g, list(range(per_device - NEIGHBOURS, per_device)))
        copy = pltpu.make_async_remote_copy(
            src_ref=enc.at[g, pl.ds(per_device, NEIGHBOURS)], dst_ref=enc.at[g, pl.ds(0, NEIGHBOURS)],
            send_sem=prior_send.at[g], recv_sem=prior_recv.at[g],
            device_id={"span": after, "head": lane}, device_id_type=MESH)
        copy.start()
        prior.append(copy)

        def rest_step(t, carry):
            cross_rows(g, [3 * t + b for b in range(3)])
            return carry

        lax.fori_loop(0, (per_device - NEIGHBOURS) // 3, rest_step, 0)

    quarter = per_device // 4
    for j in range(4):
        lax.fori_loop(j * quarter, (j + 1) * quarter, self_step, 0)
        if j > 0:
            step(2 * j - 2)
            step(2 * j - 1)
    first_stats = exchange(0, stat1, peer1)
    step(6)
    for copy in first_stats:
        copy.wait_recv()
    total1 = stat1[...]
    for k in range(heads_axis - 1):
        total1 = total1 + peer1[k]
    row_scale[...] = lax.rsqrt(total1 / full_width + epsilon) * softmax_scale
    step(7)
    forward(0)
    for g in range(GROUPS):
        forward(g + 1)
        weigh(g)
    dq_copy.wait()
    for g in range(GROUPS):
        if g + 1 < GROUPS:
            forward(GROUPS + 1 + g)
        cross(g)
        if g + 1 < GROUPS:
            for u in range(1, seg_dev):
                ask(g, u)

    second_stats = exchange(1, stat2, peer2)
    behind_stats = []
    for k in range(heads_axis):
        other = lax.rem(lane + k, heads_axis)
        copy = pltpu.make_async_remote_copy(
            src_ref=stat2, dst_ref=behind2.at[k],
            send_sem=stat_send.at[2, k], recv_sem=stat_recv.at[2, k],
            device_id={"span": after, "head": other}, device_id_type=MESH)
        copy.start()
        behind_stats.append(copy)
    for u in range(1, seg_dev):
        ask(GROUPS - 1, u)
    for copy in second_stats:
        copy.wait_recv()
    total2 = stat2[...]
    for k in range(heads_axis - 1):
        total2 = total2 + peer2[k]
    key_scale[pl.ds(NEIGHBOURS, per_device), :] = lax.rsqrt(total2 / full_width + epsilon) * softmax_scale

    def decode_step(u, carry):
        scale = jnp.concatenate([
            jnp.broadcast_to(key_scale[pl.ds(NEIGHBOURS * u + n, 1), :], (NBR_LEN, NBR_LEN)).T
            for n in range(NEIGHBOURS)], axis=0)
        weights = [softmax(asked[u, g] * scale, 0) for g in range(GROUPS)]
        outs = [dot_first(w, panel(g, u)).astype(jnp.bfloat16) for g, w in enumerate(weights)]
        for g, out in enumerate(outs):
            for h in range(group_heads):
                lo = h * HEAD_DIM
                out_ref[u, :, pl.ds(g * width + lo, HEAD_DIM)] = out[h * SEG_LEN:(h + 1) * SEG_LEN, lo:lo + HEAD_DIM]
        return carry

    lax.fori_loop(1, seg_dev, decode_step, 0)
    for copy in behind_stats:
        copy.wait_recv()
    for copy in prior:
        copy.wait_recv()
    total3 = behind2[0]
    for k in range(1, heads_axis):
        total3 = total3 + behind2[k]
    total3 = lax.rsqrt(total3 / full_width + epsilon) * softmax_scale
    key_scale[pl.ds(0, NEIGHBOURS), :] = total3[per_device - NEIGHBOURS:]

    @pl.when(me == 0)
    def _():
        enc[:, pl.ds(0, NEIGHBOURS)] = jnp.zeros((GROUPS, NEIGHBOURS, NBR_LEN, width), jnp.bfloat16)

    for g in range(GROUPS):
        ask(g, 0)
    decode_step(0, 0)
    for copy in list(sent.values()) + prior + first_stats + second_stats + behind_stats:
        copy.wait_send()


def gather_all(operands):
    columns = operands[1].shape[2]
    heads_axis = lax.axis_size("head")
    span = lax.axis_size("span")
    per_device = SEG_DEV * NEIGHBOURS
    width = columns // GROUPS
    bf16, f32 = jnp.bfloat16, jnp.float32
    neighbour_shape = (per_device, NBR_LEN, columns)
    segment_shape = (SEG_DEV, SEG_LEN, columns)
    chunks = 2 * GROUPS
    any_space = pl.BlockSpec(memory_space=pltpu.HBM)
    dma = pltpu.SemaphoreType.DMA
    return pl.pallas_call(
        functools.partial(gather_kernel, heads_axis, columns * heads_axis),
        out_shape=jax.ShapeDtypeStruct(segment_shape, bf16),
        in_specs=[pl.BlockSpec(memory_space=pltpu.SMEM)] + [any_space] * 6,
        out_specs=pl.BlockSpec(memory_space=pltpu.VMEM),
        scratch_shapes=[pltpu.VMEM(neighbour_shape, bf16)] * 3
        + [pltpu.VMEM(segment_shape, bf16)]
        + [pltpu.VMEM((span * SEG_DEV, SEG_LEN, width), bf16)] * chunks
        + [
            pltpu.VMEM((GROUPS, per_device, NBR_LEN, width), bf16),
            pltpu.VMEM((GROUPS, per_device, width // HEAD_DIM * SEG_LEN, NBR_LEN), bf16),
            pltpu.VMEM((SEG_DEV, GROUPS, NEIGHBOURS * NBR_LEN, width // HEAD_DIM * SEG_LEN), f32),
            pltpu.VMEM((GROUPS, per_device + NEIGHBOURS, NBR_LEN, width), bf16),
            pltpu.VMEM((per_device, NBR_LEN, HEAD_DIM), f32),
            pltpu.VMEM((per_device, NBR_LEN), f32),
            pltpu.VMEM((per_device + NEIGHBOURS, NBR_LEN), f32),
            pltpu.VMEM((per_device, NBR_LEN), f32),
            pltpu.VMEM((per_device, NBR_LEN), f32),
            pltpu.VMEM((heads_axis - 1, per_device, NBR_LEN), f32),
            pltpu.VMEM((heads_axis - 1, per_device, NBR_LEN), f32),
            pltpu.VMEM((heads_axis, per_device, NBR_LEN), f32),
            dma((3, per_device)),
            dma,
            dma((chunks,)),
            dma((9, chunks)),
            dma((9, chunks)),
            dma((3, heads_axis)),
            dma((3, heads_axis)),
            dma((GROUPS,)),
            dma((GROUPS,)),
        ],
        compiler_params=pltpu.CompilerParams(
            collective_id=1, has_side_effects=True, vmem_limit_bytes=53 * 1024 * 1024),
    )(*operands)


PHASES = (2, 3, 3)
SLOTS = sum(PHASES)
STARTS = tuple(sum(PHASES[:p]) for p in range(len(PHASES)))
FORWARDS = (0, 0, 1, 2, 2, 3, 4, 5)
CHIP_SEGS = 8
LANES = 128


def routes(needs, mine):
    f32, bf16 = jnp.float32, jnp.bfloat16
    lane = lax.broadcasted_iota(jnp.int32, (1, LANES), 1)
    chip = lane // CHIP_SEGS
    within = (lane % CHIP_SEGS).astype(f32)

    def at(k):
        total = jnp.zeros((1, LANES), f32)
        for t, row in enumerate(needs):
            total = total + jnp.where((chip ^ k) == t, row, 0.0)
        return total

    n1, n2, n3 = at(1), at(2), at(3)
    only1, only2 = n3 * n1 * (1 - n2), n3 * n2 * (1 - n1)
    both, none = n3 * n1 * n2, n3 * (1 - n1) * (1 - n2)
    upper = lax.broadcasted_iota(jnp.int32, (LANES, LANES), 0)
    lower = lax.broadcasted_iota(jnp.int32, (LANES, LANES), 1)
    row_chip, column_chip = upper // CHIP_SEGS, lower // CHIP_SEGS
    same = jnp.where(row_chip == column_chip, 1.0, 0.0)
    ahead = jnp.where(upper < lower, same, 0.0)
    others = [jnp.where((row_chip ^ k) == column_chip, 1.0, 0.0) for k in range(1, 4)]
    select = jnp.concatenate([same] + others + [ahead], axis=1).astype(bf16)
    zero = jnp.zeros((1, LANES), f32)
    stacked = jnp.concatenate([n1, n2, only1, only2, both, none, zero, zero], axis=0)
    counts = jnp.dot(stacked.astype(bf16), select, preferred_element_type=f32)

    def count(r):
        return [counts[r:r + 1, k * LANES:(k + 1) * LANES] for k in range(4)]

    def rank(r):
        return counts[r:r + 1, 4 * LANES:]

    n1c, n2c, o1, o2, b, n = [count(r) for r in range(6)]
    every = range(4)

    def clip(value, top):
        return jnp.minimum(jnp.maximum(value, 0.0), top)

    x = [n1c[k] + o2[k ^ 2] for k in every]
    y = [n2c[k] + o1[k ^ 1] for k in every]
    pb = [clip(jnp.floor((b[k] + x[k ^ 2] - y[k ^ 1] + 1) * 0.5), b[k]) for k in every]
    x = [x[k] + b[k ^ 2] - pb[k ^ 2] for k in every]
    y = [y[k] + pb[k ^ 1] for k in every]
    pn = [clip(jnp.floor((n[k] + jnp.maximum(y[k], x[k ^ 2]) - jnp.maximum(x[k], y[k ^ 1]) + 1) * 0.5), n[k])
          for k in every]
    x, y = ([x[k] + pn[k] + n[k ^ 2] - pn[k ^ 2] for k in every],
            [y[k] + n[k] - pn[k] + pn[k ^ 1] for k in every])
    over1 = [jnp.maximum(x[k], y[k ^ 1]) - SLOTS for k in every]
    over2 = [jnp.maximum(y[k], x[k ^ 2]) - SLOTS for k in every]
    shift = [clip(jnp.minimum(over2[k], -over1[k]), n[k] - pn[k]) - clip(jnp.minimum(over1[k], -over2[k]), pn[k])
             for k in every]
    pn = [pn[k] + shift[k] for k in every]
    x, y = ([x[k] + shift[k] - shift[k ^ 2] for k in every],
            [y[k] - shift[k] + shift[k ^ 1] for k in every])
    m1 = [clip(jnp.minimum(y[k ^ 1] - SLOTS, SLOTS - jnp.maximum(y[k], x[k ^ 2])), o1[k]) for k in every]
    m2 = [clip(jnp.minimum(x[k ^ 2] - SLOTS, SLOTS - jnp.maximum(x[k], y[k ^ 1])), o2[k]) for k in every]

    def below(r, limit, rows):
        return jnp.where(rank(r) < limit, rows, 0.0)

    path1 = only1 - below(2, m1[0], only1) + below(3, m2[0], only2) + below(4, pb[0], both) + below(5, pn[0], none)
    path2 = n3 - path1
    own_x, own_y = jnp.maximum(n1, path1), jnp.maximum(n2, path2)
    stacked = jnp.concatenate(
        [path1, path2, own_x - path1, own_y - path2, zero, zero, zero, zero], axis=0)
    again = jnp.dot(stacked.astype(bf16), jnp.concatenate([same, ahead], axis=1).astype(bf16),
                    preferred_element_type=f32)
    relays, ranks = again[:, :LANES], again[:, LANES:]
    slot_x = jnp.where(path1 > 0, ranks[0:1], relays[0:1] + ranks[2:3])
    slot_y = jnp.where(path2 > 0, ranks[1:2], relays[1:2] + ranks[3:4])

    def forwarded(own, place):
        return jnp.maximum(own, jnp.where(place < 2, 2.0, 3.0)) + place

    forward_y = forwarded(n2c[1] + n[1] - pn[1] + m1[1], ranks[0:1])
    forward_x = forwarded(n1c[2] + pn[2] + m2[2], ranks[1:2])
    last = jnp.maximum(path1 * forward_y, path2 * forward_x)
    over = jnp.max(jnp.where(last >= SLOTS, 1.0, 0.0), axis=1, keepdims=True)

    side = chip ^ mine
    place = jnp.where(
        side == 0, within,
        CHIP_SEGS + jnp.where(
            side == 1, slot_x,
            jnp.where(side == 2, SLOTS + slot_y, jnp.where(path1 > 0, SLOTS + forward_y, forward_x))))
    place = jnp.minimum(place, CHIP_SEGS + 2 * SLOTS - 1.0)

    def sends(own, slot, relay, forward, arrives):
        mine_own = (side == 0) & (own > 0)
        number = jnp.where(mine_own, slot, jnp.where(relay, forward, -1.0))
        code = jnp.where(mine_own, within, CHIP_SEGS + arrives)
        wanted = lax.broadcasted_iota(jnp.int32, (SLOTS, LANES), 0).astype(f32)
        return jnp.sum(jnp.where(number == wanted, code, 0.0), axis=1, keepdims=True)

    send_x = sends(own_x, slot_x, (side == 2) & (path2 > 0), forward_x, slot_y)
    send_y = sends(own_y, slot_y, (side == 1) & (path1 > 0), forward_y, slot_x)
    rows = [send_x, send_y, place, over]
    return jnp.concatenate([jnp.broadcast_to(r, (8, LANES)) for r in rows], axis=0).astype(jnp.int32)


ORDER = ((0, 0), (1, 0), (2, 0), (0, 1), (1, 1), (3, 0), (0, 2), (1, 2), (2, 1), (3, 1), (2, 2), (3, 2))


def kernel(
    heads_axis, full_width,
    src_ref, nq_hbm, nk_hbm, nv_hbm, sk_hbm, sv_hbm, dq_hbm, out_ref, over_ref,
    nq, nk, nv, dq, *rest,
):
    own_a, own_b, recv_a, recv_b, send_a = (rest[4 * j:4 * j + 4] for j in range(5))
    (need, needs, table, lookup, own_out, mixing, asked, enc, squares_acc, row_scale, key_scale,
     stat1, stat2, peer1, peer2, behind2,
     in_sem, dq_sem, local_sem, table_sem, need_send, need_recv, core_send, core_recv,
     link_send, link_recv, pass_send, pass_recv,
     stat_send, stat_recv, prior_send, prior_recv) = rest[20:]
    per_device = nq.shape[0]
    seg_dev = dq.shape[1]
    columns = nq.shape[2]
    width = columns // GROUPS
    group_heads = width // HEAD_DIM
    span = lax.axis_size("span")
    me = lax.axis_index("span")
    lane = lax.axis_index("head")
    side = lax.rem(me, 2)
    core, across, along = me ^ 1, me ^ 2, me ^ 4
    after = lax.rem(me + 1, span)
    before = lax.rem(me + span - 1, span)
    softmax_scale = HEAD_DIM ** (-0.5) / math.log(2.0)

    def at(target, head):
        return {"span": target, "head": head}

    def columns_of(half, q):
        return pl.ds(pl.multiple_of((2 * half + q) * width, width), width)

    def source(k, half):
        hbm = (sk_hbm, sv_hbm)[k % 2]
        return hbm.at[:, :, columns_of(half, k // 2)]

    mine_rows = pl.ds(pl.multiple_of(side * seg_dev, seg_dev), seg_dev)

    def inputs(i):
        return [pltpu.make_async_copy(hbm.at[i], vm.at[i], in_sem.at[a, i])
                for a, (hbm, vm) in enumerate(((nq_hbm, nq), (nk_hbm, nk), (nv_hbm, nv)))]

    for i in range(2):
        for copy in inputs(i):
            copy.start()
    local = {}
    for k in range(4):
        for b, (own, half) in enumerate(((own_a[k], side), (own_b[k], 1 - side))):
            copy = pltpu.make_async_copy(source(k, half), own.at[mine_rows], local_sem.at[b, k])
            copy.start()
            local[b, k] = copy
    for i in range(2, per_device):
        for copy in inputs(i):
            copy.start()
    dq_copies = []
    for g in range(GROUPS):
        copy = pltpu.make_async_copy(dq_hbm.at[:, :, pl.ds(g * width, width)], dq.at[g], dq_sem.at[g])
        copy.start()
        dq_copies.append(copy)

    segment = lax.broadcasted_iota(jnp.int32, (8, LANES), 1)
    wanted = jnp.zeros((8, LANES), jnp.float32)
    for i in range(per_device):
        wanted = jnp.where(segment == src_ref[i % NEIGHBOURS, i // NEIGHBOURS], 1.0, wanted)
    need[...] = wanted

    barrier = pltpu.get_barrier_semaphore()
    greeted = 0
    for k in range(1, span):
        pl.semaphore_signal(barrier, inc=1, device_id=at(me ^ k, lane), device_id_type=MESH)
        greeted += 1
    for k in range(1, heads_axis):
        other = lax.rem(lane + k, heads_axis)
        for target in (me, after, before):
            pl.semaphore_signal(barrier, inc=1, device_id=at(target, other), device_id_type=MESH)
            greeted += 1
    pl.semaphore_wait(barrier, greeted)

    def remote(src, dst, send_sem, recv_sem, target):
        copy = pltpu.make_async_remote_copy(
            src_ref=src, dst_ref=dst, send_sem=send_sem, recv_sem=recv_sem,
            device_id=at(*target), device_id_type=MESH)
        copy.start()
        return copy

    told = [remote(need, needs.at[me], need_send.at[k - 1], need_recv.at[k - 1], (me ^ k, lane))
            for k in range(1, span)]
    needs[me] = wanted
    given = {}
    for k in range(4):
        given[0, k] = remote(source(k, 1 - side), own_a[k].at[mine_rows], core_send.at[0, k], core_recv.at[0, k],
                             (core, lane))
        given[1, k] = remote(source(k, side), own_b[k].at[mine_rows], core_send.at[1, k], core_recv.at[1, k],
                             (core, lane))

    def owned(b, k):
        local[b, k].wait()
        given[b, k].wait_recv()

    sent, passed = {}, {}

    def slots(link, p):
        return pl.ds(link * SLOTS + STARTS[p], PHASES[p])

    def hand_on(k, p):
        for link in range(2):
            sent[k, p, link].wait_recv()
            block = slots(link, p)
            passed[k, p, link] = remote(recv_a[k].at[block], recv_b[k].at[block], pass_send.at[link, 3 * k + p],
                                        pass_recv.at[link, 3 * k + p], (core, lane))

    def advance(k, p):
        if p == 0:
            owned(0, k)
        else:
            hand_on(k, p - 1)
        for link, target in enumerate((across, along)):
            for i in range(STARTS[p], STARTS[p] + PHASES[p]):
                code = lookup[8 * link + i, 0]
                rows = own_a[k][jnp.clip(code, 0, CHIP_SEGS - 1)]
                for t in range(FORWARDS[i]):
                    rows = jnp.where(code == CHIP_SEGS + t, recv_a[k][(1 - link) * SLOTS + t], rows)
                send_a[k][link * SLOTS + i] = rows
            block = slots(link, p)
            sent[k, p, link] = remote(send_a[k].at[block], recv_a[k].at[block], link_send.at[link, 3 * k + p],
                                      link_recv.at[link, 3 * k + p], (target, lane))

    def finish(k):
        hand_on(k, len(PHASES) - 1)

    def arrived(b, k):
        if b == 1:
            owned(1, k)
            for p in range(len(PHASES)):
                for link in range(2):
                    passed[k, p, link].wait_recv()

    def rows_of(b, k, i):
        place = lookup[16, src_ref[i % NEIGHBOURS, i // NEIGHBOURS]]
        own, recv = ((own_a[k], recv_a[k]), (own_b[k], recv_b[k]))[b]
        return jnp.where(place < CHIP_SEGS, own[jnp.clip(place, 0, CHIP_SEGS - 1)],
                         recv[jnp.clip(place - CHIP_SEGS, 0, 2 * SLOTS - 1)])

    def self_step(i, carry):
        for copy in inputs(i):
            copy.wait()
        total = jnp.zeros((NBR_LEN, HEAD_DIM), jnp.float32)
        for base in range(0, columns // HEAD_DIM, 8):
            together = range(base, base + 8)
            cols = [pl.ds(h * HEAD_DIM, HEAD_DIM) for h in together]
            scores = [dot_t(nk[i, :, c], nq[i, :, c]) * softmax_scale for c in cols]
            weights = [softmax(x, 0) for x in scores]
            outs = [dot_first(w, nv[i, :, c]).astype(jnp.bfloat16) for w, c in zip(weights, cols)]
            for h, o in zip(together, outs):
                own_out[h // group_heads, i, :, pl.ds((h % group_heads) * HEAD_DIM, HEAD_DIM)] = o
                wide = o.astype(jnp.float32)
                total = total + wide * wide
        stat1[pl.ds(i, 1), :] = jnp.sum(total.T, axis=0, keepdims=True)
        return carry

    def exchange(kind, stat, peer):
        return [remote(stat, peer.at[k - 1], stat_send.at[kind, k - 1], stat_recv.at[kind, k - 1],
                       (me, lax.rem(lane + k, heads_axis))) for k in range(1, heads_axis)]

    def group(b, q):
        return 2 * (side if b == 0 else 1 - side) + q

    def weigh(b, q):
        arrived(b, 2 * q)
        g = group(b, q)

        def some(t, carry):
            rows = [4 * t + s for s in range(4)]
            keys = [apart(rows_of(b, 2 * q, i)) for i in rows]
            scores = [dot_t(k, own_out[g, i]) * row_scale[pl.ds(i, 1), :] for k, i in zip(keys, rows)]
            weights = [softmax(x.reshape(group_heads, SEG_LEN, NBR_LEN), 1) for x in scores]
            for i, w in zip(rows, weights):
                mixing[g, i] = w.reshape(group_heads * SEG_LEN, NBR_LEN)
            return carry

        lax.fori_loop(0, per_device // 4, some, 0)

    def cross_rows(b, q, rows):
        g = group(b, q)
        values = [apart(rows_of(b, 2 * q + 1, i)) for i in rows]
        crossed = [dot_first(mixing[g, i], v).astype(jnp.bfloat16) for i, v in zip(rows, values)]
        for i, x in zip(rows, crossed):
            both = (own_out[g, i].astype(jnp.float32) + x.astype(jnp.float32)).astype(jnp.bfloat16)
            enc[g, NEIGHBOURS + i] = both
            wide = both.astype(jnp.float32)
            wide = wide * wide
            total = wide[:, :HEAD_DIM]
            for h in range(1, group_heads):
                total = total + wide[:, h * HEAD_DIM:(h + 1) * HEAD_DIM]
            if (q, b) != (0, 0):
                total = total + squares_acc[i]
            if (q, b) != (1, 1):
                squares_acc[i] = total
            else:
                stat2[pl.ds(i, 1), :] = jnp.sum(total.T, axis=0, keepdims=True)

    prior = []

    def panel(g, u):
        return enc[g, pl.ds(NEIGHBOURS * u, NEIGHBOURS)].reshape(NEIGHBOURS * NBR_LEN, width)

    def ask(g, u):
        asked[u, g] = dot_t(panel(g, u), apart(dq[g, u]))

    def cross(b, q):
        arrived(b, 2 * q + 1)
        cross_rows(b, q, list(range(per_device - NEIGHBOURS, per_device)))
        g = group(b, q)
        prior.append(remote(
            enc.at[g, pl.ds(per_device, NEIGHBOURS)], enc.at[g, pl.ds(0, NEIGHBOURS)],
            prior_send.at[2 * q + b], prior_recv.at[2 * q + b], (after, lane)))

        def rest_step(t, carry):
            cross_rows(b, q, [3 * t + s for s in range(3)])
            return carry

        lax.fori_loop(0, (per_device - NEIGHBOURS) // 3, rest_step, 0)

    lax.fori_loop(0, 2, self_step, 0)
    for copy in told:
        copy.wait_recv()
    table[...] = routes([jnp.maximum(needs[2 * t][:1], needs[2 * t + 1][:1]) for t in range(span // 2)], me // 2)
    copy = pltpu.make_async_copy(table, lookup, table_sem)
    copy.start()
    copy.wait()
    for k, p in ORDER[:3]:
        advance(k, p)
    lax.fori_loop(2, 4, self_step, 0)
    advance(*ORDER[3])
    lax.fori_loop(4, 6, self_step, 0)
    advance(*ORDER[4])
    lax.fori_loop(6, per_device, self_step, 0)
    first_stats = exchange(0, stat1, peer1)
    advance(*ORDER[5])
    for copy in first_stats:
        copy.wait_recv()
    total1 = stat1[...]
    for k in range(heads_axis - 1):
        total1 = total1 + peer1[k]
    row_scale[...] = lax.rsqrt(total1 / full_width + epsilon) * softmax_scale
    for k, p in ORDER[6:10]:
        advance(k, p)
    for copy in dq_copies:
        copy.wait()
    finish(0)
    weigh(0, 0)
    weigh(1, 0)
    finish(1)
    cross(0, 0)
    advance(*ORDER[10])
    cross(1, 0)
    advance(*ORDER[11])
    for b in range(2):
        for u in range(1, seg_dev):
            ask(group(b, 0), u)
    finish(2)
    weigh(0, 1)
    weigh(1, 1)
    finish(3)
    cross(0, 1)
    cross(1, 1)

    second_stats = exchange(1, stat2, peer2)
    behind_stats = [
        remote(stat2, behind2.at[k], stat_send.at[2, k], stat_recv.at[2, k], (after, lax.rem(lane + k, heads_axis)))
        for k in range(heads_axis)]
    for b in range(2):
        for u in range(1, seg_dev):
            ask(group(b, 1), u)
    for copy in second_stats:
        copy.wait_recv()
    total2 = stat2[...]
    for k in range(heads_axis - 1):
        total2 = total2 + peer2[k]
    key_scale[pl.ds(NEIGHBOURS, per_device), :] = lax.rsqrt(total2 / full_width + epsilon) * softmax_scale

    def decode_step(u, carry):
        scale = jnp.concatenate([
            jnp.broadcast_to(key_scale[pl.ds(NEIGHBOURS * u + n, 1), :], (NBR_LEN, NBR_LEN)).T
            for n in range(NEIGHBOURS)], axis=0)
        weights = [softmax(asked[u, g] * scale, 0) for g in range(GROUPS)]
        outs = [dot_first(w, panel(g, u)).astype(jnp.bfloat16) for g, w in enumerate(weights)]
        for g, out in enumerate(outs):
            for h in range(group_heads):
                lo = h * HEAD_DIM
                out_ref[u, :, pl.ds(g * width + lo, HEAD_DIM)] = out[h * SEG_LEN:(h + 1) * SEG_LEN, lo:lo + HEAD_DIM]
        return carry

    lax.fori_loop(1, seg_dev, decode_step, 0)
    for copy in behind_stats:
        copy.wait_recv()
    for copy in prior:
        copy.wait_recv()
    total3 = behind2[0]
    for k in range(1, heads_axis):
        total3 = total3 + behind2[k]
    total3 = lax.rsqrt(total3 / full_width + epsilon) * softmax_scale
    key_scale[pl.ds(0, NEIGHBOURS), :] = total3[per_device - NEIGHBOURS:]

    @pl.when(me == 0)
    def _():
        enc[:, pl.ds(0, NEIGHBOURS)] = jnp.zeros((GROUPS, NEIGHBOURS, NBR_LEN, width), jnp.bfloat16)

    for g in range(GROUPS):
        ask(g, 0)
    decode_step(0, 0)
    over_ref[0, 0] = lookup[24, 0]
    for copy in (told + list(given.values()) + list(sent.values()) + list(passed.values()) + prior
                 + first_stats + second_stats + behind_stats):
        copy.wait_send()


def fused_body(
    neighbour_query,
    neighbour_key,
    neighbour_value,
    segment_key,
    segment_value,
    decoder_query,
    sources,
):
    columns = neighbour_query.shape[1]
    heads_axis = lax.axis_size("head")
    span = lax.axis_size("span")
    per_device = SEG_DEV * NEIGHBOURS
    width = columns // GROUPS
    bf16, f32 = jnp.bfloat16, jnp.float32
    neighbour_shape = (per_device, NBR_LEN, columns)
    segment_shape = (SEG_DEV, SEG_LEN, columns)
    any_space = pl.BlockSpec(memory_space=pltpu.HBM)
    dma = pltpu.SemaphoreType.DMA
    own = pltpu.VMEM((CHIP_SEGS, SEG_LEN, width), bf16)
    slots = pltpu.VMEM((2 * SLOTS, SEG_LEN, width), bf16)
    steps = 4 * len(PHASES)
    operands = (
        sources.T,
        neighbour_query.reshape(neighbour_shape),
        neighbour_key.reshape(neighbour_shape),
        neighbour_value.reshape(neighbour_shape),
        segment_key.reshape(segment_shape),
        segment_value.reshape(segment_shape),
        decoder_query.reshape(segment_shape),
    )
    out, over = pl.pallas_call(
        functools.partial(kernel, heads_axis, columns * heads_axis),
        out_shape=(jax.ShapeDtypeStruct(segment_shape, bf16), jax.ShapeDtypeStruct((1, 1), jnp.int32)),
        in_specs=[pl.BlockSpec(memory_space=pltpu.SMEM)] + [any_space] * 6,
        out_specs=(pl.BlockSpec(memory_space=pltpu.VMEM), pl.BlockSpec(memory_space=pltpu.SMEM)),
        scratch_shapes=[pltpu.VMEM(neighbour_shape, bf16)] * 3
        + [pltpu.VMEM((GROUPS, SEG_DEV, SEG_LEN, width), bf16)]
        + [own] * 8 + [slots] * 12
        + [
            pltpu.VMEM((8, LANES), f32),
            pltpu.VMEM((span, 8, LANES), f32),
            pltpu.VMEM((32, LANES), jnp.int32),
            pltpu.SMEM((32, LANES), jnp.int32),
            pltpu.VMEM((GROUPS, per_device, NBR_LEN, width), bf16),
            pltpu.VMEM((GROUPS, per_device, width // HEAD_DIM * SEG_LEN, NBR_LEN), bf16),
            pltpu.VMEM((SEG_DEV, GROUPS, NEIGHBOURS * NBR_LEN, width // HEAD_DIM * SEG_LEN), f32),
            pltpu.VMEM((GROUPS, per_device + NEIGHBOURS, NBR_LEN, width), bf16),
            pltpu.VMEM((per_device, NBR_LEN, HEAD_DIM), f32),
            pltpu.VMEM((per_device, NBR_LEN), f32),
            pltpu.VMEM((per_device + NEIGHBOURS, NBR_LEN), f32),
            pltpu.VMEM((per_device, NBR_LEN), f32),
            pltpu.VMEM((per_device, NBR_LEN), f32),
            pltpu.VMEM((heads_axis - 1, per_device, NBR_LEN), f32),
            pltpu.VMEM((heads_axis - 1, per_device, NBR_LEN), f32),
            pltpu.VMEM((heads_axis, per_device, NBR_LEN), f32),
            dma((3, per_device)),
            dma((GROUPS,)),
            dma((2, 4)),
            dma,
            dma((span - 1,)),
            dma((span - 1,)),
            dma((2, 4)),
            dma((2, 4)),
            dma((2, steps)),
            dma((2, steps)),
            dma((2, steps)),
            dma((2, steps)),
            dma((3, heads_axis)),
            dma((3, heads_axis)),
            dma((GROUPS,)),
            dma((GROUPS,)),
        ],
        compiler_params=pltpu.CompilerParams(
            collective_id=0, has_side_effects=True, vmem_limit_bytes=53 * 1024 * 1024),
    )(*operands)
    return lax.cond(
        over[0, 0] > 0,
        lambda: gather_all(operands).reshape(SEG_DEV * SEG_LEN, columns),
        lambda: out.reshape(SEG_DEV * SEG_LEN, columns),
    )


def solution(mesh):
    placed = (
        P("span", "head"),
        P("span", "head"),
        P("span", "head"),
        P("span", "head"),
        P("span", "head"),
        P("span", "head"),
        P("span", None),
    )
    cube = mesh.shape["span"] == 2 * 2 * 2
    return jax.shard_map(
        fused_body if cube else body, mesh=mesh, in_specs=placed, out_specs=P("span", "head"), check_vma=False
    )
```

```python
import functools
import math

import jax
import jax.numpy as jnp
from jax import lax
from jax.experimental import pallas as pl
from jax.experimental.pallas import tpu as pltpu
from jax.sharding import PartitionSpec as P

HEAD_DIM = 128
SEG_LEN = 64
NBR_LEN = 128
NEIGHBOURS = 2
SEG_DEV = 4


epsilon = 1e-06


def from_behind(x, axis, by):
    count = lax.axis_size(axis)
    pairs = [(i, i + by) for i in range(count) if 0 <= i + by < count]
    return lax.ppermute(x, axis, pairs)


def attend(query_rows, key_rows, value_rows):
    groups, length, columns = query_rows.shape
    head_count = columns // HEAD_DIM
    query_heads = query_rows.reshape(groups, length, head_count, HEAD_DIM)
    key_heads = key_rows.reshape(groups, key_rows.shape[1], head_count, HEAD_DIM)
    value_heads = value_rows.reshape(groups, value_rows.shape[1], head_count, HEAD_DIM)
    logit_scores = jnp.einsum(
        "bqhd,bkhd->bhqk", query_heads, key_heads, preferred_element_type=jnp.float32
    ) * HEAD_DIM ** (-0.5)
    logit_scores = logit_scores - jnp.max(logit_scores, axis=-1, keepdims=True)
    weights = jnp.exp(logit_scores)
    weights = (weights / jnp.sum(weights, axis=-1, keepdims=True)).astype(jnp.bfloat16)
    output = jnp.einsum("bhqk,bkhd->bqhd", weights, value_heads, preferred_element_type=jnp.float32)
    return output.reshape(groups, length, columns)


def squares(rows):
    wide = rows.astype(jnp.float32)
    return jnp.sum(wide * wide, axis=-1)


def normalize(rows, totals, full_width):
    scale = lax.rsqrt(totals / full_width + epsilon)
    return (rows.astype(jnp.float32) * scale[:, None]).astype(jnp.bfloat16)


def pick(blocks, index):
    chosen = (index[:, None] == jnp.arange(blocks.shape[0])[None, :]).astype(blocks.dtype)
    return jnp.einsum("ws,slc->wlc", chosen, blocks, preferred_element_type=jnp.float32).astype(blocks.dtype)


def body(
    neighbour_query,
    neighbour_key,
    neighbour_value,
    segment_key,
    segment_value,
    decoder_query,
    sources,
):
    columns = neighbour_query.shape[1]
    full_width = columns * lax.axis_size("head")
    devices = lax.axis_size("span")
    per_device = SEG_DEV * NEIGHBOURS
    capacity = max(2, 2 * per_device // devices)
    panel_rows = NEIGHBOURS * NBR_LEN
    self_out = attend(
        neighbour_query.reshape(per_device, NBR_LEN, columns),
        neighbour_key.reshape(per_device, NBR_LEN, columns),
        neighbour_value.reshape(per_device, NBR_LEN, columns),
    ).astype(jnp.bfloat16)
    flat_self = self_out.reshape(per_device * NBR_LEN, columns)
    totals = lax.psum(squares(flat_self), "head")
    cross_query = normalize(flat_self, totals, full_width).reshape(per_device, NBR_LEN, columns)
    listed = sources.reshape(per_device)
    owners = listed // SEG_DEV
    within = listed % SEG_DEV
    position = jnp.arange(per_device)
    earlier = (owners[:, None] == owners[None, :]) & (position[:, None] > position[None, :])
    ranked = jnp.sum(earlier.astype(jnp.int32), axis=1)
    slots = owners * capacity + ranked
    picked = (slots[:, None] == jnp.arange(devices * capacity)[None, :]).astype(jnp.int32)
    request = jnp.sum(picked * (within + 1)[:, None], axis=0).reshape(devices, capacity)
    asked = lax.all_to_all(request, "span", split_axis=0, concat_axis=0, tiled=True)
    wanted = jnp.maximum(asked - 1, 0).reshape(devices * capacity)
    own_keys = pick(segment_key.reshape(SEG_DEV, SEG_LEN, columns), wanted)
    own_values = pick(segment_value.reshape(SEG_DEV, SEG_LEN, columns), wanted)
    got_keys, got_values = (
        lax.all_to_all(
            own_keys.reshape(devices, capacity, SEG_LEN, columns),
            "span",
            split_axis=0,
            concat_axis=0,
            tiled=True,
        ),
        lax.all_to_all(
            own_values.reshape(devices, capacity, SEG_LEN, columns),
            "span",
            split_axis=0,
            concat_axis=0,
            tiled=True,
        ),
    )
    source_keys = pick(got_keys.reshape(devices * capacity, SEG_LEN, columns), slots)
    source_values = pick(got_values.reshape(devices * capacity, SEG_LEN, columns), slots)
    crossed = attend(cross_query, source_keys, source_values).astype(jnp.bfloat16)
    encoded = (self_out.astype(jnp.float32) + crossed.astype(jnp.float32)).astype(jnp.bfloat16)
    encoded = encoded.reshape(per_device * NBR_LEN, columns)
    key_totals = lax.psum(squares(encoded), "head")
    keys_all = normalize(encoded, key_totals, full_width)
    before_keys, before_values = from_behind(
        (keys_all[-panel_rows:], encoded[-panel_rows:]), "span", 1
    )
    used_keys = jnp.concatenate([before_keys, keys_all[:-panel_rows]], axis=0)
    used_values = jnp.concatenate([before_values, encoded[:-panel_rows]], axis=0)
    blended = attend(
        decoder_query.reshape(SEG_DEV, SEG_LEN, columns),
        used_keys.reshape(SEG_DEV, panel_rows, columns),
        used_values.reshape(SEG_DEV, panel_rows, columns),
    ).astype(jnp.bfloat16)
    return blended.reshape(SEG_DEV * SEG_LEN, columns)


MESH = pl.DeviceIdType.MESH
GROUPS = 4


def dot_t(a, b):
    return lax.dot_general(a, b, (((1,), (1,)), ((), ())), preferred_element_type=jnp.float32)


def dot_first(a, b):
    return lax.dot_general(a, b, (((0,), (0,)), ((), ())), preferred_element_type=jnp.float32)


def apart(rows):
    count = rows.shape[1] // HEAD_DIM
    zero = jnp.zeros((rows.shape[0], HEAD_DIM), rows.dtype)
    lines = []
    for h in range(count):
        own = rows[:, h * HEAD_DIM:(h + 1) * HEAD_DIM]
        lines.append(jnp.concatenate([own if k == h else zero for k in range(count)], axis=1))
    return jnp.concatenate(lines, axis=0)


def softmax(scores, axis):
    weights = jnp.exp2(scores - jnp.max(scores, axis=axis, keepdims=True))
    inverse = 1.0 / jnp.sum(weights, axis=axis, keepdims=True)
    return (weights * inverse).astype(jnp.bfloat16)


def gather_kernel(
    heads_axis, full_width,
    src_ref, nq_hbm, nk_hbm, nv_hbm, sk_hbm, sv_hbm, dq_hbm, out_ref,
    nq, nk, nv, dq, *rest,
):
    kbufs, vbufs = rest[:GROUPS], rest[GROUPS:2 * GROUPS]
    (own_out, mixing, asked, enc, squares_acc, row_scale, key_scale,
     stat1, stat2, peer1, peer2, behind2,
     in_sem, dq_sem, local_sem, send_sem, recv_sem,
     stat_send, stat_recv, prior_send, prior_recv) = rest[2 * GROUPS:]
    per_device = nq.shape[0]
    seg_dev = dq.shape[0]
    columns = nq.shape[2]
    width = columns // GROUPS
    group_heads = width // HEAD_DIM
    span = lax.axis_size("span")
    me = lax.axis_index("span")
    lane = lax.axis_index("head")
    core, across, along = me ^ 1, me ^ 2, me ^ 4
    after = lax.rem(me + 1, span)
    before = lax.rem(me + span - 1, span)
    softmax_scale = HEAD_DIM ** (-0.5) / math.log(2.0)

    barrier = pltpu.get_barrier_semaphore()
    greeted = 0
    for target in (core, across, along):
        pl.semaphore_signal(barrier, inc=1, device_id={"span": target, "head": lane}, device_id_type=MESH)
        greeted += 1
    for k in range(1, heads_axis):
        other = lax.rem(lane + k, heads_axis)
        pl.semaphore_signal(barrier, inc=1, device_id={"span": me, "head": other}, device_id_type=MESH)
        greeted += 1
    for k in range(heads_axis):
        other = lax.rem(lane + k, heads_axis)
        for target in (after, before):
            pl.semaphore_signal(barrier, inc=1, device_id={"span": target, "head": other}, device_id_type=MESH)
            greeted += 1
    pl.semaphore_wait(barrier, greeted)

    chunks = 2 * GROUPS

    def buffer(j):
        return (kbufs + vbufs)[j]

    def source(j):
        hbm = (sk_hbm, sv_hbm)[j // GROUPS]
        return hbm.at[:, :, pl.ds((j % GROUPS) * width, width)]

    def block(j, owner):
        return buffer(j).at[pl.ds(owner * seg_dev, seg_dev)]

    def half(j, owner, part):
        rows = seg_dev // 2
        return buffer(j).at[pl.ds(owner * seg_dev + part * rows, rows)]

    sent = {}

    def push(kind, j, src, dst, target):
        copy = pltpu.make_async_remote_copy(
            src_ref=src, dst_ref=dst, send_sem=send_sem.at[kind, j], recv_sem=recv_sem.at[kind, j],
            device_id={"span": target, "head": lane}, device_id_type=MESH)
        copy.start()
        sent[kind, j] = copy

    def direct(j):
        push(0, j, source(j), block(j, me), across)
        push(1, j, source(j), block(j, me), along)

    local = []
    for j in range(chunks):
        direct(j)

    for i in range(per_device):
        for a, (hbm, vm) in enumerate(((nq_hbm, nq), (nk_hbm, nk), (nv_hbm, nv))):
            pltpu.make_async_copy(hbm.at[i], vm.at[i], in_sem.at[a, i]).start()
    dq_copy = pltpu.make_async_copy(dq_hbm, dq, dq_sem)
    dq_copy.start()

    for j in range(chunks):
        push(4, j, source(j), block(j, me), core)
        copy = pltpu.make_async_copy(source(j), block(j, me), local_sem.at[j])
        copy.start()
        local.append(copy)

    def forward(j):
        for part in range(2):
            sent[2 + part, j].wait_recv()
            push(7 + part, j, half(j, me ^ 6, part), half(j, me ^ 6, part), core)

    def step(j):
        sent[1, j].wait_recv()
        push(2, j, half(j, along, 0), half(j, along, 0), across)
        sent[0, j].wait_recv()
        push(3, j, half(j, across, 1), half(j, across, 1), along)
        push(5, j, block(j, across), block(j, across), core)
        push(6, j, block(j, along), block(j, along), core)

    def arrived(j):
        local[j].wait()
        for kind in (4, 5, 6, 7, 8):
            sent[kind, j].wait_recv()

    def self_step(i, carry):
        for a, (hbm, vm) in enumerate(((nq_hbm, nq), (nk_hbm, nk), (nv_hbm, nv))):
            pltpu.make_async_copy(hbm.at[i], vm.at[i], in_sem.at[a, i]).wait()
        total = jnp.zeros((NBR_LEN, HEAD_DIM), jnp.float32)
        for base in range(0, columns // HEAD_DIM, 8):
            together = range(base, base + 8)
            cols = [pl.ds(h * HEAD_DIM, HEAD_DIM) for h in together]
            scores = [dot_t(nk[i, :, c], nq[i, :, c]) * softmax_scale for c in cols]
            weights = [softmax(x, 0) for x in scores]
            outs = [dot_first(w, nv[i, :, c]).astype(jnp.bfloat16) for w, c in zip(weights, cols)]
            for h, o in zip(together, outs):
                own_out[h // group_heads, i, :, pl.ds((h % group_heads) * HEAD_DIM, HEAD_DIM)] = o
                wide = o.astype(jnp.float32)
                total = total + wide * wide
        stat1[pl.ds(i, 1), :] = jnp.sum(total.T, axis=0, keepdims=True)
        return carry

    def exchange(kind, stat, peer):
        out = []
        for k in range(1, heads_axis):
            other = lax.rem(lane + k, heads_axis)
            copy = pltpu.make_async_remote_copy(
                src_ref=stat, dst_ref=peer.at[k - 1],
                send_sem=stat_send.at[kind, k - 1], recv_sem=stat_recv.at[kind, k - 1],
                device_id={"span": me, "head": other}, device_id_type=MESH)
            copy.start()
            out.append(copy)
        return out

    def weigh(g):
        arrived(g)

        def some(t, carry):
            rows = [4 * t + b for b in range(4)]
            keys = [apart(kbufs[g][src_ref[i % NEIGHBOURS, i // NEIGHBOURS]]) for i in rows]
            scores = [dot_t(k, own_out[g, i]) * row_scale[pl.ds(i, 1), :] for k, i in zip(keys, rows)]
            weights = [softmax(x.reshape(group_heads, SEG_LEN, NBR_LEN), 1) for x in scores]
            for i, w in zip(rows, weights):
                mixing[g, i] = w.reshape(group_heads * SEG_LEN, NBR_LEN)
            return carry

        lax.fori_loop(0, per_device // 4, some, 0)

    def cross_rows(g, rows):
        values = [apart(vbufs[g][src_ref[i % NEIGHBOURS, i // NEIGHBOURS]]) for i in rows]
        crossed = [dot_first(mixing[g, i], v).astype(jnp.bfloat16) for i, v in zip(rows, values)]
        for i, x in zip(rows, crossed):
            both = (own_out[g, i].astype(jnp.float32) + x.astype(jnp.float32)).astype(jnp.bfloat16)
            enc[g, NEIGHBOURS + i] = both
            wide = both.astype(jnp.float32)
            wide = wide * wide
            total = wide[:, :HEAD_DIM]
            for h in range(1, group_heads):
                total = total + wide[:, h * HEAD_DIM:(h + 1) * HEAD_DIM]
            if g > 0:
                total = total + squares_acc[i]
            if g < GROUPS - 1:
                squares_acc[i] = total
            else:
                stat2[pl.ds(i, 1), :] = jnp.sum(total.T, axis=0, keepdims=True)

    prior = []

    def panel(g, u):
        return enc[g, pl.ds(NEIGHBOURS * u, NEIGHBOURS)].reshape(NEIGHBOURS * NBR_LEN, width)

    def ask(g, u):
        asked[u, g] = dot_t(panel(g, u), apart(dq[u, :, pl.ds(g * width, width)]))

    def cross(g):
        arrived(GROUPS + g)
        cross_rows(g, list(range(per_device - NEIGHBOURS, per_device)))
        copy = pltpu.make_async_remote_copy(
            src_ref=enc.at[g, pl.ds(per_device, NEIGHBOURS)], dst_ref=enc.at[g, pl.ds(0, NEIGHBOURS)],
            send_sem=prior_send.at[g], recv_sem=prior_recv.at[g],
            device_id={"span": after, "head": lane}, device_id_type=MESH)
        copy.start()
        prior.append(copy)

        def rest_step(t, carry):
            cross_rows(g, [3 * t + b for b in range(3)])
            return carry

        lax.fori_loop(0, (per_device - NEIGHBOURS) // 3, rest_step, 0)

    quarter = per_device // 4
    for j in range(4):
        lax.fori_loop(j * quarter, (j + 1) * quarter, self_step, 0)
        if j > 0:
            step(2 * j - 2)
            step(2 * j - 1)
    first_stats = exchange(0, stat1, peer1)
    step(6)
    for copy in first_stats:
        copy.wait_recv()
    total1 = stat1[...]
    for k in range(heads_axis - 1):
        total1 = total1 + peer1[k]
    row_scale[...] = lax.rsqrt(total1 / full_width + epsilon) * softmax_scale
    step(7)
    forward(0)
    for g in range(GROUPS):
        forward(g + 1)
        weigh(g)
    dq_copy.wait()
    for g in range(GROUPS):
        if g + 1 < GROUPS:
            forward(GROUPS + 1 + g)
        cross(g)
        if g + 1 < GROUPS:
            for u in range(1, seg_dev):
                ask(g, u)

    second_stats = exchange(1, stat2, peer2)
    behind_stats = []
    for k in range(heads_axis):
        other = lax.rem(lane + k, heads_axis)
        copy = pltpu.make_async_remote_copy(
            src_ref=stat2, dst_ref=behind2.at[k],
            send_sem=stat_send.at[2, k], recv_sem=stat_recv.at[2, k],
            device_id={"span": after, "head": other}, device_id_type=MESH)
        copy.start()
        behind_stats.append(copy)
    for u in range(1, seg_dev):
        ask(GROUPS - 1, u)
    for copy in second_stats:
        copy.wait_recv()
    total2 = stat2[...]
    for k in range(heads_axis - 1):
        total2 = total2 + peer2[k]
    key_scale[pl.ds(NEIGHBOURS, per_device), :] = lax.rsqrt(total2 / full_width + epsilon) * softmax_scale

    def decode_step(u, carry):
        scale = jnp.concatenate([
            jnp.broadcast_to(key_scale[pl.ds(NEIGHBOURS * u + n, 1), :], (NBR_LEN, NBR_LEN)).T
            for n in range(NEIGHBOURS)], axis=0)
        weights = [softmax(asked[u, g] * scale, 0) for g in range(GROUPS)]
        outs = [dot_first(w, panel(g, u)).astype(jnp.bfloat16) for g, w in enumerate(weights)]
        for g, out in enumerate(outs):
            for h in range(group_heads):
                lo = h * HEAD_DIM
                out_ref[u, :, pl.ds(g * width + lo, HEAD_DIM)] = out[h * SEG_LEN:(h + 1) * SEG_LEN, lo:lo + HEAD_DIM]
        return carry

    lax.fori_loop(1, seg_dev, decode_step, 0)
    for copy in behind_stats:
        copy.wait_recv()
    for copy in prior:
        copy.wait_recv()
    total3 = behind2[0]
    for k in range(1, heads_axis):
        total3 = total3 + behind2[k]
    total3 = lax.rsqrt(total3 / full_width + epsilon) * softmax_scale
    key_scale[pl.ds(0, NEIGHBOURS), :] = total3[per_device - NEIGHBOURS:]

    @pl.when(me == 0)
    def _():
        enc[:, pl.ds(0, NEIGHBOURS)] = jnp.zeros((GROUPS, NEIGHBOURS, NBR_LEN, width), jnp.bfloat16)

    for g in range(GROUPS):
        ask(g, 0)
    decode_step(0, 0)
    for copy in list(sent.values()) + prior + first_stats + second_stats + behind_stats:
        copy.wait_send()


def gather_all(operands):
    columns = operands[1].shape[2]
    heads_axis = lax.axis_size("head")
    span = lax.axis_size("span")
    per_device = SEG_DEV * NEIGHBOURS
    width = columns // GROUPS
    bf16, f32 = jnp.bfloat16, jnp.float32
    neighbour_shape = (per_device, NBR_LEN, columns)
    segment_shape = (SEG_DEV, SEG_LEN, columns)
    chunks = 2 * GROUPS
    any_space = pl.BlockSpec(memory_space=pltpu.HBM)
    dma = pltpu.SemaphoreType.DMA
    return pl.pallas_call(
        functools.partial(gather_kernel, heads_axis, columns * heads_axis),
        out_shape=jax.ShapeDtypeStruct(segment_shape, bf16),
        in_specs=[pl.BlockSpec(memory_space=pltpu.SMEM)] + [any_space] * 6,
        out_specs=pl.BlockSpec(memory_space=pltpu.VMEM),
        scratch_shapes=[pltpu.VMEM(neighbour_shape, bf16)] * 3
        + [pltpu.VMEM(segment_shape, bf16)]
        + [pltpu.VMEM((span * SEG_DEV, SEG_LEN, width), bf16)] * chunks
        + [
            pltpu.VMEM((GROUPS, per_device, NBR_LEN, width), bf16),
            pltpu.VMEM((GROUPS, per_device, width // HEAD_DIM * SEG_LEN, NBR_LEN), bf16),
            pltpu.VMEM((SEG_DEV, GROUPS, NEIGHBOURS * NBR_LEN, width // HEAD_DIM * SEG_LEN), f32),
            pltpu.VMEM((GROUPS, per_device + NEIGHBOURS, NBR_LEN, width), bf16),
            pltpu.VMEM((per_device, NBR_LEN, HEAD_DIM), f32),
            pltpu.VMEM((per_device, NBR_LEN), f32),
            pltpu.VMEM((per_device + NEIGHBOURS, NBR_LEN), f32),
            pltpu.VMEM((per_device, NBR_LEN), f32),
            pltpu.VMEM((per_device, NBR_LEN), f32),
            pltpu.VMEM((heads_axis - 1, per_device, NBR_LEN), f32),
            pltpu.VMEM((heads_axis - 1, per_device, NBR_LEN), f32),
            pltpu.VMEM((heads_axis, per_device, NBR_LEN), f32),
            dma((3, per_device)),
            dma,
            dma((chunks,)),
            dma((9, chunks)),
            dma((9, chunks)),
            dma((3, heads_axis)),
            dma((3, heads_axis)),
            dma((GROUPS,)),
            dma((GROUPS,)),
        ],
        compiler_params=pltpu.CompilerParams(
            collective_id=1, has_side_effects=True, vmem_limit_bytes=53 * 1024 * 1024),
    )(*operands)


PHASES = (2, 3, 3)
SLOTS = sum(PHASES)
STARTS = tuple(sum(PHASES[:p]) for p in range(len(PHASES)))
FORWARDS = (0, 0, 1, 2, 2, 3, 4, 5)
CHIP_SEGS = 8
LANES = 128


def selections():
    upper = lax.broadcasted_iota(jnp.int32, (LANES, LANES), 0)
    lower = lax.broadcasted_iota(jnp.int32, (LANES, LANES), 1)
    row_chip, column_chip = upper // CHIP_SEGS, lower // CHIP_SEGS
    same = jnp.where(row_chip == column_chip, 1.0, 0.0)
    ahead = jnp.where(upper < lower, same, 0.0)
    others = [jnp.where((row_chip ^ k) == column_chip, 1.0, 0.0) for k in range(1, 4)]
    return jnp.concatenate(others + [same, ahead], axis=1).astype(jnp.bfloat16)


def routes(needs, select, mine):
    f32, bf16 = jnp.float32, jnp.bfloat16
    lane = lax.broadcasted_iota(jnp.int32, (1, LANES), 1)
    chip = lane // CHIP_SEGS
    within = (lane % CHIP_SEGS).astype(f32)

    def at(k):
        total = jnp.zeros((1, LANES), f32)
        for t, row in enumerate(needs):
            total = total + jnp.where((chip ^ k) == t, row, 0.0)
        return total

    n1, n2, n3 = at(1), at(2), at(3)
    only1, only2 = n3 * n1 * (1 - n2), n3 * n2 * (1 - n1)
    both, none = n3 * n1 * n2, n3 * (1 - n1) * (1 - n2)
    zero = jnp.zeros((1, LANES), f32)
    stacked = jnp.concatenate([n1, n2, only1, only2, both, none, zero, zero], axis=0)
    counts = jnp.dot(stacked.astype(bf16), select, preferred_element_type=f32)

    def count(r):
        return [counts[r:r + 1, k * LANES:(k + 1) * LANES] for k in (3, 0, 1, 2)]

    def rank(r):
        return counts[r:r + 1, 4 * LANES:]

    n1c, n2c, o1, o2, b, n = [count(r) for r in range(6)]
    every = range(4)

    def clip(value, top):
        return jnp.minimum(jnp.maximum(value, 0.0), top)

    x = [n1c[k] + o2[k ^ 2] for k in every]
    y = [n2c[k] + o1[k ^ 1] for k in every]
    pb = [clip(jnp.floor((b[k] + x[k ^ 2] - y[k ^ 1] + 1) * 0.5), b[k]) for k in every]
    x = [x[k] + b[k ^ 2] - pb[k ^ 2] for k in every]
    y = [y[k] + pb[k ^ 1] for k in every]
    pn = [clip(jnp.floor((n[k] + jnp.maximum(y[k], x[k ^ 2]) - jnp.maximum(x[k], y[k ^ 1]) + 1) * 0.5), n[k])
          for k in every]
    x, y = ([x[k] + pn[k] + n[k ^ 2] - pn[k ^ 2] for k in every],
            [y[k] + n[k] - pn[k] + pn[k ^ 1] for k in every])
    over1 = [jnp.maximum(x[k], y[k ^ 1]) - SLOTS for k in every]
    over2 = [jnp.maximum(y[k], x[k ^ 2]) - SLOTS for k in every]
    shift = [clip(jnp.minimum(over2[k], -over1[k]), n[k] - pn[k]) - clip(jnp.minimum(over1[k], -over2[k]), pn[k])
             for k in every]
    pn = [pn[k] + shift[k] for k in every]
    x, y = ([x[k] + shift[k] - shift[k ^ 2] for k in every],
            [y[k] - shift[k] + shift[k ^ 1] for k in every])
    m1 = [clip(jnp.minimum(y[k ^ 1] - SLOTS, SLOTS - jnp.maximum(y[k], x[k ^ 2])), o1[k]) for k in every]
    m2 = [clip(jnp.minimum(x[k ^ 2] - SLOTS, SLOTS - jnp.maximum(x[k], y[k ^ 1])), o2[k]) for k in every]

    def below(r, limit, rows):
        return jnp.where(rank(r) < limit, rows, 0.0)

    path1 = only1 - below(2, m1[0], only1) + below(3, m2[0], only2) + below(4, pb[0], both) + below(5, pn[0], none)
    path2 = n3 - path1
    own_x, own_y = jnp.maximum(n1, path1), jnp.maximum(n2, path2)
    stacked = jnp.concatenate(
        [path1, path2, own_x - path1, own_y - path2, zero, zero, zero, zero], axis=0)
    again = jnp.dot(stacked.astype(bf16), select[:, 3 * LANES:], preferred_element_type=f32)
    relays, ranks = again[:, :LANES], again[:, LANES:]
    slot_x = jnp.where(path1 > 0, ranks[0:1], relays[0:1] + ranks[2:3])
    slot_y = jnp.where(path2 > 0, ranks[1:2], relays[1:2] + ranks[3:4])

    def forwarded(own, place):
        return jnp.maximum(own, jnp.where(place < 2, 2.0, 3.0)) + place

    forward_y = forwarded(n2c[1] + n[1] - pn[1] + m1[1], ranks[0:1])
    forward_x = forwarded(n1c[2] + pn[2] + m2[2], ranks[1:2])
    last = jnp.maximum(path1 * forward_y, path2 * forward_x)
    over = jnp.max(jnp.where(last >= SLOTS, 1.0, 0.0), axis=1, keepdims=True)

    side = chip ^ mine
    place = jnp.where(
        side == 0, within,
        CHIP_SEGS + jnp.where(
            side == 1, slot_x,
            jnp.where(side == 2, SLOTS + slot_y, jnp.where(path1 > 0, SLOTS + forward_y, forward_x))))
    place = jnp.minimum(place, CHIP_SEGS + 2 * SLOTS - 1.0)

    def sends(own, slot, relay, forward, arrives):
        mine_own = (side == 0) & (own > 0)
        number = jnp.where(mine_own, slot, jnp.where(relay, forward, -1.0))
        code = jnp.where(mine_own, within, CHIP_SEGS + arrives)
        wanted = lax.broadcasted_iota(jnp.int32, (SLOTS, LANES), 0).astype(f32)
        return jnp.sum(jnp.where(number == wanted, code, 0.0), axis=1, keepdims=True)

    send_x = sends(own_x, slot_x, (side == 2) & (path2 > 0), forward_x, slot_y)
    send_y = sends(own_y, slot_y, (side == 1) & (path1 > 0), forward_y, slot_x)
    rows = [send_x, send_y, place, over]
    return jnp.concatenate([jnp.broadcast_to(r, (8, LANES)) for r in rows], axis=0).astype(jnp.int32)


ORDER = ((0, 0), (1, 0), (2, 0), (0, 1), (1, 1), (3, 0), (0, 2), (1, 2), (2, 1), (3, 1), (2, 2), (3, 2))


def kernel(
    heads_axis, full_width,
    src_ref, nq_hbm, nk_hbm, nv_hbm, sk_hbm, sv_hbm, dq_hbm, out_ref, over_ref,
    nq, nk, nv, dq, *rest,
):
    own_a, own_b, recv_a, recv_b, send_a = (rest[4 * j:4 * j + 4] for j in range(5))
    (first, answer, first_sem, ask_send, ask_recv, answer_send, answer_recv, select, need, needs, table, lookup, own_out, mixing, asked, enc, squares_acc, row_scale, key_scale,
     stat1, stat2, peer1, peer2, peer3,
     in_sem, dq_sem, local_sem, table_sem, need_send, need_recv, core_send, core_recv,
     link_send, link_recv, pass_send, pass_recv,
     stat_send, stat_recv) = rest[20:]
    per_device = nq.shape[0]
    seg_dev = dq.shape[1]
    columns = nq.shape[2]
    width = columns // GROUPS
    group_heads = width // HEAD_DIM
    span = lax.axis_size("span")
    me = lax.axis_index("span")
    lane = lax.axis_index("head")
    side = lax.rem(me, 2)
    core, across, along = me ^ 1, me ^ 2, me ^ 4
    after = lax.rem(me + 1, span)
    before = lax.rem(me + span - 1, span)
    softmax_scale = HEAD_DIM ** (-0.5) / math.log(2.0)

    def at(target, head):
        return {"span": target, "head": head}

    def columns_of(half, q):
        return pl.ds(pl.multiple_of((2 * half + q) * width, width), width)

    def source(k, half):
        hbm = (sk_hbm, sv_hbm)[k % 2]
        return hbm.at[:, :, columns_of(half, k // 2)]

    mine_rows = pl.ds(pl.multiple_of(side * seg_dev, seg_dev), seg_dev)

    def inputs(i):
        return [pltpu.make_async_copy(hbm.at[i], vm.at[i], in_sem.at[a, i])
                for a, (hbm, vm) in enumerate(((nq_hbm, nq), (nk_hbm, nk), (nv_hbm, nv)))]

    for i in range(2):
        for copy in inputs(i):
            copy.start()
    local = {}
    for k in range(4):
        for b, (own, half) in enumerate(((own_a[k], side), (own_b[k], 1 - side))):
            copy = pltpu.make_async_copy(source(k, half), own.at[mine_rows], local_sem.at[b, k])
            copy.start()
            local[b, k] = copy
    for i in range(2, per_device):
        for copy in inputs(i):
            copy.start()
    dq_copies = []
    for g in range(GROUPS):
        copy = pltpu.make_async_copy(
            dq_hbm.at[pl.ds(1, seg_dev - 1), :, pl.ds(g * width, width)], dq.at[g, pl.ds(0, seg_dev - 1)],
            dq_sem.at[g])
        copy.start()
        dq_copies.append(copy)
    stat2[1] = jnp.zeros_like(stat2[1])

    @pl.when(me == 0)
    def _():
        pltpu.make_async_copy(dq_hbm.at[0], first, first_sem).start()

    @pl.when(me == span - 1)
    def _():
        for g in range(GROUPS):
            dq[g, seg_dev - 1] = jnp.zeros((SEG_LEN, width), jnp.bfloat16)

    segment = lax.broadcasted_iota(jnp.int32, (8, LANES), 1)
    wanted = jnp.zeros((8, LANES), jnp.float32)
    for i in range(per_device):
        wanted = jnp.where(segment == src_ref[i % NEIGHBOURS, i // NEIGHBOURS], 1.0, wanted)
    need[...] = wanted
    select[...] = selections()

    barrier = pltpu.get_barrier_semaphore()
    greeted = 0
    for k in range(1, span):
        pl.semaphore_signal(barrier, inc=1, device_id=at(me ^ k, lane), device_id_type=MESH)
        greeted += 1
    for k in range(1, heads_axis):
        other = lax.rem(lane + k, heads_axis)
        pl.semaphore_signal(barrier, inc=1, device_id=at(me, other), device_id_type=MESH)
        greeted += 1
    pl.semaphore_wait(barrier, greeted)

    def remote(src, dst, send_sem, recv_sem, target):
        copy = pltpu.make_async_remote_copy(
            src_ref=src, dst_ref=dst, send_sem=send_sem, recv_sem=recv_sem,
            device_id=at(*target), device_id_type=MESH)
        copy.start()
        return copy

    told = [remote(need, needs.at[me], need_send.at[k - 1], need_recv.at[k - 1], (me ^ k, lane))
            for k in range(1, span)]
    needs[me] = wanted

    def query_copy(g):
        return pltpu.make_async_remote_copy(
            src_ref=dq_hbm.at[0, :, pl.ds(g * width, width)], dst_ref=dq.at[g, seg_dev - 1],
            send_sem=ask_send.at[g], recv_sem=ask_recv.at[g], device_id=at(before, lane), device_id_type=MESH)

    def answer_copy(g):
        block = pl.ds(g * width, width)
        return pltpu.make_async_remote_copy(
            src_ref=answer.at[:, block], dst_ref=out_ref.at[0, :, block],
            send_sem=answer_send.at[g], recv_sem=answer_recv.at[g], device_id=at(after, lane), device_id_type=MESH)

    @pl.when(me > 0)
    def _():
        for g in range(GROUPS):
            query_copy(g).start()

    given = {}
    for k in range(4):
        given[0, k] = remote(source(k, 1 - side), own_a[k].at[mine_rows], core_send.at[0, k], core_recv.at[0, k],
                             (core, lane))
        given[1, k] = remote(source(k, side), own_b[k].at[mine_rows], core_send.at[1, k], core_recv.at[1, k],
                             (core, lane))

    def owned(b, k):
        local[b, k].wait()
        given[b, k].wait_recv()

    sent, passed = {}, {}

    def slots(link, p):
        return pl.ds(link * SLOTS + STARTS[p], PHASES[p])

    def hand_on(k, p):
        for link in range(2):
            sent[k, p, link].wait_recv()
            block = slots(link, p)
            passed[k, p, link] = remote(recv_a[k].at[block], recv_b[k].at[block], pass_send.at[link, 3 * k + p],
                                        pass_recv.at[link, 3 * k + p], (core, lane))

    def advance(k, p):
        if p == 0:
            owned(0, k)
        else:
            hand_on(k, p - 1)
        for link, target in enumerate((across, along)):
            for i in range(STARTS[p], STARTS[p] + PHASES[p]):
                code = lookup[8 * link + i, 0]
                rows = own_a[k][jnp.clip(code, 0, CHIP_SEGS - 1)]
                for t in range(FORWARDS[i]):
                    rows = jnp.where(code == CHIP_SEGS + t, recv_a[k][(1 - link) * SLOTS + t], rows)
                send_a[k][link * SLOTS + i] = rows
            block = slots(link, p)
            sent[k, p, link] = remote(send_a[k].at[block], recv_a[k].at[block], link_send.at[link, 3 * k + p],
                                      link_recv.at[link, 3 * k + p], (target, lane))

    def finish(k):
        hand_on(k, len(PHASES) - 1)

    def arrived(b, k):
        if b == 1:
            owned(1, k)
            for p in range(len(PHASES)):
                for link in range(2):
                    passed[k, p, link].wait_recv()

    def rows_of(b, k, i):
        place = lookup[16, src_ref[i % NEIGHBOURS, i // NEIGHBOURS]]
        own, recv = ((own_a[k], recv_a[k]), (own_b[k], recv_b[k]))[b]
        return jnp.where(place < CHIP_SEGS, own[jnp.clip(place, 0, CHIP_SEGS - 1)],
                         recv[jnp.clip(place - CHIP_SEGS, 0, 2 * SLOTS - 1)])

    def self_step(i, carry):
        for copy in inputs(i):
            copy.wait()
        total = jnp.zeros((NBR_LEN, HEAD_DIM), jnp.float32)
        for base in range(0, columns // HEAD_DIM, 8):
            together = range(base, base + 8)
            cols = [pl.ds(h * HEAD_DIM, HEAD_DIM) for h in together]
            scores = [dot_t(nk[i, :, c], nq[i, :, c]) * softmax_scale for c in cols]
            weights = [softmax(x, 0) for x in scores]
            outs = [dot_first(w, nv[i, :, c]).astype(jnp.bfloat16) for w, c in zip(weights, cols)]
            for h, o in zip(together, outs):
                own_out[h // group_heads, i, :, pl.ds((h % group_heads) * HEAD_DIM, HEAD_DIM)] = o
                wide = o.astype(jnp.float32)
                total = total + wide * wide
        stat1[pl.ds(i, 1), :] = jnp.sum(total.T, axis=0, keepdims=True)
        return carry

    def exchange(kind, stat, peer):
        return [remote(stat, peer.at[k - 1], stat_send.at[kind, k - 1], stat_recv.at[kind, k - 1],
                       (me, lax.rem(lane + k, heads_axis))) for k in range(1, heads_axis)]

    def group(b, q):
        return 2 * (side if b == 0 else 1 - side) + q

    def weigh(b, q):
        arrived(b, 2 * q)
        g = group(b, q)

        def some(t, carry):
            rows = [4 * t + s for s in range(4)]
            keys = [apart(rows_of(b, 2 * q, i)) for i in rows]
            scores = [dot_t(k, own_out[g, i]) * row_scale[pl.ds(i, 1), :] for k, i in zip(keys, rows)]
            weights = [softmax(x.reshape(group_heads, SEG_LEN, NBR_LEN), 1) for x in scores]
            for i, w in zip(rows, weights):
                mixing[g, i] = w.reshape(group_heads * SEG_LEN, NBR_LEN)
            return carry

        lax.fori_loop(0, per_device // 4, some, 0)

    def cross_rows(b, q, rows):
        g = group(b, q)
        values = [apart(rows_of(b, 2 * q + 1, i)) for i in rows]
        crossed = [dot_first(mixing[g, i], v).astype(jnp.bfloat16) for i, v in zip(rows, values)]
        for i, x in zip(rows, crossed):
            both = (own_out[g, i].astype(jnp.float32) + x.astype(jnp.float32)).astype(jnp.bfloat16)
            enc[g, i] = both
            wide = both.astype(jnp.float32)
            wide = wide * wide
            total = wide[:, :HEAD_DIM]
            for h in range(1, group_heads):
                total = total + wide[:, h * HEAD_DIM:(h + 1) * HEAD_DIM]
            if (q, b) != (0, 0):
                total = total + squares_acc[i]
            if (q, b) != (1, 1):
                squares_acc[i] = total
            else:
                line = jnp.sum(total.T, axis=0, keepdims=True)
                stat2[0, pl.ds(i, 1), :] = line
                if len(rows) == NEIGHBOURS:
                    stat2[1, pl.ds(i, 1), :] = line

    def panel(g, u):
        return enc[g, pl.ds(NEIGHBOURS * u, NEIGHBOURS)].reshape(NEIGHBOURS * NBR_LEN, width)

    def ask(g, u):
        asked[u, g] = dot_t(panel(g, u), apart(dq[g, u]))

    def cross_last(b, q):
        arrived(b, 2 * q + 1)
        cross_rows(b, q, list(range(per_device - NEIGHBOURS, per_device)))

    def cross_others(b, q):
        def rest_step(t, carry):
            cross_rows(b, q, [3 * t + s for s in range(3)])
            return carry

        lax.fori_loop(0, (per_device - NEIGHBOURS) // 3, rest_step, 0)

    lax.fori_loop(0, 1, self_step, 0)
    for copy in told:
        copy.wait_recv()
    table[...] = routes([jnp.maximum(needs[2 * t][:1], needs[2 * t + 1][:1]) for t in range(span // 2)],
                        select[...], me // 2)
    copy = pltpu.make_async_copy(table, lookup, table_sem)
    copy.start()
    copy.wait()
    for k, p in ORDER[:3]:
        advance(k, p)
    lax.fori_loop(1, 4, self_step, 0)
    advance(*ORDER[3])
    lax.fori_loop(4, 6, self_step, 0)
    advance(*ORDER[4])
    lax.fori_loop(6, per_device, self_step, 0)
    first_stats = exchange(0, stat1, peer1)
    advance(*ORDER[5])
    for copy in first_stats:
        copy.wait_recv()
    total1 = stat1[...]
    for k in range(heads_axis - 1):
        total1 = total1 + peer1[k]
    row_scale[...] = lax.rsqrt(total1 / full_width + epsilon) * softmax_scale
    for k, p in ORDER[6:10]:
        advance(k, p)
    for copy in dq_copies:
        copy.wait()

    @pl.when(me < span - 1)
    def _():
        for g in range(GROUPS):
            query_copy(g).wait_recv()

    @pl.when(me == 0)
    def _():
        pltpu.make_async_copy(dq_hbm.at[0], first, first_sem).wait()
        for g in range(GROUPS):
            nothing = jnp.zeros((NEIGHBOURS * NBR_LEN, width), jnp.bfloat16)
            scores = dot_t(nothing, apart(first[:, g * width:(g + 1) * width])) * (epsilon ** -0.5 * softmax_scale)
            out = dot_first(softmax(scores, 0), nothing).astype(jnp.bfloat16)
            for h in range(group_heads):
                lo = h * HEAD_DIM
                out_ref[0, :, pl.ds(g * width + lo, HEAD_DIM)] = out[h * SEG_LEN:(h + 1) * SEG_LEN, lo:lo + HEAD_DIM]

    finish(0)
    weigh(0, 0)
    weigh(1, 0)
    finish(1)
    cross_last(0, 0)
    cross_others(0, 0)
    advance(*ORDER[10])
    cross_last(1, 0)
    cross_others(1, 0)
    advance(*ORDER[11])
    for b in range(2):
        for u in range(seg_dev):
            ask(group(b, 0), u)
    finish(2)
    weigh(0, 1)
    weigh(1, 1)
    finish(3)
    for b in range(2):
        cross_last(b, 1)
    last_stats = exchange(2, stat2.at[1], peer3)
    for b in range(2):
        cross_others(b, 1)
    second_stats = exchange(1, stat2.at[0], peer2)
    for b in range(2):
        for u in reversed(range(seg_dev)):
            ask(group(b, 1), u)

    def settle(mine, copies, peer, rows):
        for copy in copies:
            copy.wait_recv()
        total = mine
        for k in range(heads_axis - 1):
            total = total + peer[k]
        scale = lax.rsqrt(total / full_width + epsilon) * softmax_scale
        key_scale[rows] = scale[rows]

    def decoded(u):
        scale = jnp.concatenate([
            jnp.broadcast_to(key_scale[pl.ds(NEIGHBOURS * u + n, 1), :], (NBR_LEN, NBR_LEN)).T
            for n in range(NEIGHBOURS)], axis=0)
        weights = [softmax(asked[u, g] * scale, 0) for g in range(GROUPS)]
        outs = [dot_first(w, panel(g, u)).astype(jnp.bfloat16) for g, w in enumerate(weights)]
        for g, out in enumerate(outs):
            for h in range(group_heads):
                lo = h * HEAD_DIM
                yield g * width + lo, out[h * SEG_LEN:(h + 1) * SEG_LEN, lo:lo + HEAD_DIM]

    def decode_step(u, carry):
        for lo, out in decoded(u):
            out_ref[u + 1, :, pl.ds(lo, HEAD_DIM)] = out
        return carry

    settle(stat2[1], last_stats, peer3, slice(per_device - NEIGHBOURS, per_device))
    for lo, out in decoded(seg_dev - 1):
        answer[:, pl.ds(lo, HEAD_DIM)] = out

    @pl.when(me < span - 1)
    def _():
        for g in range(GROUPS):
            answer_copy(g).start()

    settle(stat2[0], second_stats, peer2, slice(0, per_device - NEIGHBOURS))
    lax.fori_loop(0, seg_dev - 1, decode_step, 0)
    over_ref[0, 0] = lookup[24, 0]

    @pl.when(me > 0)
    def _():
        for g in range(GROUPS):
            answer_copy(g).wait_recv()
            query_copy(g).wait_send()

    @pl.when(me < span - 1)
    def _():
        for g in range(GROUPS):
            answer_copy(g).wait_send()

    for copy in (told + list(given.values()) + list(sent.values()) + list(passed.values())
                 + first_stats + last_stats + second_stats):
        copy.wait_send()


def fused_body(
    neighbour_query,
    neighbour_key,
    neighbour_value,
    segment_key,
    segment_value,
    decoder_query,
    sources,
):
    columns = neighbour_query.shape[1]
    heads_axis = lax.axis_size("head")
    span = lax.axis_size("span")
    per_device = SEG_DEV * NEIGHBOURS
    width = columns // GROUPS
    bf16, f32 = jnp.bfloat16, jnp.float32
    neighbour_shape = (per_device, NBR_LEN, columns)
    segment_shape = (SEG_DEV, SEG_LEN, columns)
    any_space = pl.BlockSpec(memory_space=pltpu.HBM)
    dma = pltpu.SemaphoreType.DMA
    own = pltpu.VMEM((CHIP_SEGS, SEG_LEN, width), bf16)
    slots = pltpu.VMEM((2 * SLOTS, SEG_LEN, width), bf16)
    steps = 4 * len(PHASES)
    operands = (
        sources.T,
        neighbour_query.reshape(neighbour_shape),
        neighbour_key.reshape(neighbour_shape),
        neighbour_value.reshape(neighbour_shape),
        segment_key.reshape(segment_shape),
        segment_value.reshape(segment_shape),
        decoder_query.reshape(segment_shape),
    )
    out, over = pl.pallas_call(
        functools.partial(kernel, heads_axis, columns * heads_axis),
        out_shape=(jax.ShapeDtypeStruct(segment_shape, bf16), jax.ShapeDtypeStruct((1, 1), jnp.int32)),
        in_specs=[pl.BlockSpec(memory_space=pltpu.SMEM)] + [any_space] * 6,
        out_specs=(pl.BlockSpec(memory_space=pltpu.VMEM), pl.BlockSpec(memory_space=pltpu.SMEM)),
        scratch_shapes=[pltpu.VMEM(neighbour_shape, bf16)] * 3
        + [pltpu.VMEM((GROUPS, SEG_DEV, SEG_LEN, width), bf16)]
        + [own] * 8 + [slots] * 12
        + [
            pltpu.VMEM((SEG_LEN, columns), bf16),
            pltpu.VMEM((SEG_LEN, columns), bf16),
            dma,
            dma((GROUPS,)),
            dma((GROUPS,)),
            dma((GROUPS,)),
            dma((GROUPS,)),
            pltpu.VMEM((LANES, 5 * LANES), bf16),
            pltpu.VMEM((8, LANES), f32),
            pltpu.VMEM((span, 8, LANES), f32),
            pltpu.VMEM((32, LANES), jnp.int32),
            pltpu.SMEM((32, LANES), jnp.int32),
            pltpu.VMEM((GROUPS, per_device, NBR_LEN, width), bf16),
            pltpu.VMEM((GROUPS, per_device, width // HEAD_DIM * SEG_LEN, NBR_LEN), bf16),
            pltpu.VMEM((SEG_DEV, GROUPS, NEIGHBOURS * NBR_LEN, width // HEAD_DIM * SEG_LEN), f32),
            pltpu.VMEM((GROUPS, per_device, NBR_LEN, width), bf16),
            pltpu.VMEM((per_device, NBR_LEN, HEAD_DIM), f32),
            pltpu.VMEM((per_device, NBR_LEN), f32),
            pltpu.VMEM((per_device, NBR_LEN), f32),
            pltpu.VMEM((per_device, NBR_LEN), f32),
            pltpu.VMEM((2, per_device, NBR_LEN), f32),
            pltpu.VMEM((heads_axis - 1, per_device, NBR_LEN), f32),
            pltpu.VMEM((heads_axis - 1, per_device, NBR_LEN), f32),
            pltpu.VMEM((heads_axis - 1, per_device, NBR_LEN), f32),
            dma((3, per_device)),
            dma((GROUPS,)),
            dma((2, 4)),
            dma,
            dma((span - 1,)),
            dma((span - 1,)),
            dma((2, 4)),
            dma((2, 4)),
            dma((2, steps)),
            dma((2, steps)),
            dma((2, steps)),
            dma((2, steps)),
            dma((3, heads_axis)),
            dma((3, heads_axis)),
        ],
        compiler_params=pltpu.CompilerParams(
            collective_id=0, has_side_effects=True, vmem_limit_bytes=53 * 1024 * 1024),
    )(*operands)
    return lax.cond(
        over[0, 0] > 0,
        lambda: gather_all(operands).reshape(SEG_DEV * SEG_LEN, columns),
        lambda: out.reshape(SEG_DEV * SEG_LEN, columns),
    )


def solution(mesh):
    placed = (
        P("span", "head"),
        P("span", "head"),
        P("span", "head"),
        P("span", "head"),
        P("span", "head"),
        P("span", "head"),
        P("span", None),
    )
    cube = mesh.shape["span"] == 2 * 2 * 2
    return jax.shard_map(
        fused_body if cube else body, mesh=mesh, in_specs=placed, out_specs=P("span", "head"), check_vma=False
    )
```

```python
import functools
import math

import jax
import jax.numpy as jnp
from jax import lax
from jax.experimental import pallas as pl
from jax.experimental.pallas import tpu as pltpu
from jax.sharding import PartitionSpec as P

HEAD_DIM = 128
SEG_LEN = 64
NBR_LEN = 128
NEIGHBOURS = 2
SEG_DEV = 4


epsilon = 1e-06


def from_behind(x, axis, by):
    count = lax.axis_size(axis)
    pairs = [(i, i + by) for i in range(count) if 0 <= i + by < count]
    return lax.ppermute(x, axis, pairs)


def attend(query_rows, key_rows, value_rows):
    groups, length, columns = query_rows.shape
    head_count = columns // HEAD_DIM
    query_heads = query_rows.reshape(groups, length, head_count, HEAD_DIM)
    key_heads = key_rows.reshape(groups, key_rows.shape[1], head_count, HEAD_DIM)
    value_heads = value_rows.reshape(groups, value_rows.shape[1], head_count, HEAD_DIM)
    logit_scores = jnp.einsum(
        "bqhd,bkhd->bhqk", query_heads, key_heads, preferred_element_type=jnp.float32
    ) * HEAD_DIM ** (-0.5)
    logit_scores = logit_scores - jnp.max(logit_scores, axis=-1, keepdims=True)
    weights = jnp.exp(logit_scores)
    weights = (weights / jnp.sum(weights, axis=-1, keepdims=True)).astype(jnp.bfloat16)
    output = jnp.einsum("bhqk,bkhd->bqhd", weights, value_heads, preferred_element_type=jnp.float32)
    return output.reshape(groups, length, columns)


def squares(rows):
    wide = rows.astype(jnp.float32)
    return jnp.sum(wide * wide, axis=-1)


def normalize(rows, totals, full_width):
    scale = lax.rsqrt(totals / full_width + epsilon)
    return (rows.astype(jnp.float32) * scale[:, None]).astype(jnp.bfloat16)


def pick(blocks, index):
    chosen = (index[:, None] == jnp.arange(blocks.shape[0])[None, :]).astype(blocks.dtype)
    return jnp.einsum("ws,slc->wlc", chosen, blocks, preferred_element_type=jnp.float32).astype(blocks.dtype)


def body(
    neighbour_query,
    neighbour_key,
    neighbour_value,
    segment_key,
    segment_value,
    decoder_query,
    sources,
):
    columns = neighbour_query.shape[1]
    full_width = columns * lax.axis_size("head")
    devices = lax.axis_size("span")
    per_device = SEG_DEV * NEIGHBOURS
    capacity = max(2, 2 * per_device // devices)
    panel_rows = NEIGHBOURS * NBR_LEN
    self_out = attend(
        neighbour_query.reshape(per_device, NBR_LEN, columns),
        neighbour_key.reshape(per_device, NBR_LEN, columns),
        neighbour_value.reshape(per_device, NBR_LEN, columns),
    ).astype(jnp.bfloat16)
    flat_self = self_out.reshape(per_device * NBR_LEN, columns)
    totals = lax.psum(squares(flat_self), "head")
    cross_query = normalize(flat_self, totals, full_width).reshape(per_device, NBR_LEN, columns)
    listed = sources.reshape(per_device)
    owners = listed // SEG_DEV
    within = listed % SEG_DEV
    position = jnp.arange(per_device)
    earlier = (owners[:, None] == owners[None, :]) & (position[:, None] > position[None, :])
    ranked = jnp.sum(earlier.astype(jnp.int32), axis=1)
    slots = owners * capacity + ranked
    picked = (slots[:, None] == jnp.arange(devices * capacity)[None, :]).astype(jnp.int32)
    request = jnp.sum(picked * (within + 1)[:, None], axis=0).reshape(devices, capacity)
    asked = lax.all_to_all(request, "span", split_axis=0, concat_axis=0, tiled=True)
    wanted = jnp.maximum(asked - 1, 0).reshape(devices * capacity)
    own_keys = pick(segment_key.reshape(SEG_DEV, SEG_LEN, columns), wanted)
    own_values = pick(segment_value.reshape(SEG_DEV, SEG_LEN, columns), wanted)
    got_keys, got_values = (
        lax.all_to_all(
            own_keys.reshape(devices, capacity, SEG_LEN, columns),
            "span",
            split_axis=0,
            concat_axis=0,
            tiled=True,
        ),
        lax.all_to_all(
            own_values.reshape(devices, capacity, SEG_LEN, columns),
            "span",
            split_axis=0,
            concat_axis=0,
            tiled=True,
        ),
    )
    source_keys = pick(got_keys.reshape(devices * capacity, SEG_LEN, columns), slots)
    source_values = pick(got_values.reshape(devices * capacity, SEG_LEN, columns), slots)
    crossed = attend(cross_query, source_keys, source_values).astype(jnp.bfloat16)
    encoded = (self_out.astype(jnp.float32) + crossed.astype(jnp.float32)).astype(jnp.bfloat16)
    encoded = encoded.reshape(per_device * NBR_LEN, columns)
    key_totals = lax.psum(squares(encoded), "head")
    keys_all = normalize(encoded, key_totals, full_width)
    before_keys, before_values = from_behind(
        (keys_all[-panel_rows:], encoded[-panel_rows:]), "span", 1
    )
    used_keys = jnp.concatenate([before_keys, keys_all[:-panel_rows]], axis=0)
    used_values = jnp.concatenate([before_values, encoded[:-panel_rows]], axis=0)
    blended = attend(
        decoder_query.reshape(SEG_DEV, SEG_LEN, columns),
        used_keys.reshape(SEG_DEV, panel_rows, columns),
        used_values.reshape(SEG_DEV, panel_rows, columns),
    ).astype(jnp.bfloat16)
    return blended.reshape(SEG_DEV * SEG_LEN, columns)


MESH = pl.DeviceIdType.MESH
GROUPS = 4


def dot_t(a, b):
    return lax.dot_general(a, b, (((1,), (1,)), ((), ())), preferred_element_type=jnp.float32)


def dot_first(a, b):
    return lax.dot_general(a, b, (((0,), (0,)), ((), ())), preferred_element_type=jnp.float32)


def apart(rows):
    count = rows.shape[1] // HEAD_DIM
    zero = jnp.zeros((rows.shape[0], HEAD_DIM), rows.dtype)
    lines = []
    for h in range(count):
        own = rows[:, h * HEAD_DIM:(h + 1) * HEAD_DIM]
        lines.append(jnp.concatenate([own if k == h else zero for k in range(count)], axis=1))
    return jnp.concatenate(lines, axis=0)


def softmax(scores, axis):
    weights = jnp.exp2(scores - jnp.max(scores, axis=axis, keepdims=True))
    inverse = 1.0 / jnp.sum(weights, axis=axis, keepdims=True)
    return (weights * inverse).astype(jnp.bfloat16)


def gather_kernel(
    heads_axis, full_width,
    src_ref, nq_hbm, nk_hbm, nv_hbm, sk_hbm, sv_hbm, dq_hbm, out_ref,
    nq, nk, nv, dq, *rest,
):
    kbufs, vbufs = rest[:GROUPS], rest[GROUPS:2 * GROUPS]
    (own_out, mixing, asked, enc, squares_acc, row_scale, key_scale,
     stat1, stat2, peer1, peer2, behind2,
     in_sem, dq_sem, local_sem, send_sem, recv_sem,
     stat_send, stat_recv, prior_send, prior_recv) = rest[2 * GROUPS:]
    per_device = nq.shape[0]
    seg_dev = dq.shape[0]
    columns = nq.shape[2]
    width = columns // GROUPS
    group_heads = width // HEAD_DIM
    span = lax.axis_size("span")
    me = lax.axis_index("span")
    lane = lax.axis_index("head")
    core, across, along = me ^ 1, me ^ 2, me ^ 4
    after = lax.rem(me + 1, span)
    before = lax.rem(me + span - 1, span)
    softmax_scale = HEAD_DIM ** (-0.5) / math.log(2.0)

    barrier = pltpu.get_barrier_semaphore()
    greeted = 0
    for target in (core, across, along):
        pl.semaphore_signal(barrier, inc=1, device_id={"span": target, "head": lane}, device_id_type=MESH)
        greeted += 1
    for k in range(1, heads_axis):
        other = lax.rem(lane + k, heads_axis)
        pl.semaphore_signal(barrier, inc=1, device_id={"span": me, "head": other}, device_id_type=MESH)
        greeted += 1
    for k in range(heads_axis):
        other = lax.rem(lane + k, heads_axis)
        for target in (after, before):
            pl.semaphore_signal(barrier, inc=1, device_id={"span": target, "head": other}, device_id_type=MESH)
            greeted += 1
    pl.semaphore_wait(barrier, greeted)

    chunks = 2 * GROUPS

    def buffer(j):
        return (kbufs + vbufs)[j]

    def source(j):
        hbm = (sk_hbm, sv_hbm)[j // GROUPS]
        return hbm.at[:, :, pl.ds((j % GROUPS) * width, width)]

    def block(j, owner):
        return buffer(j).at[pl.ds(owner * seg_dev, seg_dev)]

    def half(j, owner, part):
        rows = seg_dev // 2
        return buffer(j).at[pl.ds(owner * seg_dev + part * rows, rows)]

    sent = {}

    def push(kind, j, src, dst, target):
        copy = pltpu.make_async_remote_copy(
            src_ref=src, dst_ref=dst, send_sem=send_sem.at[kind, j], recv_sem=recv_sem.at[kind, j],
            device_id={"span": target, "head": lane}, device_id_type=MESH)
        copy.start()
        sent[kind, j] = copy

    def direct(j):
        push(0, j, source(j), block(j, me), across)
        push(1, j, source(j), block(j, me), along)

    local = []
    for j in range(chunks):
        direct(j)

    for i in range(per_device):
        for a, (hbm, vm) in enumerate(((nq_hbm, nq), (nk_hbm, nk), (nv_hbm, nv))):
            pltpu.make_async_copy(hbm.at[i], vm.at[i], in_sem.at[a, i]).start()
    dq_copy = pltpu.make_async_copy(dq_hbm, dq, dq_sem)
    dq_copy.start()

    for j in range(chunks):
        push(4, j, source(j), block(j, me), core)
        copy = pltpu.make_async_copy(source(j), block(j, me), local_sem.at[j])
        copy.start()
        local.append(copy)

    def forward(j):
        for part in range(2):
            sent[2 + part, j].wait_recv()
            push(7 + part, j, half(j, me ^ 6, part), half(j, me ^ 6, part), core)

    def step(j):
        sent[1, j].wait_recv()
        push(2, j, half(j, along, 0), half(j, along, 0), across)
        sent[0, j].wait_recv()
        push(3, j, half(j, across, 1), half(j, across, 1), along)
        push(5, j, block(j, across), block(j, across), core)
        push(6, j, block(j, along), block(j, along), core)

    def arrived(j):
        local[j].wait()
        for kind in (4, 5, 6, 7, 8):
            sent[kind, j].wait_recv()

    def self_step(i, carry):
        for a, (hbm, vm) in enumerate(((nq_hbm, nq), (nk_hbm, nk), (nv_hbm, nv))):
            pltpu.make_async_copy(hbm.at[i], vm.at[i], in_sem.at[a, i]).wait()
        total = jnp.zeros((NBR_LEN, HEAD_DIM), jnp.float32)
        for base in range(0, columns // HEAD_DIM, 8):
            together = range(base, base + 8)
            cols = [pl.ds(h * HEAD_DIM, HEAD_DIM) for h in together]
            scores = [dot_t(nk[i, :, c], nq[i, :, c]) * softmax_scale for c in cols]
            weights = [softmax(x, 0) for x in scores]
            outs = [dot_first(w, nv[i, :, c]).astype(jnp.bfloat16) for w, c in zip(weights, cols)]
            for h, o in zip(together, outs):
                own_out[h // group_heads, i, :, pl.ds((h % group_heads) * HEAD_DIM, HEAD_DIM)] = o
                wide = o.astype(jnp.float32)
                total = total + wide * wide
        stat1[pl.ds(i, 1), :] = jnp.sum(total.T, axis=0, keepdims=True)
        return carry

    def exchange(kind, stat, peer):
        out = []
        for k in range(1, heads_axis):
            other = lax.rem(lane + k, heads_axis)
            copy = pltpu.make_async_remote_copy(
                src_ref=stat, dst_ref=peer.at[k - 1],
                send_sem=stat_send.at[kind, k - 1], recv_sem=stat_recv.at[kind, k - 1],
                device_id={"span": me, "head": other}, device_id_type=MESH)
            copy.start()
            out.append(copy)
        return out

    def weigh(g):
        arrived(g)

        def some(t, carry):
            rows = [4 * t + b for b in range(4)]
            keys = [apart(kbufs[g][src_ref[i % NEIGHBOURS, i // NEIGHBOURS]]) for i in rows]
            scores = [dot_t(k, own_out[g, i]) * row_scale[pl.ds(i, 1), :] for k, i in zip(keys, rows)]
            weights = [softmax(x.reshape(group_heads, SEG_LEN, NBR_LEN), 1) for x in scores]
            for i, w in zip(rows, weights):
                mixing[g, i] = w.reshape(group_heads * SEG_LEN, NBR_LEN)
            return carry

        lax.fori_loop(0, per_device // 4, some, 0)

    def cross_rows(g, rows):
        values = [apart(vbufs[g][src_ref[i % NEIGHBOURS, i // NEIGHBOURS]]) for i in rows]
        crossed = [dot_first(mixing[g, i], v).astype(jnp.bfloat16) for i, v in zip(rows, values)]
        for i, x in zip(rows, crossed):
            both = (own_out[g, i].astype(jnp.float32) + x.astype(jnp.float32)).astype(jnp.bfloat16)
            enc[g, NEIGHBOURS + i] = both
            wide = both.astype(jnp.float32)
            wide = wide * wide
            total = wide[:, :HEAD_DIM]
            for h in range(1, group_heads):
                total = total + wide[:, h * HEAD_DIM:(h + 1) * HEAD_DIM]
            if g > 0:
                total = total + squares_acc[i]
            if g < GROUPS - 1:
                squares_acc[i] = total
            else:
                stat2[pl.ds(i, 1), :] = jnp.sum(total.T, axis=0, keepdims=True)

    prior = []

    def panel(g, u):
        return enc[g, pl.ds(NEIGHBOURS * u, NEIGHBOURS)].reshape(NEIGHBOURS * NBR_LEN, width)

    def ask(g, u):
        asked[u, g] = dot_t(panel(g, u), apart(dq[u, :, pl.ds(g * width, width)]))

    def cross(g):
        arrived(GROUPS + g)
        cross_rows(g, list(range(per_device - NEIGHBOURS, per_device)))
        copy = pltpu.make_async_remote_copy(
            src_ref=enc.at[g, pl.ds(per_device, NEIGHBOURS)], dst_ref=enc.at[g, pl.ds(0, NEIGHBOURS)],
            send_sem=prior_send.at[g], recv_sem=prior_recv.at[g],
            device_id={"span": after, "head": lane}, device_id_type=MESH)
        copy.start()
        prior.append(copy)

        def rest_step(t, carry):
            cross_rows(g, [3 * t + b for b in range(3)])
            return carry

        lax.fori_loop(0, (per_device - NEIGHBOURS) // 3, rest_step, 0)

    quarter = per_device // 4
    for j in range(4):
        lax.fori_loop(j * quarter, (j + 1) * quarter, self_step, 0)
        if j > 0:
            step(2 * j - 2)
            step(2 * j - 1)
    first_stats = exchange(0, stat1, peer1)
    step(6)
    for copy in first_stats:
        copy.wait_recv()
    total1 = stat1[...]
    for k in range(heads_axis - 1):
        total1 = total1 + peer1[k]
    row_scale[...] = lax.rsqrt(total1 / full_width + epsilon) * softmax_scale
    step(7)
    forward(0)
    for g in range(GROUPS):
        forward(g + 1)
        weigh(g)
    dq_copy.wait()
    for g in range(GROUPS):
        if g + 1 < GROUPS:
            forward(GROUPS + 1 + g)
        cross(g)
        if g + 1 < GROUPS:
            for u in range(1, seg_dev):
                ask(g, u)

    second_stats = exchange(1, stat2, peer2)
    behind_stats = []
    for k in range(heads_axis):
        other = lax.rem(lane + k, heads_axis)
        copy = pltpu.make_async_remote_copy(
            src_ref=stat2, dst_ref=behind2.at[k],
            send_sem=stat_send.at[2, k], recv_sem=stat_recv.at[2, k],
            device_id={"span": after, "head": other}, device_id_type=MESH)
        copy.start()
        behind_stats.append(copy)
    for u in range(1, seg_dev):
        ask(GROUPS - 1, u)
    for copy in second_stats:
        copy.wait_recv()
    total2 = stat2[...]
    for k in range(heads_axis - 1):
        total2 = total2 + peer2[k]
    key_scale[pl.ds(NEIGHBOURS, per_device), :] = lax.rsqrt(total2 / full_width + epsilon) * softmax_scale

    def decode_step(u, carry):
        scale = jnp.concatenate([
            jnp.broadcast_to(key_scale[pl.ds(NEIGHBOURS * u + n, 1), :], (NBR_LEN, NBR_LEN)).T
            for n in range(NEIGHBOURS)], axis=0)
        weights = [softmax(asked[u, g] * scale, 0) for g in range(GROUPS)]
        outs = [dot_first(w, panel(g, u)).astype(jnp.bfloat16) for g, w in enumerate(weights)]
        for g, out in enumerate(outs):
            for h in range(group_heads):
                lo = h * HEAD_DIM
                out_ref[u, :, pl.ds(g * width + lo, HEAD_DIM)] = out[h * SEG_LEN:(h + 1) * SEG_LEN, lo:lo + HEAD_DIM]
        return carry

    lax.fori_loop(1, seg_dev, decode_step, 0)
    for copy in behind_stats:
        copy.wait_recv()
    for copy in prior:
        copy.wait_recv()
    total3 = behind2[0]
    for k in range(1, heads_axis):
        total3 = total3 + behind2[k]
    total3 = lax.rsqrt(total3 / full_width + epsilon) * softmax_scale
    key_scale[pl.ds(0, NEIGHBOURS), :] = total3[per_device - NEIGHBOURS:]

    @pl.when(me == 0)
    def _():
        enc[:, pl.ds(0, NEIGHBOURS)] = jnp.zeros((GROUPS, NEIGHBOURS, NBR_LEN, width), jnp.bfloat16)

    for g in range(GROUPS):
        ask(g, 0)
    decode_step(0, 0)
    for copy in list(sent.values()) + prior + first_stats + second_stats + behind_stats:
        copy.wait_send()


def gather_all(operands):
    columns = operands[1].shape[2]
    heads_axis = lax.axis_size("head")
    span = lax.axis_size("span")
    per_device = SEG_DEV * NEIGHBOURS
    width = columns // GROUPS
    bf16, f32 = jnp.bfloat16, jnp.float32
    neighbour_shape = (per_device, NBR_LEN, columns)
    segment_shape = (SEG_DEV, SEG_LEN, columns)
    chunks = 2 * GROUPS
    any_space = pl.BlockSpec(memory_space=pltpu.HBM)
    dma = pltpu.SemaphoreType.DMA
    return pl.pallas_call(
        functools.partial(gather_kernel, heads_axis, columns * heads_axis),
        out_shape=jax.ShapeDtypeStruct(segment_shape, bf16),
        in_specs=[pl.BlockSpec(memory_space=pltpu.SMEM)] + [any_space] * 6,
        out_specs=pl.BlockSpec(memory_space=pltpu.VMEM),
        scratch_shapes=[pltpu.VMEM(neighbour_shape, bf16)] * 3
        + [pltpu.VMEM(segment_shape, bf16)]
        + [pltpu.VMEM((span * SEG_DEV, SEG_LEN, width), bf16)] * chunks
        + [
            pltpu.VMEM((GROUPS, per_device, NBR_LEN, width), bf16),
            pltpu.VMEM((GROUPS, per_device, width // HEAD_DIM * SEG_LEN, NBR_LEN), bf16),
            pltpu.VMEM((SEG_DEV, GROUPS, NEIGHBOURS * NBR_LEN, width // HEAD_DIM * SEG_LEN), f32),
            pltpu.VMEM((GROUPS, per_device + NEIGHBOURS, NBR_LEN, width), bf16),
            pltpu.VMEM((per_device, NBR_LEN, HEAD_DIM), f32),
            pltpu.VMEM((per_device, NBR_LEN), f32),
            pltpu.VMEM((per_device + NEIGHBOURS, NBR_LEN), f32),
            pltpu.VMEM((per_device, NBR_LEN), f32),
            pltpu.VMEM((per_device, NBR_LEN), f32),
            pltpu.VMEM((heads_axis - 1, per_device, NBR_LEN), f32),
            pltpu.VMEM((heads_axis - 1, per_device, NBR_LEN), f32),
            pltpu.VMEM((heads_axis, per_device, NBR_LEN), f32),
            dma((3, per_device)),
            dma,
            dma((chunks,)),
            dma((9, chunks)),
            dma((9, chunks)),
            dma((3, heads_axis)),
            dma((3, heads_axis)),
            dma((GROUPS,)),
            dma((GROUPS,)),
        ],
        compiler_params=pltpu.CompilerParams(
            collective_id=1, has_side_effects=True, vmem_limit_bytes=53 * 1024 * 1024),
    )(*operands)


PHASES = (2, 3, 3)
SLOTS = sum(PHASES)
STARTS = tuple(sum(PHASES[:p]) for p in range(len(PHASES)))
FORWARDS = (0, 0, 1, 2, 2, 3, 4, 5)
CHIP_SEGS = 8
LANES = 128


def selections():
    upper = lax.broadcasted_iota(jnp.int32, (LANES, LANES), 0)
    lower = lax.broadcasted_iota(jnp.int32, (LANES, LANES), 1)
    row_chip, column_chip = upper // CHIP_SEGS, lower // CHIP_SEGS
    same = jnp.where(row_chip == column_chip, 1.0, 0.0)
    ahead = jnp.where(upper < lower, same, 0.0)
    others = [jnp.where((row_chip ^ k) == column_chip, 1.0, 0.0) for k in range(1, 4)]
    return jnp.concatenate(others + [same, ahead], axis=1).astype(jnp.bfloat16)


def routes(needs, select, mine):
    f32, bf16 = jnp.float32, jnp.bfloat16
    lane = lax.broadcasted_iota(jnp.int32, (1, LANES), 1)
    chip = lane // CHIP_SEGS
    within = (lane % CHIP_SEGS).astype(f32)

    def at(k):
        total = jnp.zeros((1, LANES), f32)
        for t, row in enumerate(needs):
            total = total + jnp.where((chip ^ k) == t, row, 0.0)
        return total

    n1, n2, n3 = at(1), at(2), at(3)
    only1, only2 = n3 * n1 * (1 - n2), n3 * n2 * (1 - n1)
    both, none = n3 * n1 * n2, n3 * (1 - n1) * (1 - n2)
    zero = jnp.zeros((1, LANES), f32)
    stacked = jnp.concatenate([n1, n2, only1, only2, both, none, zero, zero], axis=0)
    counts = jnp.dot(stacked.astype(bf16), select, preferred_element_type=f32)

    def count(r):
        return [counts[r:r + 1, k * LANES:(k + 1) * LANES] for k in (3, 0, 1, 2)]

    def rank(r):
        return counts[r:r + 1, 4 * LANES:]

    n1c, n2c, o1, o2, b, n = [count(r) for r in range(6)]
    every = range(4)

    def clip(value, top):
        return jnp.minimum(jnp.maximum(value, 0.0), top)

    x = [n1c[k] + o2[k ^ 2] for k in every]
    y = [n2c[k] + o1[k ^ 1] for k in every]
    pb = [clip(jnp.floor((b[k] + x[k ^ 2] - y[k ^ 1] + 1) * 0.5), b[k]) for k in every]
    x = [x[k] + b[k ^ 2] - pb[k ^ 2] for k in every]
    y = [y[k] + pb[k ^ 1] for k in every]
    pn = [clip(jnp.floor((n[k] + jnp.maximum(y[k], x[k ^ 2]) - jnp.maximum(x[k], y[k ^ 1]) + 1) * 0.5), n[k])
          for k in every]
    x, y = ([x[k] + pn[k] + n[k ^ 2] - pn[k ^ 2] for k in every],
            [y[k] + n[k] - pn[k] + pn[k ^ 1] for k in every])
    over1 = [jnp.maximum(x[k], y[k ^ 1]) - SLOTS for k in every]
    over2 = [jnp.maximum(y[k], x[k ^ 2]) - SLOTS for k in every]
    shift = [clip(jnp.minimum(over2[k], -over1[k]), n[k] - pn[k]) - clip(jnp.minimum(over1[k], -over2[k]), pn[k])
             for k in every]
    pn = [pn[k] + shift[k] for k in every]
    x, y = ([x[k] + shift[k] - shift[k ^ 2] for k in every],
            [y[k] - shift[k] + shift[k ^ 1] for k in every])
    m1 = [clip(jnp.minimum(y[k ^ 1] - SLOTS, SLOTS - jnp.maximum(y[k], x[k ^ 2])), o1[k]) for k in every]
    m2 = [clip(jnp.minimum(x[k ^ 2] - SLOTS, SLOTS - jnp.maximum(x[k], y[k ^ 1])), o2[k]) for k in every]

    def below(r, limit, rows):
        return jnp.where(rank(r) < limit, rows, 0.0)

    path1 = only1 - below(2, m1[0], only1) + below(3, m2[0], only2) + below(4, pb[0], both) + below(5, pn[0], none)
    path2 = n3 - path1
    own_x, own_y = jnp.maximum(n1, path1), jnp.maximum(n2, path2)
    stacked = jnp.concatenate(
        [path1, path2, own_x - path1, own_y - path2, zero, zero, zero, zero], axis=0)
    again = jnp.dot(stacked.astype(bf16), select[:, 3 * LANES:], preferred_element_type=f32)
    relays, ranks = again[:, :LANES], again[:, LANES:]
    slot_x = jnp.where(path1 > 0, ranks[0:1], relays[0:1] + ranks[2:3])
    slot_y = jnp.where(path2 > 0, ranks[1:2], relays[1:2] + ranks[3:4])

    def forwarded(own, place):
        return jnp.maximum(own, jnp.where(place < 2, 2.0, 3.0)) + place

    forward_y = forwarded(n2c[1] + n[1] - pn[1] + m1[1], ranks[0:1])
    forward_x = forwarded(n1c[2] + pn[2] + m2[2], ranks[1:2])
    last = jnp.maximum(path1 * forward_y, path2 * forward_x)
    over = jnp.max(jnp.where(last >= SLOTS, 1.0, 0.0), axis=1, keepdims=True)

    side = chip ^ mine
    place = jnp.where(
        side == 0, within,
        CHIP_SEGS + jnp.where(
            side == 1, slot_x,
            jnp.where(side == 2, SLOTS + slot_y, jnp.where(path1 > 0, SLOTS + forward_y, forward_x))))
    place = jnp.minimum(place, CHIP_SEGS + 2 * SLOTS - 1.0)

    def sends(own, slot, relay, forward, arrives):
        mine_own = (side == 0) & (own > 0)
        number = jnp.where(mine_own, slot, jnp.where(relay, forward, -1.0))
        code = jnp.where(mine_own, within, CHIP_SEGS + arrives)
        wanted = lax.broadcasted_iota(jnp.int32, (SLOTS, LANES), 0).astype(f32)
        return jnp.sum(jnp.where(number == wanted, code, 0.0), axis=1, keepdims=True)

    send_x = sends(own_x, slot_x, (side == 2) & (path2 > 0), forward_x, slot_y)
    send_y = sends(own_y, slot_y, (side == 1) & (path1 > 0), forward_y, slot_x)
    rows = [send_x, send_y, place, over]
    return jnp.concatenate([jnp.broadcast_to(r, (8, LANES)) for r in rows], axis=0).astype(jnp.int32)


ORDER = ((0, 0), (1, 0), (2, 0), (0, 1), (1, 1), (3, 0), (0, 2), (1, 2), (2, 1), (3, 1), (2, 2), (3, 2))


def kernel(
    heads_axis, full_width,
    src_ref, nq_hbm, nk_hbm, nv_hbm, sk_hbm, sv_hbm, dq_hbm, out_ref, over_ref,
    nq, nk, nv, dq, *rest,
):
    own_a, own_b, recv_a, recv_b, send_a = (rest[4 * j:4 * j + 4] for j in range(5))
    (first, answer, first_sem, ask_send, ask_recv, answer_send, answer_recv, select, need, needs, table, lookup, own_out, mixing, asked, enc, squares_acc, row_scale, key_scale,
     stat1, stat2, peer1, peer2, peer3,
     in_sem, dq_sem, local_sem, table_sem, need_send, need_recv, core_send, core_recv,
     link_send, link_recv, pass_send, pass_recv,
     stat_send, stat_recv) = rest[20:]
    per_device = nq.shape[0]
    seg_dev = dq.shape[1]
    columns = nq.shape[2]
    width = columns // GROUPS
    group_heads = width // HEAD_DIM
    span = lax.axis_size("span")
    me = lax.axis_index("span")
    lane = lax.axis_index("head")
    side = lax.rem(me, 2)
    core, across, along = me ^ 1, me ^ 2, me ^ 4
    after = lax.rem(me + 1, span)
    before = lax.rem(me + span - 1, span)
    softmax_scale = HEAD_DIM ** (-0.5) / math.log(2.0)

    def at(target, head):
        return {"span": target, "head": head}

    def columns_of(half, q):
        return pl.ds(pl.multiple_of((2 * half + q) * width, width), width)

    def source(k, half):
        hbm = (sk_hbm, sv_hbm)[k % 2]
        return hbm.at[:, :, columns_of(half, k // 2)]

    mine_rows = pl.ds(pl.multiple_of(side * seg_dev, seg_dev), seg_dev)

    def inputs(i):
        return [pltpu.make_async_copy(hbm.at[i], vm.at[i], in_sem.at[a, i])
                for a, (hbm, vm) in enumerate(((nq_hbm, nq), (nk_hbm, nk), (nv_hbm, nv)))]

    for i in range(2):
        for copy in inputs(i):
            copy.start()
    local = {}
    for k in range(4):
        for b, (own, half) in enumerate(((own_a[k], side), (own_b[k], 1 - side))):
            copy = pltpu.make_async_copy(source(k, half), own.at[mine_rows], local_sem.at[b, k])
            copy.start()
            local[b, k] = copy
    for i in range(2, per_device):
        for copy in inputs(i):
            copy.start()
    dq_copies = []
    for g in range(GROUPS):
        copy = pltpu.make_async_copy(
            dq_hbm.at[pl.ds(1, seg_dev - 1), :, pl.ds(g * width, width)], dq.at[g, pl.ds(0, seg_dev - 1)],
            dq_sem.at[g])
        copy.start()
        dq_copies.append(copy)
    stat2[1] = jnp.zeros_like(stat2[1])

    @pl.when(me == 0)
    def _():
        pltpu.make_async_copy(dq_hbm.at[0], first, first_sem).start()

    @pl.when(me == span - 1)
    def _():
        for g in range(GROUPS):
            dq[g, seg_dev - 1] = jnp.zeros((SEG_LEN, width), jnp.bfloat16)

    segment = lax.broadcasted_iota(jnp.int32, (8, LANES), 1)
    wanted = jnp.zeros((8, LANES), jnp.float32)
    for i in range(per_device):
        wanted = jnp.where(segment == src_ref[i % NEIGHBOURS, i // NEIGHBOURS], 1.0, wanted)
    need[...] = wanted
    select[...] = selections()

    barrier = pltpu.get_barrier_semaphore()
    greeted = 0
    for k in range(1, span):
        pl.semaphore_signal(barrier, inc=1, device_id=at(me ^ k, lane), device_id_type=MESH)
        greeted += 1
    for k in range(1, heads_axis):
        other = lax.rem(lane + k, heads_axis)
        pl.semaphore_signal(barrier, inc=1, device_id=at(me, other), device_id_type=MESH)
        greeted += 1
    pl.semaphore_wait(barrier, greeted)

    def remote(src, dst, send_sem, recv_sem, target):
        copy = pltpu.make_async_remote_copy(
            src_ref=src, dst_ref=dst, send_sem=send_sem, recv_sem=recv_sem,
            device_id=at(*target), device_id_type=MESH)
        copy.start()
        return copy

    told = [remote(need, needs.at[me], need_send.at[k - 1], need_recv.at[k - 1], (me ^ k, lane))
            for k in range(1, span)]
    needs[me] = wanted

    def query_copy(g):
        return pltpu.make_async_remote_copy(
            src_ref=dq_hbm.at[0, :, pl.ds(g * width, width)], dst_ref=dq.at[g, seg_dev - 1],
            send_sem=ask_send.at[g], recv_sem=ask_recv.at[g], device_id=at(before, lane), device_id_type=MESH)

    def answer_copy(g):
        block = pl.ds(g * width, width)
        return pltpu.make_async_remote_copy(
            src_ref=answer.at[:, block], dst_ref=out_ref.at[0, :, block],
            send_sem=answer_send.at[g], recv_sem=answer_recv.at[g], device_id=at(after, lane), device_id_type=MESH)

    @pl.when(me > 0)
    def _():
        for g in range(GROUPS):
            query_copy(g).start()

    given = {}
    for k in range(4):
        given[0, k] = remote(source(k, 1 - side), own_a[k].at[mine_rows], core_send.at[0, k], core_recv.at[0, k],
                             (core, lane))
        given[1, k] = remote(source(k, side), own_b[k].at[mine_rows], core_send.at[1, k], core_recv.at[1, k],
                             (core, lane))

    def owned(b, k):
        local[b, k].wait()
        given[b, k].wait_recv()

    sent, passed = {}, {}

    def slots(link, p):
        return pl.ds(link * SLOTS + STARTS[p], PHASES[p])

    def hand_on(k, p):
        for link in range(2):
            sent[k, p, link].wait_recv()
            block = slots(link, p)
            passed[k, p, link] = remote(recv_a[k].at[block], recv_b[k].at[block], pass_send.at[link, 3 * k + p],
                                        pass_recv.at[link, 3 * k + p], (core, lane))

    def advance(k, p):
        if p == 0:
            owned(0, k)
        else:
            hand_on(k, p - 1)
        for link, target in enumerate((across, along)):
            for i in range(STARTS[p], STARTS[p] + PHASES[p]):
                code = lookup[8 * link + i, 0]
                rows = own_a[k][jnp.clip(code, 0, CHIP_SEGS - 1)]
                for t in range(FORWARDS[i]):
                    rows = jnp.where(code == CHIP_SEGS + t, recv_a[k][(1 - link) * SLOTS + t], rows)
                send_a[k][link * SLOTS + i] = rows
            block = slots(link, p)
            sent[k, p, link] = remote(send_a[k].at[block], recv_a[k].at[block], link_send.at[link, 3 * k + p],
                                      link_recv.at[link, 3 * k + p], (target, lane))

    def finish(k):
        hand_on(k, len(PHASES) - 1)

    def arrived(b, k):
        if b == 1:
            owned(1, k)
            for p in range(len(PHASES)):
                for link in range(2):
                    passed[k, p, link].wait_recv()

    def rows_of(b, k, i):
        place = lookup[16, src_ref[i % NEIGHBOURS, i // NEIGHBOURS]]
        own, recv = ((own_a[k], recv_a[k]), (own_b[k], recv_b[k]))[b]
        return jnp.where(place < CHIP_SEGS, own[jnp.clip(place, 0, CHIP_SEGS - 1)],
                         recv[jnp.clip(place - CHIP_SEGS, 0, 2 * SLOTS - 1)])

    def self_step(i, carry):
        for copy in inputs(i):
            copy.wait()
        total = jnp.zeros((NBR_LEN, HEAD_DIM), jnp.float32)
        for base in range(0, columns // HEAD_DIM, 8):
            together = range(base, base + 8)
            cols = [pl.ds(h * HEAD_DIM, HEAD_DIM) for h in together]
            scores = [dot_t(nk[i, :, c], nq[i, :, c]) * softmax_scale for c in cols]
            weights = [softmax(x, 0) for x in scores]
            outs = [dot_first(w, nv[i, :, c]).astype(jnp.bfloat16) for w, c in zip(weights, cols)]
            for h, o in zip(together, outs):
                own_out[h // group_heads, i, :, pl.ds((h % group_heads) * HEAD_DIM, HEAD_DIM)] = o
                wide = o.astype(jnp.float32)
                total = total + wide * wide
        stat1[pl.ds(i, 1), :] = jnp.sum(total.T, axis=0, keepdims=True)
        return carry

    def exchange(kind, stat, peer):
        return [remote(stat, peer.at[k - 1], stat_send.at[kind, k - 1], stat_recv.at[kind, k - 1],
                       (me, lax.rem(lane + k, heads_axis))) for k in range(1, heads_axis)]

    def group(b, q):
        return 2 * (side if b == 0 else 1 - side) + q

    def weigh(b, q):
        arrived(b, 2 * q)
        g = group(b, q)

        def some(t, carry):
            rows = [4 * t + s for s in range(4)]
            keys = [apart(rows_of(b, 2 * q, i)) for i in rows]
            scores = [dot_t(k, own_out[g, i]) * row_scale[pl.ds(i, 1), :] for k, i in zip(keys, rows)]
            weights = [softmax(x.reshape(group_heads, SEG_LEN, NBR_LEN), 1) for x in scores]
            for i, w in zip(rows, weights):
                mixing[g, i] = w.reshape(group_heads * SEG_LEN, NBR_LEN)
            return carry

        lax.fori_loop(0, per_device // 4, some, 0)

    def cross_rows(b, q, rows):
        g = group(b, q)
        values = [apart(rows_of(b, 2 * q + 1, i)) for i in rows]
        crossed = [dot_first(mixing[g, i], v).astype(jnp.bfloat16) for i, v in zip(rows, values)]
        for i, x in zip(rows, crossed):
            both = (own_out[g, i].astype(jnp.float32) + x.astype(jnp.float32)).astype(jnp.bfloat16)
            enc[g, i] = both
            wide = both.astype(jnp.float32)
            wide = wide * wide
            total = wide[:, :HEAD_DIM]
            for h in range(1, group_heads):
                total = total + wide[:, h * HEAD_DIM:(h + 1) * HEAD_DIM]
            if (q, b) != (0, 0):
                total = total + squares_acc[i]
            if (q, b) != (1, 1):
                squares_acc[i] = total
            else:
                line = jnp.sum(total.T, axis=0, keepdims=True)
                stat2[0, pl.ds(i, 1), :] = line
                if len(rows) == NEIGHBOURS:
                    stat2[1, pl.ds(i, 1), :] = line

    def panel(g, u):
        return enc[g, pl.ds(NEIGHBOURS * u, NEIGHBOURS)].reshape(NEIGHBOURS * NBR_LEN, width)

    def ask(g, u):
        asked[u, g] = dot_t(panel(g, u), apart(dq[g, u]))

    def cross_last(b, q):
        arrived(b, 2 * q + 1)
        cross_rows(b, q, list(range(per_device - NEIGHBOURS, per_device)))

    def cross_others(b, q):
        def rest_step(t, carry):
            cross_rows(b, q, [3 * t + s for s in range(3)])
            return carry

        lax.fori_loop(0, (per_device - NEIGHBOURS) // 3, rest_step, 0)

    lax.fori_loop(0, 1, self_step, 0)
    for copy in told:
        copy.wait_recv()
    table[...] = routes([jnp.maximum(needs[2 * t][:1], needs[2 * t + 1][:1]) for t in range(span // 2)],
                        select[...], me // 2)
    copy = pltpu.make_async_copy(table, lookup, table_sem)
    copy.start()
    copy.wait()
    for k, p in ORDER[:3]:
        advance(k, p)
    lax.fori_loop(1, 3, self_step, 0)
    advance(*ORDER[3])
    lax.fori_loop(3, 5, self_step, 0)
    advance(*ORDER[4])
    advance(*ORDER[5])
    lax.fori_loop(5, per_device, self_step, 0)
    first_stats = exchange(0, stat1, peer1)
    for k, p in ORDER[6:8]:
        advance(k, p)
    for copy in first_stats:
        copy.wait_recv()
    total1 = stat1[...]
    for k in range(heads_axis - 1):
        total1 = total1 + peer1[k]
    row_scale[...] = lax.rsqrt(total1 / full_width + epsilon) * softmax_scale
    for k, p in ORDER[8:10]:
        advance(k, p)
    for copy in dq_copies:
        copy.wait()

    @pl.when(me < span - 1)
    def _():
        for g in range(GROUPS):
            query_copy(g).wait_recv()

    @pl.when(me == 0)
    def _():
        pltpu.make_async_copy(dq_hbm.at[0], first, first_sem).wait()
        for g in range(GROUPS):
            nothing = jnp.zeros((NEIGHBOURS * NBR_LEN, width), jnp.bfloat16)
            scores = dot_t(nothing, apart(first[:, g * width:(g + 1) * width])) * (epsilon ** -0.5 * softmax_scale)
            out = dot_first(softmax(scores, 0), nothing).astype(jnp.bfloat16)
            for h in range(group_heads):
                lo = h * HEAD_DIM
                out_ref[0, :, pl.ds(g * width + lo, HEAD_DIM)] = out[h * SEG_LEN:(h + 1) * SEG_LEN, lo:lo + HEAD_DIM]

    finish(0)
    weigh(0, 0)
    weigh(1, 0)
    finish(1)
    advance(*ORDER[10])
    cross_last(0, 0)
    cross_others(0, 0)
    advance(*ORDER[11])
    cross_last(1, 0)
    cross_others(1, 0)
    for b in range(2):
        for u in range(seg_dev):
            ask(group(b, 0), u)
    finish(2)
    weigh(0, 1)
    weigh(1, 1)
    finish(3)
    for b in range(2):
        cross_last(b, 1)
    last_stats = exchange(2, stat2.at[1], peer3)
    for b in range(2):
        cross_others(b, 1)
    second_stats = exchange(1, stat2.at[0], peer2)
    for b in range(2):
        for u in reversed(range(seg_dev)):
            ask(group(b, 1), u)

    def settle(mine, copies, peer, rows):
        for copy in copies:
            copy.wait_recv()
        total = mine
        for k in range(heads_axis - 1):
            total = total + peer[k]
        scale = lax.rsqrt(total / full_width + epsilon) * softmax_scale
        key_scale[rows] = scale[rows]

    def decoded(u):
        scale = jnp.concatenate([
            jnp.broadcast_to(key_scale[pl.ds(NEIGHBOURS * u + n, 1), :], (NBR_LEN, NBR_LEN)).T
            for n in range(NEIGHBOURS)], axis=0)
        weights = [softmax(asked[u, g] * scale, 0) for g in range(GROUPS)]
        outs = [dot_first(w, panel(g, u)).astype(jnp.bfloat16) for g, w in enumerate(weights)]
        for g, out in enumerate(outs):
            for h in range(group_heads):
                lo = h * HEAD_DIM
                yield g * width + lo, out[h * SEG_LEN:(h + 1) * SEG_LEN, lo:lo + HEAD_DIM]

    def decode_step(u, carry):
        for lo, out in decoded(u):
            out_ref[u + 1, :, pl.ds(lo, HEAD_DIM)] = out
        return carry

    settle(stat2[1], last_stats, peer3, slice(per_device - NEIGHBOURS, per_device))
    for lo, out in decoded(seg_dev - 1):
        answer[:, pl.ds(lo, HEAD_DIM)] = out

    @pl.when(me < span - 1)
    def _():
        for g in range(GROUPS):
            answer_copy(g).start()

    settle(stat2[0], second_stats, peer2, slice(0, per_device - NEIGHBOURS))
    lax.fori_loop(0, seg_dev - 1, decode_step, 0)
    over_ref[0, 0] = lookup[24, 0]

    @pl.when(me > 0)
    def _():
        for g in range(GROUPS):
            answer_copy(g).wait_recv()
            query_copy(g).wait_send()

    @pl.when(me < span - 1)
    def _():
        for g in range(GROUPS):
            answer_copy(g).wait_send()

    for copy in (told + list(given.values()) + list(sent.values()) + list(passed.values())
                 + first_stats + last_stats + second_stats):
        copy.wait_send()


def fused_body(
    neighbour_query,
    neighbour_key,
    neighbour_value,
    segment_key,
    segment_value,
    decoder_query,
    sources,
):
    columns = neighbour_query.shape[1]
    heads_axis = lax.axis_size("head")
    span = lax.axis_size("span")
    per_device = SEG_DEV * NEIGHBOURS
    width = columns // GROUPS
    bf16, f32 = jnp.bfloat16, jnp.float32
    neighbour_shape = (per_device, NBR_LEN, columns)
    segment_shape = (SEG_DEV, SEG_LEN, columns)
    any_space = pl.BlockSpec(memory_space=pltpu.HBM)
    dma = pltpu.SemaphoreType.DMA
    own = pltpu.VMEM((CHIP_SEGS, SEG_LEN, width), bf16)
    slots = pltpu.VMEM((2 * SLOTS, SEG_LEN, width), bf16)
    steps = 4 * len(PHASES)
    operands = (
        sources.T,
        neighbour_query.reshape(neighbour_shape),
        neighbour_key.reshape(neighbour_shape),
        neighbour_value.reshape(neighbour_shape),
        segment_key.reshape(segment_shape),
        segment_value.reshape(segment_shape),
        decoder_query.reshape(segment_shape),
    )
    out, over = pl.pallas_call(
        functools.partial(kernel, heads_axis, columns * heads_axis),
        out_shape=(jax.ShapeDtypeStruct(segment_shape, bf16), jax.ShapeDtypeStruct((1, 1), jnp.int32)),
        in_specs=[pl.BlockSpec(memory_space=pltpu.SMEM)] + [any_space] * 6,
        out_specs=(pl.BlockSpec(memory_space=pltpu.VMEM), pl.BlockSpec(memory_space=pltpu.SMEM)),
        scratch_shapes=[pltpu.VMEM(neighbour_shape, bf16)] * 3
        + [pltpu.VMEM((GROUPS, SEG_DEV, SEG_LEN, width), bf16)]
        + [own] * 8 + [slots] * 12
        + [
            pltpu.VMEM((SEG_LEN, columns), bf16),
            pltpu.VMEM((SEG_LEN, columns), bf16),
            dma,
            dma((GROUPS,)),
            dma((GROUPS,)),
            dma((GROUPS,)),
            dma((GROUPS,)),
            pltpu.VMEM((LANES, 5 * LANES), bf16),
            pltpu.VMEM((8, LANES), f32),
            pltpu.VMEM((span, 8, LANES), f32),
            pltpu.VMEM((32, LANES), jnp.int32),
            pltpu.SMEM((32, LANES), jnp.int32),
            pltpu.VMEM((GROUPS, per_device, NBR_LEN, width), bf16),
            pltpu.VMEM((GROUPS, per_device, width // HEAD_DIM * SEG_LEN, NBR_LEN), bf16),
            pltpu.VMEM((SEG_DEV, GROUPS, NEIGHBOURS * NBR_LEN, width // HEAD_DIM * SEG_LEN), f32),
            pltpu.VMEM((GROUPS, per_device, NBR_LEN, width), bf16),
            pltpu.VMEM((per_device, NBR_LEN, HEAD_DIM), f32),
            pltpu.VMEM((per_device, NBR_LEN), f32),
            pltpu.VMEM((per_device, NBR_LEN), f32),
            pltpu.VMEM((per_device, NBR_LEN), f32),
            pltpu.VMEM((2, per_device, NBR_LEN), f32),
            pltpu.VMEM((heads_axis - 1, per_device, NBR_LEN), f32),
            pltpu.VMEM((heads_axis - 1, per_device, NBR_LEN), f32),
            pltpu.VMEM((heads_axis - 1, per_device, NBR_LEN), f32),
            dma((3, per_device)),
            dma((GROUPS,)),
            dma((2, 4)),
            dma,
            dma((span - 1,)),
            dma((span - 1,)),
            dma((2, 4)),
            dma((2, 4)),
            dma((2, steps)),
            dma((2, steps)),
            dma((2, steps)),
            dma((2, steps)),
            dma((3, heads_axis)),
            dma((3, heads_axis)),
        ],
        compiler_params=pltpu.CompilerParams(
            collective_id=0, has_side_effects=True, vmem_limit_bytes=53 * 1024 * 1024),
    )(*operands)
    return lax.cond(
        over[0, 0] > 0,
        lambda: gather_all(operands).reshape(SEG_DEV * SEG_LEN, columns),
        lambda: out.reshape(SEG_DEV * SEG_LEN, columns),
    )


def solution(mesh):
    placed = (
        P("span", "head"),
        P("span", "head"),
        P("span", "head"),
        P("span", "head"),
        P("span", "head"),
        P("span", "head"),
        P("span", None),
    )
    cube = mesh.shape["span"] == 2 * 2 * 2
    return jax.shard_map(
        fused_body if cube else body, mesh=mesh, in_specs=placed, out_specs=P("span", "head"), check_vma=False
    )
```

```python
import functools
import math

import jax
import jax.numpy as jnp
from jax import lax
from jax.experimental import pallas as pl
from jax.experimental.pallas import tpu as pltpu
from jax.sharding import PartitionSpec as P

HEAD_DIM = 128
SEG_LEN = 64
NBR_LEN = 128
NEIGHBOURS = 2
SEG_DEV = 4


epsilon = 1e-06


def from_behind(x, axis, by):
    count = lax.axis_size(axis)
    pairs = [(i, i + by) for i in range(count) if 0 <= i + by < count]
    return lax.ppermute(x, axis, pairs)


def attend(query_rows, key_rows, value_rows):
    groups, length, columns = query_rows.shape
    head_count = columns // HEAD_DIM
    query_heads = query_rows.reshape(groups, length, head_count, HEAD_DIM)
    key_heads = key_rows.reshape(groups, key_rows.shape[1], head_count, HEAD_DIM)
    value_heads = value_rows.reshape(groups, value_rows.shape[1], head_count, HEAD_DIM)
    logit_scores = jnp.einsum(
        "bqhd,bkhd->bhqk", query_heads, key_heads, preferred_element_type=jnp.float32
    ) * HEAD_DIM ** (-0.5)
    logit_scores = logit_scores - jnp.max(logit_scores, axis=-1, keepdims=True)
    weights = jnp.exp(logit_scores)
    weights = (weights / jnp.sum(weights, axis=-1, keepdims=True)).astype(jnp.bfloat16)
    output = jnp.einsum("bhqk,bkhd->bqhd", weights, value_heads, preferred_element_type=jnp.float32)
    return output.reshape(groups, length, columns)


def squares(rows):
    wide = rows.astype(jnp.float32)
    return jnp.sum(wide * wide, axis=-1)


def normalize(rows, totals, full_width):
    scale = lax.rsqrt(totals / full_width + epsilon)
    return (rows.astype(jnp.float32) * scale[:, None]).astype(jnp.bfloat16)


def pick(blocks, index):
    chosen = (index[:, None] == jnp.arange(blocks.shape[0])[None, :]).astype(blocks.dtype)
    return jnp.einsum("ws,slc->wlc", chosen, blocks, preferred_element_type=jnp.float32).astype(blocks.dtype)


def body(
    neighbour_query,
    neighbour_key,
    neighbour_value,
    segment_key,
    segment_value,
    decoder_query,
    sources,
):
    columns = neighbour_query.shape[1]
    full_width = columns * lax.axis_size("head")
    devices = lax.axis_size("span")
    per_device = SEG_DEV * NEIGHBOURS
    capacity = max(2, 2 * per_device // devices)
    panel_rows = NEIGHBOURS * NBR_LEN
    self_out = attend(
        neighbour_query.reshape(per_device, NBR_LEN, columns),
        neighbour_key.reshape(per_device, NBR_LEN, columns),
        neighbour_value.reshape(per_device, NBR_LEN, columns),
    ).astype(jnp.bfloat16)
    flat_self = self_out.reshape(per_device * NBR_LEN, columns)
    totals = lax.psum(squares(flat_self), "head")
    cross_query = normalize(flat_self, totals, full_width).reshape(per_device, NBR_LEN, columns)
    listed = sources.reshape(per_device)
    owners = listed // SEG_DEV
    within = listed % SEG_DEV
    position = jnp.arange(per_device)
    earlier = (owners[:, None] == owners[None, :]) & (position[:, None] > position[None, :])
    ranked = jnp.sum(earlier.astype(jnp.int32), axis=1)
    slots = owners * capacity + ranked
    picked = (slots[:, None] == jnp.arange(devices * capacity)[None, :]).astype(jnp.int32)
    request = jnp.sum(picked * (within + 1)[:, None], axis=0).reshape(devices, capacity)
    asked = lax.all_to_all(request, "span", split_axis=0, concat_axis=0, tiled=True)
    wanted = jnp.maximum(asked - 1, 0).reshape(devices * capacity)
    own_keys = pick(segment_key.reshape(SEG_DEV, SEG_LEN, columns), wanted)
    own_values = pick(segment_value.reshape(SEG_DEV, SEG_LEN, columns), wanted)
    got_keys, got_values = (
        lax.all_to_all(
            own_keys.reshape(devices, capacity, SEG_LEN, columns),
            "span",
            split_axis=0,
            concat_axis=0,
            tiled=True,
        ),
        lax.all_to_all(
            own_values.reshape(devices, capacity, SEG_LEN, columns),
            "span",
            split_axis=0,
            concat_axis=0,
            tiled=True,
        ),
    )
    source_keys = pick(got_keys.reshape(devices * capacity, SEG_LEN, columns), slots)
    source_values = pick(got_values.reshape(devices * capacity, SEG_LEN, columns), slots)
    crossed = attend(cross_query, source_keys, source_values).astype(jnp.bfloat16)
    encoded = (self_out.astype(jnp.float32) + crossed.astype(jnp.float32)).astype(jnp.bfloat16)
    encoded = encoded.reshape(per_device * NBR_LEN, columns)
    key_totals = lax.psum(squares(encoded), "head")
    keys_all = normalize(encoded, key_totals, full_width)
    before_keys, before_values = from_behind(
        (keys_all[-panel_rows:], encoded[-panel_rows:]), "span", 1
    )
    used_keys = jnp.concatenate([before_keys, keys_all[:-panel_rows]], axis=0)
    used_values = jnp.concatenate([before_values, encoded[:-panel_rows]], axis=0)
    blended = attend(
        decoder_query.reshape(SEG_DEV, SEG_LEN, columns),
        used_keys.reshape(SEG_DEV, panel_rows, columns),
        used_values.reshape(SEG_DEV, panel_rows, columns),
    ).astype(jnp.bfloat16)
    return blended.reshape(SEG_DEV * SEG_LEN, columns)


MESH = pl.DeviceIdType.MESH
GROUPS = 4


def dot_t(a, b):
    return lax.dot_general(a, b, (((1,), (1,)), ((), ())), preferred_element_type=jnp.float32)


def dot_first(a, b):
    return lax.dot_general(a, b, (((0,), (0,)), ((), ())), preferred_element_type=jnp.float32)


def apart(rows):
    count = rows.shape[1] // HEAD_DIM
    zero = jnp.zeros((rows.shape[0], HEAD_DIM), rows.dtype)
    lines = []
    for h in range(count):
        own = rows[:, h * HEAD_DIM:(h + 1) * HEAD_DIM]
        lines.append(jnp.concatenate([own if k == h else zero for k in range(count)], axis=1))
    return jnp.concatenate(lines, axis=0)


def softmax(scores, axis):
    weights = jnp.exp2(scores - jnp.max(scores, axis=axis, keepdims=True))
    inverse = 1.0 / jnp.sum(weights, axis=axis, keepdims=True)
    return (weights * inverse).astype(jnp.bfloat16)


def gather_kernel(
    heads_axis, full_width,
    src_ref, nq_hbm, nk_hbm, nv_hbm, sk_hbm, sv_hbm, dq_hbm, out_ref,
    nq, nk, nv, dq, *rest,
):
    kbufs, vbufs = rest[:GROUPS], rest[GROUPS:2 * GROUPS]
    (own_out, mixing, asked, enc, squares_acc, row_scale, key_scale,
     stat1, stat2, peer1, peer2, behind2,
     in_sem, dq_sem, local_sem, send_sem, recv_sem,
     stat_send, stat_recv, prior_send, prior_recv) = rest[2 * GROUPS:]
    per_device = nq.shape[0]
    seg_dev = dq.shape[0]
    columns = nq.shape[2]
    width = columns // GROUPS
    group_heads = width // HEAD_DIM
    span = lax.axis_size("span")
    me = lax.axis_index("span")
    lane = lax.axis_index("head")
    core, across, along = me ^ 1, me ^ 2, me ^ 4
    after = lax.rem(me + 1, span)
    before = lax.rem(me + span - 1, span)
    softmax_scale = HEAD_DIM ** (-0.5) / math.log(2.0)

    barrier = pltpu.get_barrier_semaphore()
    greeted = 0
    for target in (core, across, along):
        pl.semaphore_signal(barrier, inc=1, device_id={"span": target, "head": lane}, device_id_type=MESH)
        greeted += 1
    for k in range(1, heads_axis):
        other = lax.rem(lane + k, heads_axis)
        pl.semaphore_signal(barrier, inc=1, device_id={"span": me, "head": other}, device_id_type=MESH)
        greeted += 1
    for k in range(heads_axis):
        other = lax.rem(lane + k, heads_axis)
        for target in (after, before):
            pl.semaphore_signal(barrier, inc=1, device_id={"span": target, "head": other}, device_id_type=MESH)
            greeted += 1
    pl.semaphore_wait(barrier, greeted)

    chunks = 2 * GROUPS

    def buffer(j):
        return (kbufs + vbufs)[j]

    def source(j):
        hbm = (sk_hbm, sv_hbm)[j // GROUPS]
        return hbm.at[:, :, pl.ds((j % GROUPS) * width, width)]

    def block(j, owner):
        return buffer(j).at[pl.ds(owner * seg_dev, seg_dev)]

    def half(j, owner, part):
        rows = seg_dev // 2
        return buffer(j).at[pl.ds(owner * seg_dev + part * rows, rows)]

    sent = {}

    def push(kind, j, src, dst, target):
        copy = pltpu.make_async_remote_copy(
            src_ref=src, dst_ref=dst, send_sem=send_sem.at[kind, j], recv_sem=recv_sem.at[kind, j],
            device_id={"span": target, "head": lane}, device_id_type=MESH)
        copy.start()
        sent[kind, j] = copy

    def direct(j):
        push(0, j, source(j), block(j, me), across)
        push(1, j, source(j), block(j, me), along)

    local = []
    for j in range(chunks):
        direct(j)

    for i in range(per_device):
        for a, (hbm, vm) in enumerate(((nq_hbm, nq), (nk_hbm, nk), (nv_hbm, nv))):
            pltpu.make_async_copy(hbm.at[i], vm.at[i], in_sem.at[a, i]).start()
    dq_copy = pltpu.make_async_copy(dq_hbm, dq, dq_sem)
    dq_copy.start()

    for j in range(chunks):
        push(4, j, source(j), block(j, me), core)
        copy = pltpu.make_async_copy(source(j), block(j, me), local_sem.at[j])
        copy.start()
        local.append(copy)

    def forward(j):
        for part in range(2):
            sent[2 + part, j].wait_recv()
            push(7 + part, j, half(j, me ^ 6, part), half(j, me ^ 6, part), core)

    def step(j):
        sent[1, j].wait_recv()
        push(2, j, half(j, along, 0), half(j, along, 0), across)
        sent[0, j].wait_recv()
        push(3, j, half(j, across, 1), half(j, across, 1), along)
        push(5, j, block(j, across), block(j, across), core)
        push(6, j, block(j, along), block(j, along), core)

    def arrived(j):
        local[j].wait()
        for kind in (4, 5, 6, 7, 8):
            sent[kind, j].wait_recv()

    def self_step(i, carry):
        for a, (hbm, vm) in enumerate(((nq_hbm, nq), (nk_hbm, nk), (nv_hbm, nv))):
            pltpu.make_async_copy(hbm.at[i], vm.at[i], in_sem.at[a, i]).wait()
        total = jnp.zeros((NBR_LEN, HEAD_DIM), jnp.float32)
        for base in range(0, columns // HEAD_DIM, 8):
            together = range(base, base + 8)
            cols = [pl.ds(h * HEAD_DIM, HEAD_DIM) for h in together]
            scores = [dot_t(nk[i, :, c], nq[i, :, c]) * softmax_scale for c in cols]
            weights = [softmax(x, 0) for x in scores]
            outs = [dot_first(w, nv[i, :, c]).astype(jnp.bfloat16) for w, c in zip(weights, cols)]
            for h, o in zip(together, outs):
                own_out[h // group_heads, i, :, pl.ds((h % group_heads) * HEAD_DIM, HEAD_DIM)] = o
                wide = o.astype(jnp.float32)
                total = total + wide * wide
        stat1[pl.ds(i, 1), :] = jnp.sum(total.T, axis=0, keepdims=True)
        return carry

    def exchange(kind, stat, peer):
        out = []
        for k in range(1, heads_axis):
            other = lax.rem(lane + k, heads_axis)
            copy = pltpu.make_async_remote_copy(
                src_ref=stat, dst_ref=peer.at[k - 1],
                send_sem=stat_send.at[kind, k - 1], recv_sem=stat_recv.at[kind, k - 1],
                device_id={"span": me, "head": other}, device_id_type=MESH)
            copy.start()
            out.append(copy)
        return out

    def weigh(g):
        arrived(g)

        def some(t, carry):
            rows = [4 * t + b for b in range(4)]
            keys = [apart(kbufs[g][src_ref[i % NEIGHBOURS, i // NEIGHBOURS]]) for i in rows]
            scores = [dot_t(k, own_out[g, i]) * row_scale[pl.ds(i, 1), :] for k, i in zip(keys, rows)]
            weights = [softmax(x.reshape(group_heads, SEG_LEN, NBR_LEN), 1) for x in scores]
            for i, w in zip(rows, weights):
                mixing[g, i] = w.reshape(group_heads * SEG_LEN, NBR_LEN)
            return carry

        lax.fori_loop(0, per_device // 4, some, 0)

    def cross_rows(g, rows):
        values = [apart(vbufs[g][src_ref[i % NEIGHBOURS, i // NEIGHBOURS]]) for i in rows]
        crossed = [dot_first(mixing[g, i], v).astype(jnp.bfloat16) for i, v in zip(rows, values)]
        for i, x in zip(rows, crossed):
            both = (own_out[g, i].astype(jnp.float32) + x.astype(jnp.float32)).astype(jnp.bfloat16)
            enc[g, NEIGHBOURS + i] = both
            wide = both.astype(jnp.float32)
            wide = wide * wide
            total = wide[:, :HEAD_DIM]
            for h in range(1, group_heads):
                total = total + wide[:, h * HEAD_DIM:(h + 1) * HEAD_DIM]
            if g > 0:
                total = total + squares_acc[i]
            if g < GROUPS - 1:
                squares_acc[i] = total
            else:
                stat2[pl.ds(i, 1), :] = jnp.sum(total.T, axis=0, keepdims=True)

    prior = []

    def panel(g, u):
        return enc[g, pl.ds(NEIGHBOURS * u, NEIGHBOURS)].reshape(NEIGHBOURS * NBR_LEN, width)

    def ask(g, u):
        asked[u, g] = dot_t(panel(g, u), apart(dq[u, :, pl.ds(g * width, width)]))

    def cross(g):
        arrived(GROUPS + g)
        cross_rows(g, list(range(per_device - NEIGHBOURS, per_device)))
        copy = pltpu.make_async_remote_copy(
            src_ref=enc.at[g, pl.ds(per_device, NEIGHBOURS)], dst_ref=enc.at[g, pl.ds(0, NEIGHBOURS)],
            send_sem=prior_send.at[g], recv_sem=prior_recv.at[g],
            device_id={"span": after, "head": lane}, device_id_type=MESH)
        copy.start()
        prior.append(copy)

        def rest_step(t, carry):
            cross_rows(g, [3 * t + b for b in range(3)])
            return carry

        lax.fori_loop(0, (per_device - NEIGHBOURS) // 3, rest_step, 0)

    quarter = per_device // 4
    for j in range(4):
        lax.fori_loop(j * quarter, (j + 1) * quarter, self_step, 0)
        if j > 0:
            step(2 * j - 2)
            step(2 * j - 1)
    first_stats = exchange(0, stat1, peer1)
    step(6)
    for copy in first_stats:
        copy.wait_recv()
    total1 = stat1[...]
    for k in range(heads_axis - 1):
        total1 = total1 + peer1[k]
    row_scale[...] = lax.rsqrt(total1 / full_width + epsilon) * softmax_scale
    step(7)
    forward(0)
    for g in range(GROUPS):
        forward(g + 1)
        weigh(g)
    dq_copy.wait()
    for g in range(GROUPS):
        if g + 1 < GROUPS:
            forward(GROUPS + 1 + g)
        cross(g)
        if g + 1 < GROUPS:
            for u in range(1, seg_dev):
                ask(g, u)

    second_stats = exchange(1, stat2, peer2)
    behind_stats = []
    for k in range(heads_axis):
        other = lax.rem(lane + k, heads_axis)
        copy = pltpu.make_async_remote_copy(
            src_ref=stat2, dst_ref=behind2.at[k],
            send_sem=stat_send.at[2, k], recv_sem=stat_recv.at[2, k],
            device_id={"span": after, "head": other}, device_id_type=MESH)
        copy.start()
        behind_stats.append(copy)
    for u in range(1, seg_dev):
        ask(GROUPS - 1, u)
    for copy in second_stats:
        copy.wait_recv()
    total2 = stat2[...]
    for k in range(heads_axis - 1):
        total2 = total2 + peer2[k]
    key_scale[pl.ds(NEIGHBOURS, per_device), :] = lax.rsqrt(total2 / full_width + epsilon) * softmax_scale

    def decode_step(u, carry):
        scale = jnp.concatenate([
            jnp.broadcast_to(key_scale[pl.ds(NEIGHBOURS * u + n, 1), :], (NBR_LEN, NBR_LEN)).T
            for n in range(NEIGHBOURS)], axis=0)
        weights = [softmax(asked[u, g] * scale, 0) for g in range(GROUPS)]
        outs = [dot_first(w, panel(g, u)).astype(jnp.bfloat16) for g, w in enumerate(weights)]
        for g, out in enumerate(outs):
            for h in range(group_heads):
                lo = h * HEAD_DIM
                out_ref[u, :, pl.ds(g * width + lo, HEAD_DIM)] = out[h * SEG_LEN:(h + 1) * SEG_LEN, lo:lo + HEAD_DIM]
        return carry

    lax.fori_loop(1, seg_dev, decode_step, 0)
    for copy in behind_stats:
        copy.wait_recv()
    for copy in prior:
        copy.wait_recv()
    total3 = behind2[0]
    for k in range(1, heads_axis):
        total3 = total3 + behind2[k]
    total3 = lax.rsqrt(total3 / full_width + epsilon) * softmax_scale
    key_scale[pl.ds(0, NEIGHBOURS), :] = total3[per_device - NEIGHBOURS:]

    @pl.when(me == 0)
    def _():
        enc[:, pl.ds(0, NEIGHBOURS)] = jnp.zeros((GROUPS, NEIGHBOURS, NBR_LEN, width), jnp.bfloat16)

    for g in range(GROUPS):
        ask(g, 0)
    decode_step(0, 0)
    for copy in list(sent.values()) + prior + first_stats + second_stats + behind_stats:
        copy.wait_send()


def gather_all(operands):
    columns = operands[1].shape[2]
    heads_axis = lax.axis_size("head")
    span = lax.axis_size("span")
    per_device = SEG_DEV * NEIGHBOURS
    width = columns // GROUPS
    bf16, f32 = jnp.bfloat16, jnp.float32
    neighbour_shape = (per_device, NBR_LEN, columns)
    segment_shape = (SEG_DEV, SEG_LEN, columns)
    chunks = 2 * GROUPS
    any_space = pl.BlockSpec(memory_space=pltpu.HBM)
    dma = pltpu.SemaphoreType.DMA
    return pl.pallas_call(
        functools.partial(gather_kernel, heads_axis, columns * heads_axis),
        out_shape=jax.ShapeDtypeStruct(segment_shape, bf16),
        in_specs=[pl.BlockSpec(memory_space=pltpu.SMEM)] + [any_space] * 6,
        out_specs=pl.BlockSpec(memory_space=pltpu.VMEM),
        scratch_shapes=[pltpu.VMEM(neighbour_shape, bf16)] * 3
        + [pltpu.VMEM(segment_shape, bf16)]
        + [pltpu.VMEM((span * SEG_DEV, SEG_LEN, width), bf16)] * chunks
        + [
            pltpu.VMEM((GROUPS, per_device, NBR_LEN, width), bf16),
            pltpu.VMEM((GROUPS, per_device, width // HEAD_DIM * SEG_LEN, NBR_LEN), bf16),
            pltpu.VMEM((SEG_DEV, GROUPS, NEIGHBOURS * NBR_LEN, width // HEAD_DIM * SEG_LEN), f32),
            pltpu.VMEM((GROUPS, per_device + NEIGHBOURS, NBR_LEN, width), bf16),
            pltpu.VMEM((per_device, NBR_LEN, HEAD_DIM), f32),
            pltpu.VMEM((per_device, NBR_LEN), f32),
            pltpu.VMEM((per_device + NEIGHBOURS, NBR_LEN), f32),
            pltpu.VMEM((per_device, NBR_LEN), f32),
            pltpu.VMEM((per_device, NBR_LEN), f32),
            pltpu.VMEM((heads_axis - 1, per_device, NBR_LEN), f32),
            pltpu.VMEM((heads_axis - 1, per_device, NBR_LEN), f32),
            pltpu.VMEM((heads_axis, per_device, NBR_LEN), f32),
            dma((3, per_device)),
            dma,
            dma((chunks,)),
            dma((9, chunks)),
            dma((9, chunks)),
            dma((3, heads_axis)),
            dma((3, heads_axis)),
            dma((GROUPS,)),
            dma((GROUPS,)),
        ],
        compiler_params=pltpu.CompilerParams(
            collective_id=1, has_side_effects=True, vmem_limit_bytes=53 * 1024 * 1024),
    )(*operands)


PHASES = (2, 3, 3)
SLOTS = sum(PHASES)
STARTS = tuple(sum(PHASES[:p]) for p in range(len(PHASES)))
FORWARDS = (0, 0, 1, 2, 2, 3, 4, 5)
CHIP_SEGS = 8
LANES = 128


def selections():
    upper = lax.broadcasted_iota(jnp.int32, (LANES, LANES), 0)
    lower = lax.broadcasted_iota(jnp.int32, (LANES, LANES), 1)
    row_chip, column_chip = upper // CHIP_SEGS, lower // CHIP_SEGS
    same = jnp.where(row_chip == column_chip, 1.0, 0.0)
    ahead = jnp.where(upper < lower, same, 0.0)
    others = [jnp.where((row_chip ^ k) == column_chip, 1.0, 0.0) for k in range(1, 4)]
    return jnp.concatenate(others + [same, ahead], axis=1).astype(jnp.bfloat16)


def routes(needs, select, mine):
    f32, bf16 = jnp.float32, jnp.bfloat16
    lane = lax.broadcasted_iota(jnp.int32, (1, LANES), 1)
    chip = lane // CHIP_SEGS
    within = (lane % CHIP_SEGS).astype(f32)

    def at(k):
        total = jnp.zeros((1, LANES), f32)
        for t, row in enumerate(needs):
            total = total + jnp.where((chip ^ k) == t, row, 0.0)
        return total

    n1, n2, n3 = at(1), at(2), at(3)
    only1, only2 = n3 * n1 * (1 - n2), n3 * n2 * (1 - n1)
    both, none = n3 * n1 * n2, n3 * (1 - n1) * (1 - n2)
    zero = jnp.zeros((1, LANES), f32)
    stacked = jnp.concatenate([n1, n2, only1, only2, both, none, zero, zero], axis=0)
    counts = jnp.dot(stacked.astype(bf16), select, preferred_element_type=f32)

    def count(r):
        return [counts[r:r + 1, k * LANES:(k + 1) * LANES] for k in (3, 0, 1, 2)]

    def rank(r):
        return counts[r:r + 1, 4 * LANES:]

    n1c, n2c, o1, o2, b, n = [count(r) for r in range(6)]
    every = range(4)

    def clip(value, top):
        return jnp.minimum(jnp.maximum(value, 0.0), top)

    x = [n1c[k] + o2[k ^ 2] for k in every]
    y = [n2c[k] + o1[k ^ 1] for k in every]
    pb = [clip(jnp.floor((b[k] + x[k ^ 2] - y[k ^ 1] + 1) * 0.5), b[k]) for k in every]
    x = [x[k] + b[k ^ 2] - pb[k ^ 2] for k in every]
    y = [y[k] + pb[k ^ 1] for k in every]
    pn = [clip(jnp.floor((n[k] + jnp.maximum(y[k], x[k ^ 2]) - jnp.maximum(x[k], y[k ^ 1]) + 1) * 0.5), n[k])
          for k in every]
    x, y = ([x[k] + pn[k] + n[k ^ 2] - pn[k ^ 2] for k in every],
            [y[k] + n[k] - pn[k] + pn[k ^ 1] for k in every])
    over1 = [jnp.maximum(x[k], y[k ^ 1]) - SLOTS for k in every]
    over2 = [jnp.maximum(y[k], x[k ^ 2]) - SLOTS for k in every]
    shift = [clip(jnp.minimum(over2[k], -over1[k]), n[k] - pn[k]) - clip(jnp.minimum(over1[k], -over2[k]), pn[k])
             for k in every]
    pn = [pn[k] + shift[k] for k in every]
    x, y = ([x[k] + shift[k] - shift[k ^ 2] for k in every],
            [y[k] - shift[k] + shift[k ^ 1] for k in every])
    m1 = [clip(jnp.minimum(y[k ^ 1] - SLOTS, SLOTS - jnp.maximum(y[k], x[k ^ 2])), o1[k]) for k in every]
    m2 = [clip(jnp.minimum(x[k ^ 2] - SLOTS, SLOTS - jnp.maximum(x[k], y[k ^ 1])), o2[k]) for k in every]

    def below(r, limit, rows):
        return jnp.where(rank(r) < limit, rows, 0.0)

    path1 = only1 - below(2, m1[0], only1) + below(3, m2[0], only2) + below(4, pb[0], both) + below(5, pn[0], none)
    path2 = n3 - path1
    own_x, own_y = jnp.maximum(n1, path1), jnp.maximum(n2, path2)
    stacked = jnp.concatenate(
        [path1, path2, own_x - path1, own_y - path2, zero, zero, zero, zero], axis=0)
    again = jnp.dot(stacked.astype(bf16), select[:, 3 * LANES:], preferred_element_type=f32)
    relays, ranks = again[:, :LANES], again[:, LANES:]
    slot_x = jnp.where(path1 > 0, ranks[0:1], relays[0:1] + ranks[2:3])
    slot_y = jnp.where(path2 > 0, ranks[1:2], relays[1:2] + ranks[3:4])

    def forwarded(own, place):
        return jnp.maximum(own, jnp.where(place < 2, 2.0, 3.0)) + place

    forward_y = forwarded(n2c[1] + n[1] - pn[1] + m1[1], ranks[0:1])
    forward_x = forwarded(n1c[2] + pn[2] + m2[2], ranks[1:2])
    last = jnp.maximum(path1 * forward_y, path2 * forward_x)
    over = jnp.max(jnp.where(last >= SLOTS, 1.0, 0.0), axis=1, keepdims=True)

    side = chip ^ mine
    place = jnp.where(
        side == 0, within,
        CHIP_SEGS + jnp.where(
            side == 1, slot_x,
            jnp.where(side == 2, SLOTS + slot_y, jnp.where(path1 > 0, SLOTS + forward_y, forward_x))))
    place = jnp.minimum(place, CHIP_SEGS + 2 * SLOTS - 1.0)

    def sends(own, slot, relay, forward, arrives):
        mine_own = (side == 0) & (own > 0)
        number = jnp.where(mine_own, slot, jnp.where(relay, forward, -1.0))
        code = jnp.where(mine_own, within, CHIP_SEGS + arrives)
        wanted = lax.broadcasted_iota(jnp.int32, (SLOTS, LANES), 0).astype(f32)
        return jnp.sum(jnp.where(number == wanted, code, 0.0), axis=1, keepdims=True)

    send_x = sends(own_x, slot_x, (side == 2) & (path2 > 0), forward_x, slot_y)
    send_y = sends(own_y, slot_y, (side == 1) & (path1 > 0), forward_y, slot_x)
    rows = [send_x, send_y, place, over]
    return jnp.concatenate([jnp.broadcast_to(r, (8, LANES)) for r in rows], axis=0).astype(jnp.int32)


ORDER = ((0, 0), (1, 0), (2, 0), (0, 1), (1, 1), (3, 0), (0, 2), (1, 2), (2, 1), (3, 1), (2, 2), (3, 2))


def kernel(
    heads_axis, full_width,
    src_ref, nq_hbm, nk_hbm, nv_hbm, sk_hbm, sv_hbm, dq_hbm, out_ref, over_ref,
    nq, nk, nv, dq, *rest,
):
    own_a, own_b, recv_a, recv_b, send_a = (rest[4 * j:4 * j + 4] for j in range(5))
    (first, answer, first_sem, ask_send, ask_recv, answer_send, answer_recv, select, need, needs, table, lookup, own_out, mixing, asked, enc, squares_acc, row_scale, key_scale,
     stat1, stat2, peer1, peer2, peer3,
     in_sem, dq_sem, local_sem, table_sem, need_send, need_recv, core_send, core_recv,
     link_send, link_recv, pass_send, pass_recv,
     stat_send, stat_recv) = rest[20:]
    per_device = nq.shape[0]
    seg_dev = dq.shape[1]
    columns = nq.shape[2]
    width = columns // GROUPS
    group_heads = width // HEAD_DIM
    span = lax.axis_size("span")
    me = lax.axis_index("span")
    lane = lax.axis_index("head")
    side = lax.rem(me, 2)
    core, across, along = me ^ 1, me ^ 2, me ^ 4
    after = lax.rem(me + 1, span)
    before = lax.rem(me + span - 1, span)
    softmax_scale = HEAD_DIM ** (-0.5) / math.log(2.0)

    def at(target, head):
        return {"span": target, "head": head}

    def columns_of(half, q):
        return pl.ds(pl.multiple_of((2 * half + q) * width, width), width)

    def source(k, half):
        hbm = (sk_hbm, sv_hbm)[k % 2]
        return hbm.at[:, :, columns_of(half, k // 2)]

    mine_rows = pl.ds(pl.multiple_of(side * seg_dev, seg_dev), seg_dev)

    def inputs(i):
        return [pltpu.make_async_copy(hbm.at[i], vm.at[i], in_sem.at[a, i])
                for a, (hbm, vm) in enumerate(((nq_hbm, nq), (nk_hbm, nk), (nv_hbm, nv)))]

    for i in range(2):
        for copy in inputs(i):
            copy.start()
    local = {}
    for k in range(4):
        for b, (own, half) in enumerate(((own_a[k], side), (own_b[k], 1 - side))):
            copy = pltpu.make_async_copy(source(k, half), own.at[mine_rows], local_sem.at[b, k])
            copy.start()
            local[b, k] = copy
    for i in range(2, per_device):
        for copy in inputs(i):
            copy.start()
    dq_copies = []
    for g in range(GROUPS):
        copy = pltpu.make_async_copy(
            dq_hbm.at[pl.ds(1, seg_dev - 1), :, pl.ds(g * width, width)], dq.at[g, pl.ds(0, seg_dev - 1)],
            dq_sem.at[g])
        copy.start()
        dq_copies.append(copy)
    stat2[1] = jnp.zeros_like(stat2[1])

    @pl.when(me == 0)
    def _():
        pltpu.make_async_copy(dq_hbm.at[0], first, first_sem).start()

    @pl.when(me == span - 1)
    def _():
        for g in range(GROUPS):
            dq[g, seg_dev - 1] = jnp.zeros((SEG_LEN, width), jnp.bfloat16)

    segment = lax.broadcasted_iota(jnp.int32, (8, LANES), 1)
    wanted = jnp.zeros((8, LANES), jnp.float32)
    for i in range(per_device):
        wanted = jnp.where(segment == src_ref[i % NEIGHBOURS, i // NEIGHBOURS], 1.0, wanted)
    need[...] = wanted
    select[...] = selections()

    barrier = pltpu.get_barrier_semaphore()
    greeted = 0
    for k in range(1, span):
        pl.semaphore_signal(barrier, inc=1, device_id=at(me ^ k, lane), device_id_type=MESH)
        greeted += 1
    for k in range(1, heads_axis):
        other = lax.rem(lane + k, heads_axis)
        pl.semaphore_signal(barrier, inc=1, device_id=at(me, other), device_id_type=MESH)
        greeted += 1
    pl.semaphore_wait(barrier, greeted)

    def remote(src, dst, send_sem, recv_sem, target):
        copy = pltpu.make_async_remote_copy(
            src_ref=src, dst_ref=dst, send_sem=send_sem, recv_sem=recv_sem,
            device_id=at(*target), device_id_type=MESH)
        copy.start()
        return copy

    told = [remote(need, needs.at[me], need_send.at[k - 1], need_recv.at[k - 1], (me ^ k, lane))
            for k in range(1, span)]
    needs[me] = wanted

    def query_copy(g):
        return pltpu.make_async_remote_copy(
            src_ref=dq_hbm.at[0, :, pl.ds(g * width, width)], dst_ref=dq.at[g, seg_dev - 1],
            send_sem=ask_send.at[g], recv_sem=ask_recv.at[g], device_id=at(before, lane), device_id_type=MESH)

    def answer_copy(g):
        block = pl.ds(g * width, width)
        return pltpu.make_async_remote_copy(
            src_ref=answer.at[:, block], dst_ref=out_ref.at[0, :, block],
            send_sem=answer_send.at[g], recv_sem=answer_recv.at[g], device_id=at(after, lane), device_id_type=MESH)

    @pl.when(me > 0)
    def _():
        for g in range(GROUPS):
            query_copy(g).start()

    given = {}
    for k in range(4):
        given[0, k] = remote(source(k, 1 - side), own_a[k].at[mine_rows], core_send.at[0, k], core_recv.at[0, k],
                             (core, lane))
        given[1, k] = remote(source(k, side), own_b[k].at[mine_rows], core_send.at[1, k], core_recv.at[1, k],
                             (core, lane))

    def owned(b, k):
        local[b, k].wait()
        given[b, k].wait_recv()

    sent, passed = {}, {}

    def slots(link, p):
        return pl.ds(link * SLOTS + STARTS[p], PHASES[p])

    def hand_on(k, p):
        for link in range(2):
            sent[k, p, link].wait_recv()
            block = slots(link, p)
            passed[k, p, link] = remote(recv_a[k].at[block], recv_b[k].at[block], pass_send.at[link, 3 * k + p],
                                        pass_recv.at[link, 3 * k + p], (core, lane))

    def advance(k, p):
        if p == 0:
            owned(0, k)
        else:
            hand_on(k, p - 1)
        for link, target in enumerate((across, along)):
            for i in range(STARTS[p], STARTS[p] + PHASES[p]):
                code = lookup[8 * link + i, 0]
                rows = own_a[k][jnp.clip(code, 0, CHIP_SEGS - 1)]
                for t in range(FORWARDS[i]):
                    rows = jnp.where(code == CHIP_SEGS + t, recv_a[k][(1 - link) * SLOTS + t], rows)
                send_a[k][link * SLOTS + i] = rows
            block = slots(link, p)
            sent[k, p, link] = remote(send_a[k].at[block], recv_a[k].at[block], link_send.at[link, 3 * k + p],
                                      link_recv.at[link, 3 * k + p], (target, lane))

    def finish(k):
        hand_on(k, len(PHASES) - 1)

    def arrived(b, k):
        if b == 1:
            owned(1, k)
            for p in range(len(PHASES)):
                for link in range(2):
                    passed[k, p, link].wait_recv()

    def rows_of(b, k, i):
        place = lookup[16, src_ref[i % NEIGHBOURS, i // NEIGHBOURS]]
        own, recv = ((own_a[k], recv_a[k]), (own_b[k], recv_b[k]))[b]
        return jnp.where(place < CHIP_SEGS, own[jnp.clip(place, 0, CHIP_SEGS - 1)],
                         recv[jnp.clip(place - CHIP_SEGS, 0, 2 * SLOTS - 1)])

    def self_step(i, carry):
        for copy in inputs(i):
            copy.wait()
        total = jnp.zeros((NBR_LEN, HEAD_DIM), jnp.float32)
        for base in range(0, columns // HEAD_DIM, 8):
            together = range(base, base + 8)
            cols = [pl.ds(h * HEAD_DIM, HEAD_DIM) for h in together]
            scores = [dot_t(nk[i, :, c], nq[i, :, c]) * softmax_scale for c in cols]
            weights = [softmax(x, 0) for x in scores]
            outs = [dot_first(w, nv[i, :, c]).astype(jnp.bfloat16) for w, c in zip(weights, cols)]
            for h, o in zip(together, outs):
                own_out[h // group_heads, i, :, pl.ds((h % group_heads) * HEAD_DIM, HEAD_DIM)] = o
                wide = o.astype(jnp.float32)
                total = total + wide * wide
        stat1[pl.ds(i, 1), :] = jnp.sum(total.T, axis=0, keepdims=True)
        return carry

    def exchange(kind, stat, peer):
        return [remote(stat, peer.at[k - 1], stat_send.at[kind, k - 1], stat_recv.at[kind, k - 1],
                       (me, lax.rem(lane + k, heads_axis))) for k in range(1, heads_axis)]

    def group(b, q):
        return 2 * (side if b == 0 else 1 - side) + q

    def weigh(b, q):
        arrived(b, 2 * q)
        g = group(b, q)

        def some(t, carry):
            rows = [4 * t + s for s in range(4)]
            keys = [apart(rows_of(b, 2 * q, i)) for i in rows]
            scores = [dot_t(k, own_out[g, i]) * row_scale[pl.ds(i, 1), :] for k, i in zip(keys, rows)]
            weights = [softmax(x.reshape(group_heads, SEG_LEN, NBR_LEN), 1) for x in scores]
            for i, w in zip(rows, weights):
                mixing[g, i] = w.reshape(group_heads * SEG_LEN, NBR_LEN)
            return carry

        lax.fori_loop(0, per_device // 4, some, 0)

    def cross_rows(b, q, rows):
        g = group(b, q)
        values = [apart(rows_of(b, 2 * q + 1, i)) for i in rows]
        crossed = [dot_first(mixing[g, i], v).astype(jnp.bfloat16) for i, v in zip(rows, values)]
        for i, x in zip(rows, crossed):
            both = (own_out[g, i].astype(jnp.float32) + x.astype(jnp.float32)).astype(jnp.bfloat16)
            enc[g, i] = both
            wide = both.astype(jnp.float32)
            wide = wide * wide
            total = wide[:, :HEAD_DIM]
            for h in range(1, group_heads):
                total = total + wide[:, h * HEAD_DIM:(h + 1) * HEAD_DIM]
            if (q, b) != (0, 0):
                total = total + squares_acc[i]
            if (q, b) != (1, 1):
                squares_acc[i] = total
            else:
                line = jnp.sum(total.T, axis=0, keepdims=True)
                stat2[0, pl.ds(i, 1), :] = line
                if len(rows) == NEIGHBOURS:
                    stat2[1, pl.ds(i, 1), :] = line

    def panel(g, u):
        return enc[g, pl.ds(NEIGHBOURS * u, NEIGHBOURS)].reshape(NEIGHBOURS * NBR_LEN, width)

    def ask(g, u):
        asked[u, g] = dot_t(panel(g, u), apart(dq[g, u]))

    def cross_last(b, q):
        arrived(b, 2 * q + 1)
        cross_rows(b, q, list(range(per_device - NEIGHBOURS, per_device)))

    def cross_others(b, q):
        def rest_step(t, carry):
            cross_rows(b, q, [3 * t + s for s in range(3)])
            return carry

        lax.fori_loop(0, (per_device - NEIGHBOURS) // 3, rest_step, 0)

    lax.fori_loop(0, 1, self_step, 0)
    for copy in told:
        copy.wait_recv()
    table[...] = routes([jnp.maximum(needs[2 * t][:1], needs[2 * t + 1][:1]) for t in range(span // 2)],
                        select[...], me // 2)
    copy = pltpu.make_async_copy(table, lookup, table_sem)
    copy.start()
    copy.wait()
    for k, p in ORDER[:3]:
        advance(k, p)
    lax.fori_loop(1, 3, self_step, 0)
    advance(*ORDER[3])
    lax.fori_loop(3, 5, self_step, 0)
    advance(*ORDER[4])
    advance(*ORDER[5])
    lax.fori_loop(5, per_device, self_step, 0)
    first_stats = exchange(0, stat1, peer1)
    for k, p in ORDER[6:8]:
        advance(k, p)
    for copy in first_stats:
        copy.wait_recv()
    total1 = stat1[...]
    for k in range(heads_axis - 1):
        total1 = total1 + peer1[k]
    row_scale[...] = lax.rsqrt(total1 / full_width + epsilon) * softmax_scale
    for k, p in ORDER[8:10]:
        advance(k, p)
    for copy in dq_copies:
        copy.wait()

    @pl.when(me < span - 1)
    def _():
        for g in range(GROUPS):
            query_copy(g).wait_recv()

    @pl.when(me == 0)
    def _():
        pltpu.make_async_copy(dq_hbm.at[0], first, first_sem).wait()
        for g in range(GROUPS):
            nothing = jnp.zeros((NEIGHBOURS * NBR_LEN, width), jnp.bfloat16)
            scores = dot_t(nothing, apart(first[:, g * width:(g + 1) * width])) * (epsilon ** -0.5 * softmax_scale)
            out = dot_first(softmax(scores, 0), nothing).astype(jnp.bfloat16)
            for h in range(group_heads):
                lo = h * HEAD_DIM
                out_ref[0, :, pl.ds(g * width + lo, HEAD_DIM)] = out[h * SEG_LEN:(h + 1) * SEG_LEN, lo:lo + HEAD_DIM]

    finish(0)
    weigh(0, 0)
    weigh(1, 0)
    finish(1)
    advance(*ORDER[10])
    cross_last(0, 0)
    cross_others(0, 0)
    advance(*ORDER[11])
    cross_last(1, 0)
    cross_others(1, 0)
    for b in range(2):
        for u in range(seg_dev):
            ask(group(b, 0), u)
    finish(2)
    weigh(0, 1)
    finish(3)
    weigh(1, 1)
    cross_last(0, 1)
    cross_others(0, 1)
    cross_last(1, 1)
    last_stats = exchange(2, stat2.at[1], peer3)
    cross_others(1, 1)
    second_stats = exchange(1, stat2.at[0], peer2)
    for b in range(2):
        for u in reversed(range(seg_dev)):
            ask(group(b, 1), u)

    def settle(mine, copies, peer, rows):
        for copy in copies:
            copy.wait_recv()
        total = mine
        for k in range(heads_axis - 1):
            total = total + peer[k]
        scale = lax.rsqrt(total / full_width + epsilon) * softmax_scale
        key_scale[rows] = scale[rows]

    def decoded(u):
        scale = jnp.concatenate([
            jnp.broadcast_to(key_scale[pl.ds(NEIGHBOURS * u + n, 1), :], (NBR_LEN, NBR_LEN)).T
            for n in range(NEIGHBOURS)], axis=0)
        weights = [softmax(asked[u, g] * scale, 0) for g in range(GROUPS)]
        outs = [dot_first(w, panel(g, u)).astype(jnp.bfloat16) for g, w in enumerate(weights)]
        for g, out in enumerate(outs):
            for h in range(group_heads):
                lo = h * HEAD_DIM
                yield g * width + lo, out[h * SEG_LEN:(h + 1) * SEG_LEN, lo:lo + HEAD_DIM]

    def decode_step(u, carry):
        for lo, out in decoded(u):
            out_ref[u + 1, :, pl.ds(lo, HEAD_DIM)] = out
        return carry

    settle(stat2[1], last_stats, peer3, slice(per_device - NEIGHBOURS, per_device))
    for lo, out in decoded(seg_dev - 1):
        answer[:, pl.ds(lo, HEAD_DIM)] = out

    @pl.when(me < span - 1)
    def _():
        for g in range(GROUPS):
            answer_copy(g).start()

    settle(stat2[0], second_stats, peer2, slice(0, per_device - NEIGHBOURS))
    lax.fori_loop(0, seg_dev - 1, decode_step, 0)
    over_ref[0, 0] = lookup[24, 0]

    @pl.when(me > 0)
    def _():
        for g in range(GROUPS):
            answer_copy(g).wait_recv()
            query_copy(g).wait_send()

    @pl.when(me < span - 1)
    def _():
        for g in range(GROUPS):
            answer_copy(g).wait_send()

    for copy in (told + list(given.values()) + list(sent.values()) + list(passed.values())
                 + first_stats + last_stats + second_stats):
        copy.wait_send()


def fused_body(
    neighbour_query,
    neighbour_key,
    neighbour_value,
    segment_key,
    segment_value,
    decoder_query,
    sources,
):
    columns = neighbour_query.shape[1]
    heads_axis = lax.axis_size("head")
    span = lax.axis_size("span")
    per_device = SEG_DEV * NEIGHBOURS
    width = columns // GROUPS
    bf16, f32 = jnp.bfloat16, jnp.float32
    neighbour_shape = (per_device, NBR_LEN, columns)
    segment_shape = (SEG_DEV, SEG_LEN, columns)
    any_space = pl.BlockSpec(memory_space=pltpu.HBM)
    dma = pltpu.SemaphoreType.DMA
    own = pltpu.VMEM((CHIP_SEGS, SEG_LEN, width), bf16)
    slots = pltpu.VMEM((2 * SLOTS, SEG_LEN, width), bf16)
    steps = 4 * len(PHASES)
    operands = (
        sources.T,
        neighbour_query.reshape(neighbour_shape),
        neighbour_key.reshape(neighbour_shape),
        neighbour_value.reshape(neighbour_shape),
        segment_key.reshape(segment_shape),
        segment_value.reshape(segment_shape),
        decoder_query.reshape(segment_shape),
    )
    out, over = pl.pallas_call(
        functools.partial(kernel, heads_axis, columns * heads_axis),
        out_shape=(jax.ShapeDtypeStruct(segment_shape, bf16), jax.ShapeDtypeStruct((1, 1), jnp.int32)),
        in_specs=[pl.BlockSpec(memory_space=pltpu.SMEM)] + [any_space] * 6,
        out_specs=(pl.BlockSpec(memory_space=pltpu.VMEM), pl.BlockSpec(memory_space=pltpu.SMEM)),
        scratch_shapes=[pltpu.VMEM(neighbour_shape, bf16)] * 3
        + [pltpu.VMEM((GROUPS, SEG_DEV, SEG_LEN, width), bf16)]
        + [own] * 8 + [slots] * 12
        + [
            pltpu.VMEM((SEG_LEN, columns), bf16),
            pltpu.VMEM((SEG_LEN, columns), bf16),
            dma,
            dma((GROUPS,)),
            dma((GROUPS,)),
            dma((GROUPS,)),
            dma((GROUPS,)),
            pltpu.VMEM((LANES, 5 * LANES), bf16),
            pltpu.VMEM((8, LANES), f32),
            pltpu.VMEM((span, 8, LANES), f32),
            pltpu.VMEM((32, LANES), jnp.int32),
            pltpu.SMEM((32, LANES), jnp.int32),
            pltpu.VMEM((GROUPS, per_device, NBR_LEN, width), bf16),
            pltpu.VMEM((GROUPS, per_device, width // HEAD_DIM * SEG_LEN, NBR_LEN), bf16),
            pltpu.VMEM((SEG_DEV, GROUPS, NEIGHBOURS * NBR_LEN, width // HEAD_DIM * SEG_LEN), f32),
            pltpu.VMEM((GROUPS, per_device, NBR_LEN, width), bf16),
            pltpu.VMEM((per_device, NBR_LEN, HEAD_DIM), f32),
            pltpu.VMEM((per_device, NBR_LEN), f32),
            pltpu.VMEM((per_device, NBR_LEN), f32),
            pltpu.VMEM((per_device, NBR_LEN), f32),
            pltpu.VMEM((2, per_device, NBR_LEN), f32),
            pltpu.VMEM((heads_axis - 1, per_device, NBR_LEN), f32),
            pltpu.VMEM((heads_axis - 1, per_device, NBR_LEN), f32),
            pltpu.VMEM((heads_axis - 1, per_device, NBR_LEN), f32),
            dma((3, per_device)),
            dma((GROUPS,)),
            dma((2, 4)),
            dma,
            dma((span - 1,)),
            dma((span - 1,)),
            dma((2, 4)),
            dma((2, 4)),
            dma((2, steps)),
            dma((2, steps)),
            dma((2, steps)),
            dma((2, steps)),
            dma((3, heads_axis)),
            dma((3, heads_axis)),
        ],
        compiler_params=pltpu.CompilerParams(
            collective_id=0, has_side_effects=True, vmem_limit_bytes=53 * 1024 * 1024),
    )(*operands)
    return lax.cond(
        over[0, 0] > 0,
        lambda: gather_all(operands).reshape(SEG_DEV * SEG_LEN, columns),
        lambda: out.reshape(SEG_DEV * SEG_LEN, columns),
    )


def solution(mesh):
    placed = (
        P("span", "head"),
        P("span", "head"),
        P("span", "head"),
        P("span", "head"),
        P("span", "head"),
        P("span", "head"),
        P("span", None),
    )
    cube = mesh.shape["span"] == 2 * 2 * 2
    return jax.shard_map(
        fused_body if cube else body, mesh=mesh, in_specs=placed, out_specs=P("span", "head"), check_vma=False
    )
```

```python
import functools
import math

import jax
import jax.numpy as jnp
from jax import lax
from jax.experimental import pallas as pl
from jax.experimental.pallas import tpu as pltpu
from jax.sharding import PartitionSpec as P

HEAD_DIM = 128
SEG_LEN = 64
NBR_LEN = 128
NEIGHBOURS = 2
SEG_DEV = 4


epsilon = 1e-06


def from_behind(x, axis, by):
    count = lax.axis_size(axis)
    pairs = [(i, i + by) for i in range(count) if 0 <= i + by < count]
    return lax.ppermute(x, axis, pairs)


def attend(query_rows, key_rows, value_rows):
    groups, length, columns = query_rows.shape
    head_count = columns // HEAD_DIM
    query_heads = query_rows.reshape(groups, length, head_count, HEAD_DIM)
    key_heads = key_rows.reshape(groups, key_rows.shape[1], head_count, HEAD_DIM)
    value_heads = value_rows.reshape(groups, value_rows.shape[1], head_count, HEAD_DIM)
    logit_scores = jnp.einsum(
        "bqhd,bkhd->bhqk", query_heads, key_heads, preferred_element_type=jnp.float32
    ) * HEAD_DIM ** (-0.5)
    logit_scores = logit_scores - jnp.max(logit_scores, axis=-1, keepdims=True)
    weights = jnp.exp(logit_scores)
    weights = (weights / jnp.sum(weights, axis=-1, keepdims=True)).astype(jnp.bfloat16)
    output = jnp.einsum("bhqk,bkhd->bqhd", weights, value_heads, preferred_element_type=jnp.float32)
    return output.reshape(groups, length, columns)


def squares(rows):
    wide = rows.astype(jnp.float32)
    return jnp.sum(wide * wide, axis=-1)


def normalize(rows, totals, full_width):
    scale = lax.rsqrt(totals / full_width + epsilon)
    return (rows.astype(jnp.float32) * scale[:, None]).astype(jnp.bfloat16)


def pick(blocks, index):
    chosen = (index[:, None] == jnp.arange(blocks.shape[0])[None, :]).astype(blocks.dtype)
    return jnp.einsum("ws,slc->wlc", chosen, blocks, preferred_element_type=jnp.float32).astype(blocks.dtype)


def body(
    neighbour_query,
    neighbour_key,
    neighbour_value,
    segment_key,
    segment_value,
    decoder_query,
    sources,
):
    columns = neighbour_query.shape[1]
    full_width = columns * lax.axis_size("head")
    devices = lax.axis_size("span")
    per_device = SEG_DEV * NEIGHBOURS
    capacity = max(2, 2 * per_device // devices)
    panel_rows = NEIGHBOURS * NBR_LEN
    self_out = attend(
        neighbour_query.reshape(per_device, NBR_LEN, columns),
        neighbour_key.reshape(per_device, NBR_LEN, columns),
        neighbour_value.reshape(per_device, NBR_LEN, columns),
    ).astype(jnp.bfloat16)
    flat_self = self_out.reshape(per_device * NBR_LEN, columns)
    totals = lax.psum(squares(flat_self), "head")
    cross_query = normalize(flat_self, totals, full_width).reshape(per_device, NBR_LEN, columns)
    listed = sources.reshape(per_device)
    owners = listed // SEG_DEV
    within = listed % SEG_DEV
    position = jnp.arange(per_device)
    earlier = (owners[:, None] == owners[None, :]) & (position[:, None] > position[None, :])
    ranked = jnp.sum(earlier.astype(jnp.int32), axis=1)
    slots = owners * capacity + ranked
    picked = (slots[:, None] == jnp.arange(devices * capacity)[None, :]).astype(jnp.int32)
    request = jnp.sum(picked * (within + 1)[:, None], axis=0).reshape(devices, capacity)
    asked = lax.all_to_all(request, "span", split_axis=0, concat_axis=0, tiled=True)
    wanted = jnp.maximum(asked - 1, 0).reshape(devices * capacity)
    own_keys = pick(segment_key.reshape(SEG_DEV, SEG_LEN, columns), wanted)
    own_values = pick(segment_value.reshape(SEG_DEV, SEG_LEN, columns), wanted)
    got_keys, got_values = (
        lax.all_to_all(
            own_keys.reshape(devices, capacity, SEG_LEN, columns),
            "span",
            split_axis=0,
            concat_axis=0,
            tiled=True,
        ),
        lax.all_to_all(
            own_values.reshape(devices, capacity, SEG_LEN, columns),
            "span",
            split_axis=0,
            concat_axis=0,
            tiled=True,
        ),
    )
    source_keys = pick(got_keys.reshape(devices * capacity, SEG_LEN, columns), slots)
    source_values = pick(got_values.reshape(devices * capacity, SEG_LEN, columns), slots)
    crossed = attend(cross_query, source_keys, source_values).astype(jnp.bfloat16)
    encoded = (self_out.astype(jnp.float32) + crossed.astype(jnp.float32)).astype(jnp.bfloat16)
    encoded = encoded.reshape(per_device * NBR_LEN, columns)
    key_totals = lax.psum(squares(encoded), "head")
    keys_all = normalize(encoded, key_totals, full_width)
    before_keys, before_values = from_behind(
        (keys_all[-panel_rows:], encoded[-panel_rows:]), "span", 1
    )
    used_keys = jnp.concatenate([before_keys, keys_all[:-panel_rows]], axis=0)
    used_values = jnp.concatenate([before_values, encoded[:-panel_rows]], axis=0)
    blended = attend(
        decoder_query.reshape(SEG_DEV, SEG_LEN, columns),
        used_keys.reshape(SEG_DEV, panel_rows, columns),
        used_values.reshape(SEG_DEV, panel_rows, columns),
    ).astype(jnp.bfloat16)
    return blended.reshape(SEG_DEV * SEG_LEN, columns)


MESH = pl.DeviceIdType.MESH
GROUPS = 4


def dot_t(a, b):
    return lax.dot_general(a, b, (((1,), (1,)), ((), ())), preferred_element_type=jnp.float32)


def dot_first(a, b):
    return lax.dot_general(a, b, (((0,), (0,)), ((), ())), preferred_element_type=jnp.float32)


def apart(rows):
    count = rows.shape[1] // HEAD_DIM
    zero = jnp.zeros((rows.shape[0], HEAD_DIM), rows.dtype)
    lines = []
    for h in range(count):
        own = rows[:, h * HEAD_DIM:(h + 1) * HEAD_DIM]
        lines.append(jnp.concatenate([own if k == h else zero for k in range(count)], axis=1))
    return jnp.concatenate(lines, axis=0)


def softmax(scores, axis):
    weights = jnp.exp2(scores - jnp.max(scores, axis=axis, keepdims=True))
    inverse = 1.0 / jnp.sum(weights, axis=axis, keepdims=True)
    return (weights * inverse).astype(jnp.bfloat16)


def gather_kernel(
    heads_axis, full_width,
    src_ref, nq_hbm, nk_hbm, nv_hbm, sk_hbm, sv_hbm, dq_hbm, out_ref,
    nq, nk, nv, dq, *rest,
):
    kbufs, vbufs = rest[:GROUPS], rest[GROUPS:2 * GROUPS]
    (own_out, mixing, asked, enc, squares_acc, row_scale, key_scale,
     stat1, stat2, peer1, peer2, behind2,
     in_sem, dq_sem, local_sem, send_sem, recv_sem,
     stat_send, stat_recv, prior_send, prior_recv) = rest[2 * GROUPS:]
    per_device = nq.shape[0]
    seg_dev = dq.shape[0]
    columns = nq.shape[2]
    width = columns // GROUPS
    group_heads = width // HEAD_DIM
    span = lax.axis_size("span")
    me = lax.axis_index("span")
    lane = lax.axis_index("head")
    core, across, along = me ^ 1, me ^ 2, me ^ 4
    after = lax.rem(me + 1, span)
    before = lax.rem(me + span - 1, span)
    softmax_scale = HEAD_DIM ** (-0.5) / math.log(2.0)

    barrier = pltpu.get_barrier_semaphore()
    greeted = 0
    for target in (core, across, along):
        pl.semaphore_signal(barrier, inc=1, device_id={"span": target, "head": lane}, device_id_type=MESH)
        greeted += 1
    for k in range(1, heads_axis):
        other = lax.rem(lane + k, heads_axis)
        pl.semaphore_signal(barrier, inc=1, device_id={"span": me, "head": other}, device_id_type=MESH)
        greeted += 1
    for k in range(heads_axis):
        other = lax.rem(lane + k, heads_axis)
        for target in (after, before):
            pl.semaphore_signal(barrier, inc=1, device_id={"span": target, "head": other}, device_id_type=MESH)
            greeted += 1
    pl.semaphore_wait(barrier, greeted)

    chunks = 2 * GROUPS

    def buffer(j):
        return (kbufs + vbufs)[j]

    def source(j):
        hbm = (sk_hbm, sv_hbm)[j // GROUPS]
        return hbm.at[:, :, pl.ds((j % GROUPS) * width, width)]

    def block(j, owner):
        return buffer(j).at[pl.ds(owner * seg_dev, seg_dev)]

    def half(j, owner, part):
        rows = seg_dev // 2
        return buffer(j).at[pl.ds(owner * seg_dev + part * rows, rows)]

    sent = {}

    def push(kind, j, src, dst, target):
        copy = pltpu.make_async_remote_copy(
            src_ref=src, dst_ref=dst, send_sem=send_sem.at[kind, j], recv_sem=recv_sem.at[kind, j],
            device_id={"span": target, "head": lane}, device_id_type=MESH)
        copy.start()
        sent[kind, j] = copy

    def direct(j):
        push(0, j, source(j), block(j, me), across)
        push(1, j, source(j), block(j, me), along)

    local = []
    for j in range(chunks):
        direct(j)

    for i in range(per_device):
        for a, (hbm, vm) in enumerate(((nq_hbm, nq), (nk_hbm, nk), (nv_hbm, nv))):
            pltpu.make_async_copy(hbm.at[i], vm.at[i], in_sem.at[a, i]).start()
    dq_copy = pltpu.make_async_copy(dq_hbm, dq, dq_sem)
    dq_copy.start()

    for j in range(chunks):
        push(4, j, source(j), block(j, me), core)
        copy = pltpu.make_async_copy(source(j), block(j, me), local_sem.at[j])
        copy.start()
        local.append(copy)

    def forward(j):
        for part in range(2):
            sent[2 + part, j].wait_recv()
            push(7 + part, j, half(j, me ^ 6, part), half(j, me ^ 6, part), core)

    def step(j):
        sent[1, j].wait_recv()
        push(2, j, half(j, along, 0), half(j, along, 0), across)
        sent[0, j].wait_recv()
        push(3, j, half(j, across, 1), half(j, across, 1), along)
        push(5, j, block(j, across), block(j, across), core)
        push(6, j, block(j, along), block(j, along), core)

    def arrived(j):
        local[j].wait()
        for kind in (4, 5, 6, 7, 8):
            sent[kind, j].wait_recv()

    def self_step(i, carry):
        for a, (hbm, vm) in enumerate(((nq_hbm, nq), (nk_hbm, nk), (nv_hbm, nv))):
            pltpu.make_async_copy(hbm.at[i], vm.at[i], in_sem.at[a, i]).wait()
        total = jnp.zeros((NBR_LEN, HEAD_DIM), jnp.float32)
        for base in range(0, columns // HEAD_DIM, 8):
            together = range(base, base + 8)
            cols = [pl.ds(h * HEAD_DIM, HEAD_DIM) for h in together]
            scores = [dot_t(nk[i, :, c], nq[i, :, c]) * softmax_scale for c in cols]
            weights = [softmax(x, 0) for x in scores]
            outs = [dot_first(w, nv[i, :, c]).astype(jnp.bfloat16) for w, c in zip(weights, cols)]
            for h, o in zip(together, outs):
                own_out[h // group_heads, i, :, pl.ds((h % group_heads) * HEAD_DIM, HEAD_DIM)] = o
                wide = o.astype(jnp.float32)
                total = total + wide * wide
        stat1[pl.ds(i, 1), :] = jnp.sum(total.T, axis=0, keepdims=True)
        return carry

    def exchange(kind, stat, peer):
        out = []
        for k in range(1, heads_axis):
            other = lax.rem(lane + k, heads_axis)
            copy = pltpu.make_async_remote_copy(
                src_ref=stat, dst_ref=peer.at[k - 1],
                send_sem=stat_send.at[kind, k - 1], recv_sem=stat_recv.at[kind, k - 1],
                device_id={"span": me, "head": other}, device_id_type=MESH)
            copy.start()
            out.append(copy)
        return out

    def weigh(g):
        arrived(g)

        def some(t, carry):
            rows = [4 * t + b for b in range(4)]
            keys = [apart(kbufs[g][src_ref[i % NEIGHBOURS, i // NEIGHBOURS]]) for i in rows]
            scores = [dot_t(k, own_out[g, i]) * row_scale[pl.ds(i, 1), :] for k, i in zip(keys, rows)]
            weights = [softmax(x.reshape(group_heads, SEG_LEN, NBR_LEN), 1) for x in scores]
            for i, w in zip(rows, weights):
                mixing[g, i] = w.reshape(group_heads * SEG_LEN, NBR_LEN)
            return carry

        lax.fori_loop(0, per_device // 4, some, 0)

    def cross_rows(g, rows):
        values = [apart(vbufs[g][src_ref[i % NEIGHBOURS, i // NEIGHBOURS]]) for i in rows]
        crossed = [dot_first(mixing[g, i], v).astype(jnp.bfloat16) for i, v in zip(rows, values)]
        for i, x in zip(rows, crossed):
            both = (own_out[g, i].astype(jnp.float32) + x.astype(jnp.float32)).astype(jnp.bfloat16)
            enc[g, NEIGHBOURS + i] = both
            wide = both.astype(jnp.float32)
            wide = wide * wide
            total = wide[:, :HEAD_DIM]
            for h in range(1, group_heads):
                total = total + wide[:, h * HEAD_DIM:(h + 1) * HEAD_DIM]
            if g > 0:
                total = total + squares_acc[i]
            if g < GROUPS - 1:
                squares_acc[i] = total
            else:
                stat2[pl.ds(i, 1), :] = jnp.sum(total.T, axis=0, keepdims=True)

    prior = []

    def panel(g, u):
        return enc[g, pl.ds(NEIGHBOURS * u, NEIGHBOURS)].reshape(NEIGHBOURS * NBR_LEN, width)

    def ask(g, u):
        asked[u, g] = dot_t(panel(g, u), apart(dq[u, :, pl.ds(g * width, width)]))

    def cross(g):
        arrived(GROUPS + g)
        cross_rows(g, list(range(per_device - NEIGHBOURS, per_device)))
        copy = pltpu.make_async_remote_copy(
            src_ref=enc.at[g, pl.ds(per_device, NEIGHBOURS)], dst_ref=enc.at[g, pl.ds(0, NEIGHBOURS)],
            send_sem=prior_send.at[g], recv_sem=prior_recv.at[g],
            device_id={"span": after, "head": lane}, device_id_type=MESH)
        copy.start()
        prior.append(copy)

        def rest_step(t, carry):
            cross_rows(g, [3 * t + b for b in range(3)])
            return carry

        lax.fori_loop(0, (per_device - NEIGHBOURS) // 3, rest_step, 0)

    quarter = per_device // 4
    for j in range(4):
        lax.fori_loop(j * quarter, (j + 1) * quarter, self_step, 0)
        if j > 0:
            step(2 * j - 2)
            step(2 * j - 1)
    first_stats = exchange(0, stat1, peer1)
    step(6)
    for copy in first_stats:
        copy.wait_recv()
    total1 = stat1[...]
    for k in range(heads_axis - 1):
        total1 = total1 + peer1[k]
    row_scale[...] = lax.rsqrt(total1 / full_width + epsilon) * softmax_scale
    step(7)
    forward(0)
    for g in range(GROUPS):
        forward(g + 1)
        weigh(g)
    dq_copy.wait()
    for g in range(GROUPS):
        if g + 1 < GROUPS:
            forward(GROUPS + 1 + g)
        cross(g)
        if g + 1 < GROUPS:
            for u in range(1, seg_dev):
                ask(g, u)

    second_stats = exchange(1, stat2, peer2)
    behind_stats = []
    for k in range(heads_axis):
        other = lax.rem(lane + k, heads_axis)
        copy = pltpu.make_async_remote_copy(
            src_ref=stat2, dst_ref=behind2.at[k],
            send_sem=stat_send.at[2, k], recv_sem=stat_recv.at[2, k],
            device_id={"span": after, "head": other}, device_id_type=MESH)
        copy.start()
        behind_stats.append(copy)
    for u in range(1, seg_dev):
        ask(GROUPS - 1, u)
    for copy in second_stats:
        copy.wait_recv()
    total2 = stat2[...]
    for k in range(heads_axis - 1):
        total2 = total2 + peer2[k]
    key_scale[pl.ds(NEIGHBOURS, per_device), :] = lax.rsqrt(total2 / full_width + epsilon) * softmax_scale

    def decode_step(u, carry):
        scale = jnp.concatenate([
            jnp.broadcast_to(key_scale[pl.ds(NEIGHBOURS * u + n, 1), :], (NBR_LEN, NBR_LEN)).T
            for n in range(NEIGHBOURS)], axis=0)
        weights = [softmax(asked[u, g] * scale, 0) for g in range(GROUPS)]
        outs = [dot_first(w, panel(g, u)).astype(jnp.bfloat16) for g, w in enumerate(weights)]
        for g, out in enumerate(outs):
            for h in range(group_heads):
                lo = h * HEAD_DIM
                out_ref[u, :, pl.ds(g * width + lo, HEAD_DIM)] = out[h * SEG_LEN:(h + 1) * SEG_LEN, lo:lo + HEAD_DIM]
        return carry

    lax.fori_loop(1, seg_dev, decode_step, 0)
    for copy in behind_stats:
        copy.wait_recv()
    for copy in prior:
        copy.wait_recv()
    total3 = behind2[0]
    for k in range(1, heads_axis):
        total3 = total3 + behind2[k]
    total3 = lax.rsqrt(total3 / full_width + epsilon) * softmax_scale
    key_scale[pl.ds(0, NEIGHBOURS), :] = total3[per_device - NEIGHBOURS:]

    @pl.when(me == 0)
    def _():
        enc[:, pl.ds(0, NEIGHBOURS)] = jnp.zeros((GROUPS, NEIGHBOURS, NBR_LEN, width), jnp.bfloat16)

    for g in range(GROUPS):
        ask(g, 0)
    decode_step(0, 0)
    for copy in list(sent.values()) + prior + first_stats + second_stats + behind_stats:
        copy.wait_send()


def gather_all(operands):
    columns = operands[1].shape[2]
    heads_axis = lax.axis_size("head")
    span = lax.axis_size("span")
    per_device = SEG_DEV * NEIGHBOURS
    width = columns // GROUPS
    bf16, f32 = jnp.bfloat16, jnp.float32
    neighbour_shape = (per_device, NBR_LEN, columns)
    segment_shape = (SEG_DEV, SEG_LEN, columns)
    chunks = 2 * GROUPS
    any_space = pl.BlockSpec(memory_space=pltpu.HBM)
    dma = pltpu.SemaphoreType.DMA
    return pl.pallas_call(
        functools.partial(gather_kernel, heads_axis, columns * heads_axis),
        out_shape=jax.ShapeDtypeStruct(segment_shape, bf16),
        in_specs=[pl.BlockSpec(memory_space=pltpu.SMEM)] + [any_space] * 6,
        out_specs=pl.BlockSpec(memory_space=pltpu.VMEM),
        scratch_shapes=[pltpu.VMEM(neighbour_shape, bf16)] * 3
        + [pltpu.VMEM(segment_shape, bf16)]
        + [pltpu.VMEM((span * SEG_DEV, SEG_LEN, width), bf16)] * chunks
        + [
            pltpu.VMEM((GROUPS, per_device, NBR_LEN, width), bf16),
            pltpu.VMEM((GROUPS, per_device, width // HEAD_DIM * SEG_LEN, NBR_LEN), bf16),
            pltpu.VMEM((SEG_DEV, GROUPS, NEIGHBOURS * NBR_LEN, width // HEAD_DIM * SEG_LEN), f32),
            pltpu.VMEM((GROUPS, per_device + NEIGHBOURS, NBR_LEN, width), bf16),
            pltpu.VMEM((per_device, NBR_LEN, HEAD_DIM), f32),
            pltpu.VMEM((per_device, NBR_LEN), f32),
            pltpu.VMEM((per_device + NEIGHBOURS, NBR_LEN), f32),
            pltpu.VMEM((per_device, NBR_LEN), f32),
            pltpu.VMEM((per_device, NBR_LEN), f32),
            pltpu.VMEM((heads_axis - 1, per_device, NBR_LEN), f32),
            pltpu.VMEM((heads_axis - 1, per_device, NBR_LEN), f32),
            pltpu.VMEM((heads_axis, per_device, NBR_LEN), f32),
            dma((3, per_device)),
            dma,
            dma((chunks,)),
            dma((9, chunks)),
            dma((9, chunks)),
            dma((3, heads_axis)),
            dma((3, heads_axis)),
            dma((GROUPS,)),
            dma((GROUPS,)),
        ],
        compiler_params=pltpu.CompilerParams(
            collective_id=1, has_side_effects=True, vmem_limit_bytes=53 * 1024 * 1024),
    )(*operands)


PHASES = (2, 3, 3)
SLOTS = sum(PHASES)
STARTS = tuple(sum(PHASES[:p]) for p in range(len(PHASES)))
FORWARDS = (0, 0, 1, 2, 2, 3, 4, 5)
CHIP_SEGS = 8
LANES = 128


def selections():
    upper = lax.broadcasted_iota(jnp.int32, (LANES, LANES), 0)
    lower = lax.broadcasted_iota(jnp.int32, (LANES, LANES), 1)
    row_chip, column_chip = upper // CHIP_SEGS, lower // CHIP_SEGS
    same = jnp.where(row_chip == column_chip, 1.0, 0.0)
    ahead = jnp.where(upper < lower, same, 0.0)
    others = [jnp.where((row_chip ^ k) == column_chip, 1.0, 0.0) for k in range(1, 4)]
    return jnp.concatenate(others + [same, ahead], axis=1).astype(jnp.bfloat16)


def routes(needs, select, mine):
    f32, bf16 = jnp.float32, jnp.bfloat16
    lane = lax.broadcasted_iota(jnp.int32, (1, LANES), 1)
    chip = lane // CHIP_SEGS
    within = (lane % CHIP_SEGS).astype(f32)

    def at(k):
        total = jnp.zeros((1, LANES), f32)
        for t, row in enumerate(needs):
            total = total + jnp.where((chip ^ k) == t, row, 0.0)
        return total

    n1, n2, n3 = at(1), at(2), at(3)
    only1, only2 = n3 * n1 * (1 - n2), n3 * n2 * (1 - n1)
    both, none = n3 * n1 * n2, n3 * (1 - n1) * (1 - n2)
    zero = jnp.zeros((1, LANES), f32)
    stacked = jnp.concatenate([n1, n2, only1, only2, both, none, zero, zero], axis=0)
    counts = jnp.dot(stacked.astype(bf16), select, preferred_element_type=f32)

    def count(r):
        return [counts[r:r + 1, k * LANES:(k + 1) * LANES] for k in (3, 0, 1, 2)]

    def rank(r):
        return counts[r:r + 1, 4 * LANES:]

    n1c, n2c, o1, o2, b, n = [count(r) for r in range(6)]
    every = range(4)

    def clip(value, top):
        return jnp.minimum(jnp.maximum(value, 0.0), top)

    x = [n1c[k] + o2[k ^ 2] for k in every]
    y = [n2c[k] + o1[k ^ 1] for k in every]
    pb = [clip(jnp.floor((b[k] + x[k ^ 2] - y[k ^ 1] + 1) * 0.5), b[k]) for k in every]
    x = [x[k] + b[k ^ 2] - pb[k ^ 2] for k in every]
    y = [y[k] + pb[k ^ 1] for k in every]
    pn = [clip(jnp.floor((n[k] + jnp.maximum(y[k], x[k ^ 2]) - jnp.maximum(x[k], y[k ^ 1]) + 1) * 0.5), n[k])
          for k in every]
    x, y = ([x[k] + pn[k] + n[k ^ 2] - pn[k ^ 2] for k in every],
            [y[k] + n[k] - pn[k] + pn[k ^ 1] for k in every])
    over1 = [jnp.maximum(x[k], y[k ^ 1]) - SLOTS for k in every]
    over2 = [jnp.maximum(y[k], x[k ^ 2]) - SLOTS for k in every]
    shift = [clip(jnp.minimum(over2[k], -over1[k]), n[k] - pn[k]) - clip(jnp.minimum(over1[k], -over2[k]), pn[k])
             for k in every]
    pn = [pn[k] + shift[k] for k in every]
    x, y = ([x[k] + shift[k] - shift[k ^ 2] for k in every],
            [y[k] - shift[k] + shift[k ^ 1] for k in every])
    m1 = [clip(jnp.minimum(y[k ^ 1] - SLOTS, SLOTS - jnp.maximum(y[k], x[k ^ 2])), o1[k]) for k in every]
    m2 = [clip(jnp.minimum(x[k ^ 2] - SLOTS, SLOTS - jnp.maximum(x[k], y[k ^ 1])), o2[k]) for k in every]

    def below(r, limit, rows):
        return jnp.where(rank(r) < limit, rows, 0.0)

    path1 = only1 - below(2, m1[0], only1) + below(3, m2[0], only2) + below(4, pb[0], both) + below(5, pn[0], none)
    path2 = n3 - path1
    own_x, own_y = jnp.maximum(n1, path1), jnp.maximum(n2, path2)
    stacked = jnp.concatenate(
        [path1, path2, own_x - path1, own_y - path2, zero, zero, zero, zero], axis=0)
    again = jnp.dot(stacked.astype(bf16), select[:, 3 * LANES:], preferred_element_type=f32)
    relays, ranks = again[:, :LANES], again[:, LANES:]
    slot_x = jnp.where(path1 > 0, ranks[0:1], relays[0:1] + ranks[2:3])
    slot_y = jnp.where(path2 > 0, ranks[1:2], relays[1:2] + ranks[3:4])

    def forwarded(own, place):
        return jnp.maximum(own, jnp.where(place < 2, 2.0, 3.0)) + place

    forward_y = forwarded(n2c[1] + n[1] - pn[1] + m1[1], ranks[0:1])
    forward_x = forwarded(n1c[2] + pn[2] + m2[2], ranks[1:2])
    last = jnp.maximum(path1 * forward_y, path2 * forward_x)
    over = jnp.max(jnp.where(last >= SLOTS, 1.0, 0.0), axis=1, keepdims=True)

    side = chip ^ mine
    place = jnp.where(
        side == 0, within,
        CHIP_SEGS + jnp.where(
            side == 1, slot_x,
            jnp.where(side == 2, SLOTS + slot_y, jnp.where(path1 > 0, SLOTS + forward_y, forward_x))))
    place = jnp.minimum(place, CHIP_SEGS + 2 * SLOTS - 1.0)

    def sends(own, slot, relay, forward, arrives):
        mine_own = (side == 0) & (own > 0)
        number = jnp.where(mine_own, slot, jnp.where(relay, forward, -1.0))
        code = jnp.where(mine_own, within, CHIP_SEGS + arrives)
        wanted = lax.broadcasted_iota(jnp.int32, (SLOTS, LANES), 0).astype(f32)
        return jnp.sum(jnp.where(number == wanted, code, 0.0), axis=1, keepdims=True)

    send_x = sends(own_x, slot_x, (side == 2) & (path2 > 0), forward_x, slot_y)
    send_y = sends(own_y, slot_y, (side == 1) & (path1 > 0), forward_y, slot_x)
    rows = [send_x, send_y, place, over]
    return jnp.concatenate([jnp.broadcast_to(r, (8, LANES)) for r in rows], axis=0).astype(jnp.int32)


ORDER = ((0, 0), (1, 0), (2, 0), (0, 1), (1, 1), (3, 0), (0, 2), (1, 2), (2, 1), (3, 1), (2, 2), (3, 2))


def kernel(
    heads_axis, full_width,
    src_ref, nq_hbm, nk_hbm, nv_hbm, sk_hbm, sv_hbm, dq_hbm, out_ref, over_ref,
    nq, nk, nv, dq, *rest,
):
    own_a, own_b, recv_a, recv_b, send_a = (rest[4 * j:4 * j + 4] for j in range(5))
    (first, answer, first_sem, ask_send, ask_recv, answer_send, answer_recv, select, need, needs, table, lookup, own_out, mixing, asked, enc, squares_acc, row_scale, key_scale,
     stat1, stat2, peer1, peer2, peer3,
     in_sem, dq_sem, local_sem, table_sem, need_send, need_recv, core_send, core_recv,
     link_send, link_recv, pass_send, pass_recv,
     stat_send, stat_recv) = rest[20:]
    per_device = nq.shape[0]
    seg_dev = dq.shape[1]
    columns = nq.shape[2]
    width = columns // GROUPS
    group_heads = width // HEAD_DIM
    span = lax.axis_size("span")
    me = lax.axis_index("span")
    lane = lax.axis_index("head")
    side = lax.rem(me, 2)
    core, across, along = me ^ 1, me ^ 2, me ^ 4
    after = lax.rem(me + 1, span)
    before = lax.rem(me + span - 1, span)
    softmax_scale = HEAD_DIM ** (-0.5) / math.log(2.0)

    def at(target, head):
        return {"span": target, "head": head}

    def columns_of(half, q):
        return pl.ds(pl.multiple_of((2 * half + q) * width, width), width)

    def source(k, half):
        hbm = (sk_hbm, sv_hbm)[k % 2]
        return hbm.at[:, :, columns_of(half, k // 2)]

    mine_rows = pl.ds(pl.multiple_of(side * seg_dev, seg_dev), seg_dev)

    def inputs(i):
        return [pltpu.make_async_copy(hbm.at[i], vm.at[i], in_sem.at[a, i])
                for a, (hbm, vm) in enumerate(((nq_hbm, nq), (nk_hbm, nk), (nv_hbm, nv)))]

    for i in range(2):
        for copy in inputs(i):
            copy.start()
    local = {}
    for k in range(4):
        for b, (own, half) in enumerate(((own_a[k], side), (own_b[k], 1 - side))):
            copy = pltpu.make_async_copy(source(k, half), own.at[mine_rows], local_sem.at[b, k])
            copy.start()
            local[b, k] = copy
    for i in range(2, per_device):
        for copy in inputs(i):
            copy.start()
    dq_copies = []
    for g in range(GROUPS):
        copy = pltpu.make_async_copy(
            dq_hbm.at[pl.ds(1, seg_dev - 1), :, pl.ds(g * width, width)], dq.at[g, pl.ds(0, seg_dev - 1)],
            dq_sem.at[g])
        copy.start()
        dq_copies.append(copy)
    stat2[1] = jnp.zeros_like(stat2[1])

    @pl.when(me == 0)
    def _():
        pltpu.make_async_copy(dq_hbm.at[0], first, first_sem).start()

    @pl.when(me == span - 1)
    def _():
        for g in range(GROUPS):
            dq[g, seg_dev - 1] = jnp.zeros((SEG_LEN, width), jnp.bfloat16)

    segment = lax.broadcasted_iota(jnp.int32, (8, LANES), 1)
    wanted = jnp.zeros((8, LANES), jnp.float32)
    for i in range(per_device):
        wanted = jnp.where(segment == src_ref[i % NEIGHBOURS, i // NEIGHBOURS], 1.0, wanted)
    need[...] = wanted
    select[...] = selections()

    barrier = pltpu.get_barrier_semaphore()
    greeted = 0
    for k in range(1, span):
        pl.semaphore_signal(barrier, inc=1, device_id=at(me ^ k, lane), device_id_type=MESH)
        greeted += 1
    for k in range(1, heads_axis):
        other = lax.rem(lane + k, heads_axis)
        pl.semaphore_signal(barrier, inc=1, device_id=at(me, other), device_id_type=MESH)
        greeted += 1
    pl.semaphore_wait(barrier, greeted)

    def remote(src, dst, send_sem, recv_sem, target):
        copy = pltpu.make_async_remote_copy(
            src_ref=src, dst_ref=dst, send_sem=send_sem, recv_sem=recv_sem,
            device_id=at(*target), device_id_type=MESH)
        copy.start()
        return copy

    told = [remote(need, needs.at[me], need_send.at[k - 1], need_recv.at[k - 1], (me ^ k, lane))
            for k in range(1, span)]
    needs[me] = wanted

    def query_copy(g):
        return pltpu.make_async_remote_copy(
            src_ref=dq_hbm.at[0, :, pl.ds(g * width, width)], dst_ref=dq.at[g, seg_dev - 1],
            send_sem=ask_send.at[g], recv_sem=ask_recv.at[g], device_id=at(before, lane), device_id_type=MESH)

    def answer_copy(g):
        block = pl.ds(g * width, width)
        return pltpu.make_async_remote_copy(
            src_ref=answer.at[:, block], dst_ref=out_ref.at[0, :, block],
            send_sem=answer_send.at[g], recv_sem=answer_recv.at[g], device_id=at(after, lane), device_id_type=MESH)

    @pl.when(me > 0)
    def _():
        for g in range(GROUPS):
            query_copy(g).start()

    given = {}
    for k in range(4):
        given[0, k] = remote(source(k, 1 - side), own_a[k].at[mine_rows], core_send.at[0, k], core_recv.at[0, k],
                             (core, lane))
        given[1, k] = remote(source(k, side), own_b[k].at[mine_rows], core_send.at[1, k], core_recv.at[1, k],
                             (core, lane))

    def owned(b, k):
        local[b, k].wait()
        given[b, k].wait_recv()

    sent, passed = {}, {}

    def slots(link, p):
        return pl.ds(link * SLOTS + STARTS[p], PHASES[p])

    def hand_on(k, p):
        for link in range(2):
            sent[k, p, link].wait_recv()
            block = slots(link, p)
            passed[k, p, link] = remote(recv_a[k].at[block], recv_b[k].at[block], pass_send.at[link, 3 * k + p],
                                        pass_recv.at[link, 3 * k + p], (core, lane))

    def advance(k, p):
        if p == 0:
            owned(0, k)
        else:
            hand_on(k, p - 1)
        for link, target in enumerate((across, along)):
            for i in range(STARTS[p], STARTS[p] + PHASES[p]):
                code = lookup[8 * link + i, 0]
                rows = own_a[k][jnp.clip(code, 0, CHIP_SEGS - 1)]
                for t in range(FORWARDS[i]):
                    rows = jnp.where(code == CHIP_SEGS + t, recv_a[k][(1 - link) * SLOTS + t], rows)
                send_a[k][link * SLOTS + i] = rows
            block = slots(link, p)
            sent[k, p, link] = remote(send_a[k].at[block], recv_a[k].at[block], link_send.at[link, 3 * k + p],
                                      link_recv.at[link, 3 * k + p], (target, lane))

    def finish(k):
        hand_on(k, len(PHASES) - 1)

    def arrived(b, k):
        if b == 1:
            owned(1, k)
            for p in range(len(PHASES)):
                for link in range(2):
                    passed[k, p, link].wait_recv()

    def rows_of(b, k, i):
        place = lookup[16, src_ref[i % NEIGHBOURS, i // NEIGHBOURS]]
        own, recv = ((own_a[k], recv_a[k]), (own_b[k], recv_b[k]))[b]
        return jnp.where(place < CHIP_SEGS, own[jnp.clip(place, 0, CHIP_SEGS - 1)],
                         recv[jnp.clip(place - CHIP_SEGS, 0, 2 * SLOTS - 1)])

    def self_step(i, carry):
        for copy in inputs(i):
            copy.wait()
        total = jnp.zeros((NBR_LEN, HEAD_DIM), jnp.float32)
        for base in range(0, columns // HEAD_DIM, 8):
            together = range(base, base + 8)
            cols = [pl.ds(h * HEAD_DIM, HEAD_DIM) for h in together]
            scores = [dot_t(nk[i, :, c], nq[i, :, c]) * softmax_scale for c in cols]
            weights = [softmax(x, 0) for x in scores]
            outs = [dot_first(w, nv[i, :, c]).astype(jnp.bfloat16) for w, c in zip(weights, cols)]
            for h, o in zip(together, outs):
                own_out[h // group_heads, i, :, pl.ds((h % group_heads) * HEAD_DIM, HEAD_DIM)] = o
                wide = o.astype(jnp.float32)
                total = total + wide * wide
        stat1[pl.ds(i, 1), :] = jnp.sum(total.T, axis=0, keepdims=True)
        return carry

    def exchange(kind, stat, peer):
        return [remote(stat, peer.at[k - 1], stat_send.at[kind, k - 1], stat_recv.at[kind, k - 1],
                       (me, lax.rem(lane + k, heads_axis))) for k in range(1, heads_axis)]

    def group(b, q):
        return 2 * (side if b == 0 else 1 - side) + q

    def weigh(b, q):
        arrived(b, 2 * q)
        g = group(b, q)

        def some(t, carry):
            rows = [4 * t + s for s in range(4)]
            keys = [apart(rows_of(b, 2 * q, i)) for i in rows]
            scores = [dot_t(k, own_out[g, i]) * row_scale[pl.ds(i, 1), :] for k, i in zip(keys, rows)]
            weights = [softmax(x.reshape(group_heads, SEG_LEN, NBR_LEN), 1) for x in scores]
            for i, w in zip(rows, weights):
                mixing[g, i] = w.reshape(group_heads * SEG_LEN, NBR_LEN)
            return carry

        lax.fori_loop(0, per_device // 4, some, 0)

    def cross_rows(b, q, rows):
        g = group(b, q)
        values = [apart(rows_of(b, 2 * q + 1, i)) for i in rows]
        crossed = [dot_first(mixing[g, i], v).astype(jnp.bfloat16) for i, v in zip(rows, values)]
        for i, x in zip(rows, crossed):
            both = (own_out[g, i].astype(jnp.float32) + x.astype(jnp.float32)).astype(jnp.bfloat16)
            enc[g, i] = both
            wide = both.astype(jnp.float32)
            wide = wide * wide
            total = wide[:, :HEAD_DIM]
            for h in range(1, group_heads):
                total = total + wide[:, h * HEAD_DIM:(h + 1) * HEAD_DIM]
            if (q, b) != (0, 0):
                total = total + squares_acc[i]
            if (q, b) != (1, 1):
                squares_acc[i] = total
            else:
                line = jnp.sum(total.T, axis=0, keepdims=True)
                stat2[0, pl.ds(i, 1), :] = line
                if len(rows) == NEIGHBOURS:
                    stat2[1, pl.ds(i, 1), :] = line

    def panel(g, u):
        return enc[g, pl.ds(NEIGHBOURS * u, NEIGHBOURS)].reshape(NEIGHBOURS * NBR_LEN, width)

    def ask(g, u):
        asked[u, g] = dot_t(panel(g, u), apart(dq[g, u]))

    def cross_last(b, q):
        arrived(b, 2 * q + 1)
        cross_rows(b, q, list(range(per_device - NEIGHBOURS, per_device)))

    def cross_others(b, q):
        def rest_step(t, carry):
            cross_rows(b, q, [3 * t + s for s in range(3)])
            return carry

        lax.fori_loop(0, (per_device - NEIGHBOURS) // 3, rest_step, 0)

    lax.fori_loop(0, 1, self_step, 0)
    for copy in told:
        copy.wait_recv()
    table[...] = routes([jnp.maximum(needs[2 * t][:1], needs[2 * t + 1][:1]) for t in range(span // 2)],
                        select[...], me // 2)
    copy = pltpu.make_async_copy(table, lookup, table_sem)
    copy.start()
    copy.wait()
    for k, p in ORDER[:3]:
        advance(k, p)
    lax.fori_loop(1, 3, self_step, 0)
    advance(*ORDER[3])
    lax.fori_loop(3, 5, self_step, 0)
    advance(*ORDER[4])
    advance(*ORDER[5])
    lax.fori_loop(5, per_device, self_step, 0)
    first_stats = exchange(0, stat1, peer1)
    for k, p in ORDER[6:8]:
        advance(k, p)
    for copy in first_stats:
        copy.wait_recv()
    total1 = stat1[...]
    for k in range(heads_axis - 1):
        total1 = total1 + peer1[k]
    row_scale[...] = lax.rsqrt(total1 / full_width + epsilon) * softmax_scale
    for k, p in ORDER[8:10]:
        advance(k, p)
    for copy in dq_copies:
        copy.wait()

    @pl.when(me < span - 1)
    def _():
        for g in range(GROUPS):
            query_copy(g).wait_recv()

    @pl.when(me == 0)
    def _():
        pltpu.make_async_copy(dq_hbm.at[0], first, first_sem).wait()
        for g in range(GROUPS):
            nothing = jnp.zeros((NEIGHBOURS * NBR_LEN, width), jnp.bfloat16)
            scores = dot_t(nothing, apart(first[:, g * width:(g + 1) * width])) * (epsilon ** -0.5 * softmax_scale)
            out = dot_first(softmax(scores, 0), nothing).astype(jnp.bfloat16)
            for h in range(group_heads):
                lo = h * HEAD_DIM
                out_ref[0, :, pl.ds(g * width + lo, HEAD_DIM)] = out[h * SEG_LEN:(h + 1) * SEG_LEN, lo:lo + HEAD_DIM]

    finish(0)
    weigh(0, 0)
    finish(1)
    advance(*ORDER[10])
    weigh(1, 0)
    cross_last(0, 0)
    advance(*ORDER[11])
    cross_others(0, 0)
    cross_last(1, 0)
    cross_others(1, 0)
    for b in range(2):
        for u in range(seg_dev):
            ask(group(b, 0), u)
    finish(2)
    weigh(0, 1)
    finish(3)
    weigh(1, 1)
    cross_last(0, 1)
    cross_others(0, 1)
    cross_last(1, 1)
    last_stats = exchange(2, stat2.at[1], peer3)
    cross_others(1, 1)
    second_stats = exchange(1, stat2.at[0], peer2)
    for b in range(2):
        for u in reversed(range(seg_dev)):
            ask(group(b, 1), u)

    def settle(mine, copies, peer, rows):
        for copy in copies:
            copy.wait_recv()
        total = mine
        for k in range(heads_axis - 1):
            total = total + peer[k]
        scale = lax.rsqrt(total / full_width + epsilon) * softmax_scale
        key_scale[rows] = scale[rows]

    def decoded(u):
        scale = jnp.concatenate([
            jnp.broadcast_to(key_scale[pl.ds(NEIGHBOURS * u + n, 1), :], (NBR_LEN, NBR_LEN)).T
            for n in range(NEIGHBOURS)], axis=0)
        weights = [softmax(asked[u, g] * scale, 0) for g in range(GROUPS)]
        outs = [dot_first(w, panel(g, u)).astype(jnp.bfloat16) for g, w in enumerate(weights)]
        for g, out in enumerate(outs):
            for h in range(group_heads):
                lo = h * HEAD_DIM
                yield g * width + lo, out[h * SEG_LEN:(h + 1) * SEG_LEN, lo:lo + HEAD_DIM]

    def decode_step(u, carry):
        for lo, out in decoded(u):
            out_ref[u + 1, :, pl.ds(lo, HEAD_DIM)] = out
        return carry

    settle(stat2[1], last_stats, peer3, slice(per_device - NEIGHBOURS, per_device))
    for lo, out in decoded(seg_dev - 1):
        answer[:, pl.ds(lo, HEAD_DIM)] = out

    @pl.when(me < span - 1)
    def _():
        for g in range(GROUPS):
            answer_copy(g).start()

    settle(stat2[0], second_stats, peer2, slice(0, per_device - NEIGHBOURS))
    lax.fori_loop(0, seg_dev - 1, decode_step, 0)
    over_ref[0, 0] = lookup[24, 0]

    @pl.when(me > 0)
    def _():
        for g in range(GROUPS):
            answer_copy(g).wait_recv()
            query_copy(g).wait_send()

    @pl.when(me < span - 1)
    def _():
        for g in range(GROUPS):
            answer_copy(g).wait_send()

    for copy in (told + list(given.values()) + list(sent.values()) + list(passed.values())
                 + first_stats + last_stats + second_stats):
        copy.wait_send()


def fused_body(
    neighbour_query,
    neighbour_key,
    neighbour_value,
    segment_key,
    segment_value,
    decoder_query,
    sources,
):
    columns = neighbour_query.shape[1]
    heads_axis = lax.axis_size("head")
    span = lax.axis_size("span")
    per_device = SEG_DEV * NEIGHBOURS
    width = columns // GROUPS
    bf16, f32 = jnp.bfloat16, jnp.float32
    neighbour_shape = (per_device, NBR_LEN, columns)
    segment_shape = (SEG_DEV, SEG_LEN, columns)
    any_space = pl.BlockSpec(memory_space=pltpu.HBM)
    dma = pltpu.SemaphoreType.DMA
    own = pltpu.VMEM((CHIP_SEGS, SEG_LEN, width), bf16)
    slots = pltpu.VMEM((2 * SLOTS, SEG_LEN, width), bf16)
    steps = 4 * len(PHASES)
    operands = (
        sources.T,
        neighbour_query.reshape(neighbour_shape),
        neighbour_key.reshape(neighbour_shape),
        neighbour_value.reshape(neighbour_shape),
        segment_key.reshape(segment_shape),
        segment_value.reshape(segment_shape),
        decoder_query.reshape(segment_shape),
    )
    out, over = pl.pallas_call(
        functools.partial(kernel, heads_axis, columns * heads_axis),
        out_shape=(jax.ShapeDtypeStruct(segment_shape, bf16), jax.ShapeDtypeStruct((1, 1), jnp.int32)),
        in_specs=[pl.BlockSpec(memory_space=pltpu.SMEM)] + [any_space] * 6,
        out_specs=(pl.BlockSpec(memory_space=pltpu.VMEM), pl.BlockSpec(memory_space=pltpu.SMEM)),
        scratch_shapes=[pltpu.VMEM(neighbour_shape, bf16)] * 3
        + [pltpu.VMEM((GROUPS, SEG_DEV, SEG_LEN, width), bf16)]
        + [own] * 8 + [slots] * 12
        + [
            pltpu.VMEM((SEG_LEN, columns), bf16),
            pltpu.VMEM((SEG_LEN, columns), bf16),
            dma,
            dma((GROUPS,)),
            dma((GROUPS,)),
            dma((GROUPS,)),
            dma((GROUPS,)),
            pltpu.VMEM((LANES, 5 * LANES), bf16),
            pltpu.VMEM((8, LANES), f32),
            pltpu.VMEM((span, 8, LANES), f32),
            pltpu.VMEM((32, LANES), jnp.int32),
            pltpu.SMEM((32, LANES), jnp.int32),
            pltpu.VMEM((GROUPS, per_device, NBR_LEN, width), bf16),
            pltpu.VMEM((GROUPS, per_device, width // HEAD_DIM * SEG_LEN, NBR_LEN), bf16),
            pltpu.VMEM((SEG_DEV, GROUPS, NEIGHBOURS * NBR_LEN, width // HEAD_DIM * SEG_LEN), f32),
            pltpu.VMEM((GROUPS, per_device, NBR_LEN, width), bf16),
            pltpu.VMEM((per_device, NBR_LEN, HEAD_DIM), f32),
            pltpu.VMEM((per_device, NBR_LEN), f32),
            pltpu.VMEM((per_device, NBR_LEN), f32),
            pltpu.VMEM((per_device, NBR_LEN), f32),
            pltpu.VMEM((2, per_device, NBR_LEN), f32),
            pltpu.VMEM((heads_axis - 1, per_device, NBR_LEN), f32),
            pltpu.VMEM((heads_axis - 1, per_device, NBR_LEN), f32),
            pltpu.VMEM((heads_axis - 1, per_device, NBR_LEN), f32),
            dma((3, per_device)),
            dma((GROUPS,)),
            dma((2, 4)),
            dma,
            dma((span - 1,)),
            dma((span - 1,)),
            dma((2, 4)),
            dma((2, 4)),
            dma((2, steps)),
            dma((2, steps)),
            dma((2, steps)),
            dma((2, steps)),
            dma((3, heads_axis)),
            dma((3, heads_axis)),
        ],
        compiler_params=pltpu.CompilerParams(
            collective_id=0, has_side_effects=True, vmem_limit_bytes=53 * 1024 * 1024),
    )(*operands)
    return lax.cond(
        over[0, 0] > 0,
        lambda: gather_all(operands).reshape(SEG_DEV * SEG_LEN, columns),
        lambda: out.reshape(SEG_DEV * SEG_LEN, columns),
    )


def solution(mesh):
    placed = (
        P("span", "head"),
        P("span", "head"),
        P("span", "head"),
        P("span", "head"),
        P("span", "head"),
        P("span", "head"),
        P("span", None),
    )
    cube = mesh.shape["span"] == 2 * 2 * 2
    return jax.shard_map(
        fused_body if cube else body, mesh=mesh, in_specs=placed, out_specs=P("span", "head"), check_vma=False
    )
```
